32 devices in a mesh: groups: 2 (over y), space: 4 (over z), date: 2 (over x), band: 2 (over core).
Axes of the slice: x: 2, y: 2, z: 4, core: 2. Of those that a mesh axis runs over, the one named last changes fastest.
Arguments:
- reflect: float32 [16, 8, 256, 256], P('date', 'band', ('groups', 'space')), parts along dimension 2, may hold values from -6 to 6
- kernels: float32 [3, 8, 33], P(None, 'band'), may hold values from 0.2 to 2
- strength: float32 [3, 8], P(None, 'band'), may hold values from 0.2 to 0.6
- destinations: int32 [128, 1], P(('groups', 'space')), parts along dimension 0, may hold values from 0 to 3; in each aligned block of 16 rows (0 to 15, 16 to 31, ...) at most 8 rows name the same one
- offsets: int32 [128], P(('groups', 'space')), parts along dimension 0, may hold values from 0 to 60
- counts: int32 [16, 8], P('date', ('groups', 'space')), parts along dimension 1, may hold values from 1 to 8192
- resample_rows: float32 [8, 4, 4], P(('groups', 'space')), parts along dimension 0, may hold values from -3 to 3
- resample_columns: float32 [8, 128, 128], P(('groups', 'space')), parts along dimension 0, may hold values from -0.5 to 0.5
Outputs:
- geomedian: float32 [8, 512, 128], P('band', ('groups', 'space')), parts along dimension 1
The draws below stay inside these ranges and needn't reach their ends.
There are 2 independent parts, one for each index of `groups`. The reference program is written for one: setup_inputs(seed, part) draws one part's arguments, and reference() takes and returns one part's arrays. A program takes and returns all parts, laid end to end along the dimension named above; an argument that names none is the same for every part. Nothing has to cross between parts.
Inputs may be any that keep to these rules, and one draw needn't show every extreme that they name: `destinations`: in each aligned block of 16 entries (the blocks of one strip) no tile is named more than 8 times, a bound that some block reaches.
All inputs are finite; a program needn't handle non-finite values.
Results may differ from the reference program's by a relative error of at most 0.00011.
Values sent between devices are 32-bit elements; how exact they have to be, the bound alone decides.
No kernel may reach another device: no remote copies, remote signals or barrier semaphores. Data moves between devices by JAX's collectives and lax.ppermute only.
A program may use at most 128 MiB of HBM per device.

```python
import math
import jax
import jax.numpy as jnp
import numpy as np
from jax import lax

COLS = 256
BANDS = 8
PASSES = 3
RADIUS = 16
BROWS = 4
BCOLS = 128
ITERS = 4
TAPS = 33
DATES = 16
ROWS = 128
NCB = 2
NBLK_DEV = 16
NBLK = 64
TILES = 4
TROWS = 64
MROWS = 256
MOST = 8


def touch_ends(entries, rng, smallest, largest):
    longest = entries.shape.index(max(entries.shape))
    spots = []
    for shift in (0, 1):
        where = [jax.random.randint(jax.random.fold_in(rng, axis), (), 0, length) for axis, length in enumerate(entries.shape)]
        where[longest] = (where[longest] + shift) % entries.shape[longest]
        spots.append(tuple(where))
    return entries.at[spots[0]].set(smallest).at[spots[1]].set(largest)


def levels(key, dims, split, low, largest):
    level, own = 1.0, jax.random.fold_in(key, 6)
    for dim, shards_of in split:
        heights = jnp.exp(jax.random.uniform(jax.random.fold_in(own, dim), (shards_of,), jnp.float32, low / len(split), largest / len(split)))
        level = level * jnp.repeat(heights, dims[dim] // shards_of).reshape([-1 if axis == dim else 1 for axis in range(len(dims))])
    return level


def assign_block(own_key, own, number, rows, number_of, top, reach, skew):
    ranking = jax.random.permutation(own_key, number_of)
    packed, ordinary = load_shares(number_of, rows * top, reach, skew, True), load_shares(number_of, rows * top, reach, skew, False)
    places = jnp.arange(number_of)

    def named(lengths, turn):
        used = int((lengths > 0).sum())
        fixed = max(1, used // 4)
        moved = fixed + (places - fixed + turn * (used - fixed)) % max(1, number_of - fixed)
        return jnp.zeros((number_of,), jnp.int32).at[ranking[jnp.where(places < fixed, places, moved)]].set(jnp.asarray(lengths, jnp.int32))

    lengths = jnp.where(number % 4 == 0, named(packed, number // 4), named(ordinary, number - number // 4 - 1))
    mixed = jax.random.permutation(jax.random.fold_in(own, 3), number_of)
    giver, receiver = mixed[0:number_of // 2 * 2:2], mixed[1:number_of // 2 * 2:2]
    room = jnp.minimum(lengths[giver] - 1, reach - lengths[receiver]) // 2
    room = jnp.where((giver == ranking[0]) | (receiver == ranking[0]) | (lengths[receiver] == 0), 0, jnp.maximum(room, 0))
    moved = jax.random.randint(jax.random.fold_in(own, 4), (number_of // 2,), 0, 1 << 20) % (room + 1)
    lengths = lengths.at[giver].add(-moved).at[receiver].add(moved)
    members = jnp.searchsorted(jnp.cumsum(lengths), jnp.arange(rows * top), side="right").astype(jnp.int32)
    table = members.reshape(top, rows).T
    table = table[jax.random.permutation(jax.random.fold_in(own, 1), rows)]
    turn = jax.random.randint(jax.random.fold_in(own, 2), (rows, 1), 0, top)
    return jnp.take_along_axis(table, (jnp.arange(top)[None, :] + turn) % top, axis=1)


def load_shares(amount, total, most, skew, full):
    loads = [(1 << 20) // math.isqrt(grade ** skew) + 1 for grade in range(1, amount + 1)]
    largest = most if full else min(most, max(-(-total // amount), total * loads[0] // sum(loads)))
    least = 1 if total - largest >= amount - 1 else 0
    holding, rest = [largest] + [least] * (amount - 1), total - largest - least * (amount - 1)
    while rest > 0:
        movable = [i for i in range(1, amount) if holding[i] < largest] or [i for i in range(1, amount) if holding[i] < most]
        whole, left = sum([loads[i] for i in movable]), rest
        for i in movable:
            more = min(most - holding[i], max(1, left * loads[i] // whole), rest)
            holding[i] = holding[i] + more
            rest = rest - more
    return np.array(holding)


def bell_draw(rng, shape, width, bound, split=(), kind=jnp.bfloat16):
    loudness = levels(rng, shape, split, -0.22, 0.18) if split else 1.0
    result = jax.random.normal(rng, shape, jnp.float32) * width * loudness
    return jnp.minimum(jnp.maximum(result, -bound), bound).astype(kind)


def setup_inputs(seed: int = 0, part: int = 0) -> dict:
    streams_of = jax.random.split(jax.random.key(seed), 9)
    part_splits = jax.random.split(jax.random.fold_in(streams_of[8], part), 9)
    reflect = bell_draw(part_splits[0], (DATES, BANDS, ROWS, COLS), 1.0, 6.0, ((0, 2), (1, 2), (2, 4)), jnp.float32)
    kernels = jnp.clip(jnp.exp(math.log(2.0) - 2.3025851 * jax.random.uniform(streams_of[1], (PASSES, BANDS, TAPS), jnp.float32) ** levels(streams_of[1], (PASSES, BANDS, TAPS), ((1, 2),), -0.2, 0.2)), 0.2, 2.0)
    strength = jnp.clip(0.2 + 0.400000021 * jax.random.uniform(streams_of[2], (PASSES, BANDS), jnp.float32) ** levels(streams_of[2], (PASSES, BANDS), ((1, 2),), -0.2, 0.2), 0.2, 0.6)
    destinations_keys = jax.random.split(jax.random.fold_in(part_splits[3], 1), NBLK // NBLK_DEV)
    destinations_turns = jax.random.permutation(jax.random.fold_in(part_splits[3], 3), NBLK // NBLK_DEV)
    destinations = jax.vmap(lambda own, number: assign_block(jax.random.fold_in(part_splits[3], 2), own, number, NBLK_DEV, TILES, 1, MOST, 2))(destinations_keys, destinations_turns).reshape((NBLK, 1))
    offsets = touch_ends(jax.random.randint(part_splits[4], (NBLK,), 0, TROWS - BROWS + 1), jax.random.fold_in(part_splits[4], 1), 0, TROWS - BROWS).astype(jnp.int32)
    counts = touch_ends(jax.random.randint(part_splits[5], (DATES, TILES), 1, TROWS * BCOLS + 1), jax.random.fold_in(part_splits[5], 1), 1, TROWS * BCOLS).astype(jnp.int32)
    resample_rows = bell_draw(part_splits[6], (TILES, BROWS, BROWS), BROWS ** -0.5, 3.0, ((0, 4),), jnp.float32)
    resample_columns = bell_draw(part_splits[7], (TILES, BCOLS, BCOLS), BCOLS ** -0.5, 0.5, ((0, 4),), jnp.float32)
    return {"reflect": reflect, "kernels": kernels, "strength": strength, "destinations": destinations, "offsets": offsets, "counts": counts, "resample_rows": resample_rows, "resample_columns": resample_columns}


highest = lax.Precision.HIGHEST
smooth_sq = 0.01

def band_matrix(weights, count_out, count_in, lead_shift):
    tap_count = weights.shape[1]
    offset = jnp.arange(count_in)[None, :] - jnp.arange(count_out)[:, None] + lead_shift
    matrix = jnp.zeros((weights.shape[0], count_out, count_in), jnp.float32)
    for tap_index in range(tap_count):
        chosen = (offset == tap_index).astype(jnp.float32)
        matrix = matrix + weights[:, tap_index, None, None] * chosen[None, :, :]
    return matrix

def reference(reflect, kernels, strength, destinations, offsets, counts, resample_rows, resample_columns):
    values = reflect
    for pass_index in range(PASSES):
        norm_taps = kernels[pass_index] / lax.optimization_barrier(jnp.sum(kernels[pass_index], axis=1, keepdims=True))
        row_matrix = band_matrix(norm_taps, ROWS, ROWS, RADIUS)
        column_matrix = band_matrix(norm_taps, COLS, COLS, RADIUS)
        row_pass = jnp.einsum('bij,tbjc->tbic', row_matrix, values, precision=highest)
        blurred = jnp.einsum('tbrj,bcj->tbrc', row_pass, column_matrix, precision=highest)
        values = values + strength[pass_index][None, :, None, None] * (values - blurred)
    shaped = values.reshape(DATES, BANDS, ROWS // BROWS, BROWS, NCB, BCOLS)
    blocks = shaped.transpose(2, 4, 0, 1, 3, 5).reshape(NBLK, DATES, BANDS, BROWS, BCOLS)
    targets = destinations[:, 0]
    block_rows = resample_rows[targets]
    block_columns = resample_columns[targets]
    row_pass = jnp.einsum('nij,ntbjc->ntbic', block_rows, blocks, precision=highest)
    resampled = jnp.einsum('ntbic,ncv->ntbiv', row_pass, block_columns, precision=highest)
    map_row = targets[:, None] * TROWS + offsets[:, None] + jnp.arange(BROWS, dtype=jnp.int32)[None, :]
    flat_rows = resampled.transpose(0, 3, 1, 2, 4).reshape(NBLK * BROWS, DATES, BANDS, BCOLS)
    assembled = jax.ops.segment_sum(flat_rows, map_row.reshape(-1).astype(jnp.int32), num_segments=MROWS)
    stacked = assembled.transpose(1, 2, 0, 3).reshape(DATES, BANDS, MROWS * BCOLS)
    count_values = counts.astype(jnp.float32)
    mean_count = jnp.sum(count_values) / (DATES * TILES)
    weight_tile = count_values / (count_values + mean_count)
    weight_pixel = jnp.repeat(weight_tile, TROWS * BCOLS, axis=1)
    numerator = lax.optimization_barrier(jnp.sum(weight_pixel[:, None, :] * stacked, axis=0))
    denominator = lax.optimization_barrier(jnp.sum(weight_pixel, axis=0))
    estimate = numerator / denominator[None, :]
    for iter_index in range(ITERS):
        distance = jnp.sqrt(lax.optimization_barrier(jnp.sum((stacked - estimate[None]) ** 2, axis=1)) + smooth_sq)
        scaled = weight_pixel / distance
        numerator = lax.optimization_barrier(jnp.sum(scaled[:, None, :] * stacked, axis=0))
        denominator = lax.optimization_barrier(jnp.sum(scaled, axis=0))
        estimate = numerator / denominator[None, :]
    return estimate.reshape(BANDS, MROWS, BCOLS)
```

```python
import functools

import jax
import jax.numpy as jnp
from jax import lax
from jax.experimental import pallas as pl
from jax.experimental.pallas import tpu as pltpu
from jax.sharding import PartitionSpec as P

BROWS = 4
BCOLS = 128
ITERS = 4
LANES = 128

smooth_sq = 0.01
f32 = jnp.float32
bf16 = jnp.bfloat16


def split(x):
    high = x.astype(bf16)
    return high, (x - high.astype(f32)).astype(bf16)


def mm(a, b):
    return jnp.dot(a, b, preferred_element_type=f32)


def toeplitz_kernel(row_ref, col_ref, rh_ref, rl_ref, ch_ref, cl_ref):
    count, wide = row_ref.shape
    for src, high_ref, low_ref in ((row_ref, rh_ref, rl_ref), (col_ref, ch_ref, cl_ref)):
        size = high_ref.shape[1]
        for k in range(count):
            line = jnp.broadcast_to(src[k : k + 1, :], (size, wide))
            band = pltpu.roll(line, 0, 1, stride=1, stride_axis=0)[:, :size]
            high, low = split(band)
            high_ref[k] = high
            low_ref[k] = low


def wrapped(taps, wide):
    taps_count = taps.shape[-1]
    half = taps_count // 2
    pad = jnp.zeros(taps.shape[:-1] + (wide - taps_count,), f32)
    return jnp.concatenate([taps[..., half:], pad, taps[..., :half]], axis=-1)


def correct_kernel(
    gain_ref, x_ref, rh_ref, rl_ref, ch_ref, cl_ref, base_ref, rows_ref, out_ref, *, passes, bands
):
    spaces, per, strip, width = x_ref.shape
    rows = spaces * strip
    halves = width // BCOLS
    done = [None] * per
    for band in range(bands):
        members = range(band, per, bands)
        images = [
            jnp.concatenate([x_ref[s, i] for s in range(spaces)], axis=0) for i in members
        ]
        for step in range(passes):
            k = step * bands + band
            rh, rl, ch, cl = rh_ref[k], rl_ref[k], ch_ref[k], cl_ref[k]
            gain = gain_ref[k]
            parts = []
            for image in images:
                xh, xl = split(image)
                parts.append(mm(rh, xh) + (mm(rl, xh) + mm(rh, xl)))
            stacked = jnp.concatenate(parts, axis=0)
            yh, yl = split(stacked)
            blurred = mm(yh, ch) + (mm(yl, ch) + mm(yh, cl))
            images = [
                gain * image - blurred[q * rows : (q + 1) * rows]
                for q, image in enumerate(images)
            ]
        for i, image in zip(members, images):
            done[i] = jnp.concatenate(
                [image[:, h * BCOLS : (h + 1) * BCOLS] for h in range(halves)], axis=0
            )
    line = lax.broadcasted_iota(jnp.int32, (out_ref.shape[0] * out_ref.shape[2], rows * halves), 0)
    first = line - base_ref[...]
    placer = jnp.zeros(line.shape, f32)
    for i in range(BROWS):
        placer = jnp.where(first == i, rows_ref[i : i + 1, :], placer)
    ah, al = split(placer)
    share = out_ref.shape[2]
    for i in range(per):
        zh, zl = split(done[i])
        laid = mm(ah, zh) + (mm(al, zh) + mm(ah, zl))
        for d in range(out_ref.shape[0]):
            out_ref[d, i] = laid[d * share : (d + 1) * share]


def median_kernel(weight_ref, y_ref, cols_ref, out_ref, full_ref, *, spaces, dates, cores, bands, local_dates):
    sources, per, share, width = y_ref.shape
    kh, kl = split(cols_ref[...])
    for s in range(sources):
        block = y_ref[s].reshape(per * share, width)
        bh, bl = split(block)
        full = mm(bh, kh) + (mm(bl, kh) + mm(bh, kl))
        full_ref[s] = full.reshape(per, share, width)
    total_bands = cores * bands
    where = [[None] * total_bands for _ in range(dates * local_dates)]
    for z in range(spaces):
        for x in range(dates):
            for c in range(cores):
                for i in range(per):
                    t, b = divmod(z * per + i, bands)
                    where[x * local_dates + t][c * bands + b] = ((z * dates + x) * cores + c, i)
    tile = min(share, 8)
    for start in range(0, share, tile):
        rows = pl.ds(start, tile)

        def load(t):
            return [full_ref[s, i, rows, :] for s, i in where[t]]

        number = [jnp.zeros((tile, width), f32)] * total_bands
        weight_sum = f32(0)
        for t, _ in enumerate(where):
            w = weight_ref[t]
            weight_sum = weight_sum + w
            number = [n + w * v for n, v in zip(number, load(t))]
        estimate = [n / weight_sum for n in number]
        for _ in range(ITERS):
            number = [jnp.zeros((tile, width), f32)] * total_bands
            below = jnp.zeros((tile, width), f32)
            for t, _ in enumerate(where):
                values = load(t)
                square = jnp.full((tile, width), smooth_sq, f32)
                for v, e in zip(values, estimate):
                    d = v - e
                    square = square + d * d
                scaled = weight_ref[t] / jnp.sqrt(square)
                below = below + scaled
                number = [n + scaled * v for n, v in zip(number, values)]
            estimate = [n / below for n in number]
        for x in range(dates):
            for b in range(total_bands):
                out_ref[x * cores + b // bands, b % bands, rows, :] = estimate[b]


def vmem(count):
    return [pl.BlockSpec(memory_space=pltpu.VMEM)] * count


def smem():
    return pl.BlockSpec(memory_space=pltpu.SMEM)


def local(
    reflect, kernels, strength, destinations, offsets, counts, resample_rows, resample_columns
):
    spaces, dates, cores = (lax.axis_size(a) for a in ("space", "date", "band"))
    local_dates, bands, strip, width = reflect.shape
    passes = kernels.shape[0]
    blocks = offsets.shape[0]
    rows = spaces * strip
    halves = width // BCOLS
    tile_rows = blocks * BROWS
    sources = spaces * dates * cores
    share = tile_rows // (dates * cores)
    per = local_dates * bands // spaces

    images = reflect.reshape(local_dates * bands, strip, width)
    whole = lax.all_to_all(images, "space", split_axis=0, concat_axis=0, tiled=True)

    packed = jnp.concatenate(
        [
            destinations[:, 0].astype(f32),
            offsets.astype(f32),
            resample_rows.reshape(-1),
            counts[:, 0].astype(f32),
        ]
    )
    used = packed.shape[0]
    lanes = -(-used // LANES) * LANES
    packed = jnp.pad(packed, (0, lanes - used))
    spread = jnp.broadcast_to(packed[None, None, :], (spaces * dates, 1, lanes))
    small = lax.all_to_all(spread, ("space", "date"), split_axis=0, concat_axis=0, tiled=True)
    small = small.reshape(spaces, dates, lanes)

    here = bands if per % bands == 0 else per
    if here != bands:
        first_band = (lax.axis_index("space") * per) % bands
        kernels = lax.dynamic_slice_in_dim(kernels, first_band, here, axis=1)
        strength = lax.dynamic_slice_in_dim(strength, first_band, here, axis=1)
    taps = kernels / jnp.sum(kernels, axis=2, keepdims=True)
    wide = max(rows, width) + LANES
    row_taps = wrapped(taps * strength[:, :, None], wide).reshape(passes * here, wide)
    column_taps = wrapped(taps[:, :, ::-1], wide).reshape(passes * here, wide)
    gains = (1.0 + strength).reshape(-1)
    count = passes * here
    rh, rl, ch, cl = pl.pallas_call(
        toeplitz_kernel,
        out_shape=[jax.ShapeDtypeStruct((count, rows, rows), bf16)] * 2
        + [jax.ShapeDtypeStruct((count, width, width), bf16)] * 2,
        in_specs=vmem(2),
        out_specs=vmem(4),
        name="toeplitz",
    )(row_taps, column_taps)

    of_strip = small[:, 0, :]
    targets = of_strip[:, :blocks]
    starts = of_strip[:, blocks : 2 * blocks]
    matrices = of_strip[:, 2 * blocks : 2 * blocks + BROWS * BROWS].reshape(spaces, BROWS, BROWS)

    def by_row(table):
        table = table.reshape(spaces, strip // BROWS, halves).transpose(2, 0, 1)
        table = jnp.broadcast_to(table[..., None], table.shape + (BROWS,))
        return table.reshape(1, halves * rows)

    base = by_row(targets * tile_rows + starts).astype(jnp.int32)
    target_of = by_row(targets)
    repeats = halves * rows // BROWS
    entries = jnp.zeros((BROWS, halves * rows), f32)
    for g in range(spaces):
        entries = entries + jnp.where(target_of == g, jnp.tile(matrices[g], (1, repeats)), 0.0)

    laid = pl.pallas_call(
        functools.partial(correct_kernel, passes=passes, bands=here),
        out_shape=jax.ShapeDtypeStruct((sources, per, share, BCOLS), f32),
        in_specs=[smem()] + vmem(7),
        out_specs=pl.BlockSpec(memory_space=pltpu.VMEM),
        name="correct",
    )(gains, whole.reshape(spaces, per, strip, width), rh, rl, ch, cl, base, entries)

    pixels = lax.all_to_all(
        laid, ("space", "date", "band"), split_axis=0, concat_axis=0, tiled=True
    )

    counted = small[:, :, 2 * blocks + BROWS * BROWS :][:, :, :local_dates]
    mean_count = jnp.sum(counted) / (spaces * dates * local_dates)
    own = lax.dynamic_slice_in_dim(counted, lax.axis_index("space"), 1, axis=0).reshape(-1)
    weights = own / (own + mean_count)

    parts = pl.pallas_call(
        functools.partial(
            median_kernel,
            spaces=spaces,
            dates=dates,
            cores=cores,
            bands=bands,
            local_dates=local_dates,
        ),
        out_shape=jax.ShapeDtypeStruct((dates * cores, bands, share, BCOLS), f32),
        in_specs=[smem()] + vmem(2),
        out_specs=pl.BlockSpec(memory_space=pltpu.VMEM),
        scratch_shapes=[pltpu.VMEM((sources, per, share, BCOLS), f32)],
        name="median",
    )(weights, pixels, resample_columns[0])

    shares = lax.all_to_all(parts, ("date", "band"), split_axis=0, concat_axis=0, tiled=True)
    return shares.transpose(1, 0, 2, 3).reshape(bands, tile_rows, BCOLS)


def solution(mesh):
    in_specs = (
        P("date", "band", ("groups", "space"), None),
        P(None, "band", None),
        P(None, "band"),
        P(("groups", "space"), None),
        P(("groups", "space")),
        P("date", ("groups", "space")),
        P(("groups", "space"), None, None),
        P(("groups", "space"), None, None),
    )
    out_specs = P("band", ("groups", "space"), None)
    return jax.shard_map(local, mesh=mesh, in_specs=in_specs, out_specs=out_specs, check_vma=False)
```

```python
import functools

import jax
import jax.numpy as jnp
from jax import lax
from jax.experimental import pallas as pl
from jax.experimental.pallas import tpu as pltpu
from jax.sharding import PartitionSpec as P

BROWS = 4
BCOLS = 128
ITERS = 4
LANES = 128
SUBLANES = 8


smooth_sq = 0.01
f32 = jnp.float32
bf16 = jnp.bfloat16


def split(x):
    high = x.astype(bf16)
    return high, (x - high.astype(f32)).astype(bf16)


def mm(a, b):
    return jnp.dot(a, b, preferred_element_type=f32)


def total(terms):
    terms = list(terms)
    while len(terms) > 1:
        terms = [a + b for a, b in zip(terms[::2], terms[1::2])] + terms[len(terms) & ~1 :]
    return terms[0]


def round_up(value, unit):
    return -(-value // unit) * unit


def vmem(count):
    return [pl.BlockSpec(memory_space=pltpu.VMEM)] * count


def smem():
    return pl.BlockSpec(memory_space=pltpu.SMEM)


def params(mib):
    return pltpu.CompilerParams(vmem_limit_bytes=mib << 20)


def upright(line):
    size = line.shape[1]
    eye = lax.broadcasted_iota(jnp.int32, (size, size), 0) == lax.broadcasted_iota(
        jnp.int32, (size, size), 1
    )
    spread = jnp.broadcast_to(line, (size, size))
    return jnp.sum(jnp.where(eye, spread, 0.0), axis=1, keepdims=True)


def pack_kernel(
    target_ref, start_ref, rows_ref, images_ref, *refs, spaces, chunks, part, halves, table_lines
):
    outs, sem = refs[:-1], refs[-1]
    width = images_ref.shape[1]
    size = images_ref.shape[0] // spaces // chunks
    strip = size // part
    own = lax.axis_index("space")
    copies = []
    for q in range(chunks):
        for d in range(spaces):
            to = lax.rem(own + d, spaces)
            out = outs[q * spaces + d]
            copy = pltpu.make_async_copy(
                images_ref.at[pl.ds(pl.multiple_of((to * chunks + q) * size, size), size)],
                out.at[pl.ds(0, size)],
                sem.at[q * spaces + d],
            )
            copy.start()
            copies.append(copy)
    blocks = target_ref.shape[1]
    rows = spaces * strip
    matrix = rows_ref[0]
    lane = lax.broadcasted_iota(jnp.int32, (BROWS, width), 1) & (BROWS - 1)
    spread = jnp.zeros((BROWS, width), f32)
    for k in range(BROWS):
        spread = jnp.where(lane == k, jnp.broadcast_to(matrix[:, k : k + 1], spread.shape), spread)
    target = upright(target_ref[...].astype(f32))
    start = target * f32(blocks * BROWS) + upright(start_ref[...].astype(f32))
    length = halves * rows
    place = lax.broadcasted_iota(jnp.int32, (blocks, length), 1)
    block = lax.broadcasted_iota(jnp.int32, (blocks, length), 0)
    first = own * strip
    shift = halves.bit_length() - 1
    low = (block & (halves - 1)) * rows + (block >> shift) * BROWS + first
    inside = (place >= low) & (place < low + BROWS)
    lines = [
        jnp.sum(jnp.where(inside, table, 0.0), axis=0, keepdims=True) for table in (start, target)
    ]
    for d in range(spaces):
        out = outs[d]
        out[size:, :] = jnp.zeros((out.shape[0] - size, width), f32)
        out[size : size + BROWS, :] = spread
        for t, line in enumerate(lines):
            for k in range(table_lines):
                at = size + BROWS + t * table_lines + k
                used = min(width, length - k * width)
                out[at : at + 1, 0:used] = line[:, k * width : k * width + used]
    for copy in copies:
        copy.wait()


def toeplitz_kernel(row_ref, col_ref, rh_ref, rl_ref, ch_ref, cl_ref):
    count, wide = row_ref.shape
    for src, high_ref, low_ref in ((row_ref, rh_ref, rl_ref), (col_ref, ch_ref, cl_ref)):
        size = high_ref.shape[1]
        for k in range(count):
            line = jnp.broadcast_to(src[k : k + 1, :], (size, wide))
            band = pltpu.roll(line, 0, 1, stride=1, stride_axis=0)[:, :size]
            high, low = split(band)
            high_ref[k] = high
            low_ref[k] = low


def wrapped(taps, wide):
    taps_count = taps.shape[-1]
    half = taps_count // 2
    pad = jnp.zeros(taps.shape[:-1] + (wide - taps_count,), f32)
    return jnp.concatenate([taps[..., half:], pad, taps[..., :half]], axis=-1)


def correct_kernel(gain_ref, *refs, spaces, part, first, passes, bands, share, table_lines):
    x_refs, refs, state = refs[:spaces], refs[spaces:-1], refs[-1]
    rh_ref, rl_ref, ch_ref, cl_ref = refs[:4]
    rows, width = state.shape[1:]
    strip = rows // spaces
    tables = part * strip
    halves = width // BCOLS
    length = halves * rows
    if first == 0:
        count_ref, out_ref, ah_ref, al_ref = refs[4:]
    else:
        ah_ref, al_ref, out_ref = refs[4:]
    own = lax.axis_index("space")
    for d in range(spaces):
        src = lax.rem(own + (spaces - d), spaces)
        at = pl.ds(pl.multiple_of(src * strip, strip), strip)
        for i in range(part):
            state[i, at, :] = x_refs[d][i * strip : (i + 1) * strip, :]
    if first == 0:
        def table(t):
            lines = []
            for k in range(table_lines):
                at = tables + BROWS + t * table_lines + k
                used = min(width, length - k * width)
                lines.append(total(x[at : at + 1, 0:used] for x in x_refs))
            return jnp.concatenate(lines, axis=1)

        start, target = table(0), table(1)
        entries = jnp.zeros((BROWS, length), f32)
        for d in range(spaces):
            src = lax.rem(own + (spaces - d), spaces).astype(f32)
            matrix = x_refs[d][tables : tables + BROWS, :]
            matrix = jnp.concatenate([matrix] * (length // width), axis=1)
            entries = jnp.where(target == src, matrix, entries)
        map_rows = ah_ref.shape[0]
        line = lax.broadcasted_iota(jnp.int32, (map_rows, length), 0)
        offset = line - start.astype(jnp.int32)
        placer = jnp.zeros((map_rows, length), f32)
        for i in range(BROWS):
            placer = jnp.where(offset == i, entries[i : i + 1, :], placer)
        ah, al = split(placer)
        ah_ref[...] = ah
        al_ref[...] = al
    slots = [(first + i) % bands for i in range(part)]
    for step in range(passes):
        middle = []
        for i, slot in enumerate(slots):
            k = step * bands + slot
            xh, xl = split(state[i])
            rh = rh_ref[k]
            both = mm(jnp.concatenate([rh, rh], axis=1), jnp.concatenate([xh, xl], axis=0))
            middle.append(split(both + mm(rl_ref[k], xh)))
        for i, slot in enumerate(slots):
            k = step * bands + slot
            yh, yl = middle[i]
            both = mm(jnp.concatenate([yh, yl], axis=0), ch_ref[k])
            blurred = both[:rows] + both[rows:] + mm(yh, cl_ref[k])
            state[i] = gain_ref[k] * state[i] - blurred
    ah, al = ah_ref[...], al_ref[...]
    map_rows = ah.shape[0]
    stacked = jnp.concatenate([ah, al], axis=0)
    for i in range(0, part, 2):
        pair = range(i, min(i + 2, part))
        z = jnp.concatenate(
            [
                jnp.concatenate(
                    [state[j, :, h * BCOLS : (h + 1) * BCOLS] for h in range(halves)], axis=0
                )
                for j in pair
            ],
            axis=1,
        )
        zh, zl = split(z)
        both = mm(stacked, zh)
        laid = both[:map_rows] + both[map_rows:] + mm(ah, zl)
        for p, j in enumerate(pair):
            for d in range(out_ref.shape[0]):
                out_ref[d, j * share : (j + 1) * share, :] = laid[
                    d * share : (d + 1) * share, p * BCOLS : (p + 1) * BCOLS
                ]
    if first == 0:
        dates = count_ref.shape[1]
        counted = count_ref[...].astype(f32)
        for d in range(out_ref.shape[0]):
            out_ref[d, part * share :, :] = jnp.zeros((SUBLANES, BCOLS), f32)
            out_ref[d, part * share : part * share + 1, 0:dates] = counted


def columns_of(block, kh, kl):
    bh, bl = split(block)
    both = mm(jnp.concatenate([bh, bl], axis=0), kh)
    size = block.shape[0]
    return both[:size] + both[size:] + mm(bh, kl)


def columns_kernel(y_ref, cols_ref, full_ref, weight_ref, *, spaces, dates, cores, local_dates):
    sources, part, share, width = full_ref.shape
    kh, kl = split(cols_ref[0])
    for s in range(sources):
        full = columns_of(y_ref[s, : part * share, :], kh, kl)
        full_ref[s] = full.reshape(part, share, width)
    at = slice(part * share, part * share + 1)
    summed = total(y_ref[s, at, :] for s in range(0, sources, cores))
    mean_count = jnp.sum(summed, axis=1, keepdims=True) / f32(spaces * dates * local_dates)
    own = lax.axis_index("space")
    for x in range(dates):
        counted = y_ref[(own * dates + x) * cores, at, :]
        weight = counted / (counted + mean_count)
        for t in range(local_dates):
            weight_ref[x * local_dates + t] = jnp.broadcast_to(
                weight[:, t : t + 1], weight_ref.shape[1:]
            )


def median_kernel(weight_ref, cols_ref, first_ref, *refs, spaces, dates, cores, bands, local_dates):
    sources, part, share, width = first_ref.shape
    chunks = local_dates * bands // spaces // part
    y_refs, refs = refs[: chunks - 1], refs[chunks - 1 :]
    out_refs, refs = refs[:cores], refs[cores:]
    full_refs = [first_ref] + list(refs[: chunks - 1])
    result = refs[-1]
    kh, kl = split(cols_ref[0])
    for y_ref, full_ref in zip(y_refs, full_refs[1:]):
        for s in range(sources):
            full_ref[s] = columns_of(y_ref[s], kh, kl).reshape(part, share, width)
    total_bands = cores * bands
    where = [[None] * total_bands for _ in range(dates * local_dates)]
    for z in range(spaces):
        for x in range(dates):
            for c in range(cores):
                for i in range(part * chunks):
                    t, b = divmod(z * part * chunks + i, bands)
                    where[x * local_dates + t][c * bands + b] = (
                        i // part,
                        (z * dates + x) * cores + c,
                        i % part,
                    )
    tile = weight_ref.shape[1]
    for start in range(0, share, tile):
        rows = pl.ds(start, tile)

        def load(t):
            return [full_refs[q][s, i, rows, :] for q, s, i in where[t]]

        number = [jnp.zeros((tile, width), f32)] * total_bands
        below = jnp.zeros((tile, width), f32)
        for t, _ in enumerate(where):
            w = weight_ref[t]
            below = below + w
            number = [n + w * v for n, v in zip(number, load(t))]
        estimate = [n / below for n in number]
        for _ in range(ITERS):
            number = [jnp.zeros((tile, width), f32)] * total_bands
            below = jnp.zeros((tile, width), f32)
            for t, _ in enumerate(where):
                values = load(t)
                squares = []
                for v, e in zip(values, estimate):
                    d = v - e
                    squares.append(d * d)
                scaled = weight_ref[t] / jnp.sqrt(total(squares) + smooth_sq)
                below = below + scaled
                number = [n + scaled * v for n, v in zip(number, values)]
            estimate = [n / below for n in number]
        for b in range(total_bands):
            result[b // bands, b % bands, rows, :] = estimate[b]
    own = lax.axis_index("band")
    for k in range(cores):
        out_refs[k][...] = result[lax.rem(own + k, cores)]


def place_kernel(*refs, dates, cores):
    out_ref = refs[-1]
    share = refs[0].shape[1]
    x, c = lax.axis_index("date"), lax.axis_index("band")
    for dx in range(dates):
        for dc in range(cores):
            j = lax.rem(x + (dates - dx), dates) * cores + lax.rem(c + (cores - dc), cores)
            at = pl.ds(pl.multiple_of(j * share, share), share)
            out_ref[:, at, :] = refs[dx * cores + dc][...]


def local(
    reflect, kernels, strength, destinations, offsets, counts, resample_rows, resample_columns
):
    spaces, dates, cores = (lax.axis_size(a) for a in ("space", "date", "band"))
    local_dates, bands, strip, width = reflect.shape
    passes = kernels.shape[0]
    blocks = offsets.shape[0]
    rows = spaces * strip
    halves = width // BCOLS
    length = halves * rows
    table_lines = -(-length // width)
    tile_rows = blocks * BROWS
    sources = spaces * dates * cores
    share = tile_rows // (dates * cores)
    tile = min(share, SUBLANES)
    per = local_dates * bands // spaces
    chunks = 2 if per % 2 == 0 else 1
    part = per // chunks

    images = reflect.reshape(local_dates * bands * strip, width)
    extra_lines = round_up(BROWS + 2 * table_lines, SUBLANES)
    packed = pl.pallas_call(
        functools.partial(
            pack_kernel,
            spaces=spaces,
            chunks=chunks,
            part=part,
            halves=halves,
            table_lines=table_lines,
        ),
        out_shape=[
            jax.ShapeDtypeStruct((part * strip + (extra_lines if q == 0 else 0), width), f32)
            for q in range(chunks)
            for _ in range(spaces)
        ],
        in_specs=vmem(3) + [pl.BlockSpec(memory_space=pl.ANY)],
        out_specs=vmem(chunks * spaces),
        scratch_shapes=[pltpu.SemaphoreType.DMA((chunks * spaces,))],
        compiler_params=params(8),
        name="pack",
    )(destinations.reshape(1, blocks), offsets.reshape(1, blocks), resample_rows, images)
    strips = []
    for q in range(chunks):
        mine = packed[q * spaces : (q + 1) * spaces]
        strips.append(
            [mine[0]]
            + [
                lax.ppermute(mine[d], "space", [(i, (i + d) % spaces) for i in range(spaces)])
                for d in range(1, spaces)
            ]
        )

    here = bands if per % bands == 0 else per
    if here != bands:
        first_band = (lax.axis_index("space") * per) % bands
        kernels = lax.dynamic_slice_in_dim(kernels, first_band, here, axis=1)
        strength = lax.dynamic_slice_in_dim(strength, first_band, here, axis=1)
    taps = kernels / jnp.sum(kernels, axis=2, keepdims=True)
    wide = max(rows, width) + LANES
    row_taps = wrapped(taps * strength[:, :, None], wide).reshape(passes * here, wide)
    column_taps = wrapped(taps[:, :, ::-1], wide).reshape(passes * here, wide)
    gains = (1.0 + strength).reshape(-1)
    count = passes * here
    matrices = pl.pallas_call(
        toeplitz_kernel,
        out_shape=[jax.ShapeDtypeStruct((count, rows, rows), bf16)] * 2
        + [jax.ShapeDtypeStruct((count, width, width), bf16)] * 2,
        in_specs=vmem(2),
        out_specs=vmem(4),
        compiler_params=params(16),
        name="toeplitz",
    )(row_taps, column_taps)

    pixels = []
    placer = None
    for q in range(chunks):
        out_shape = [
            jax.ShapeDtypeStruct((sources, part * share + (SUBLANES if q == 0 else 0), BCOLS), f32)
        ]
        if q == 0:
            out_shape += [jax.ShapeDtypeStruct((spaces * tile_rows, length), bf16)] * 2
            extra = [counts.reshape(1, local_dates)]
        else:
            extra = placer
        results = pl.pallas_call(
            functools.partial(
                correct_kernel,
                spaces=spaces,
                part=part,
                first=q * part,
                passes=passes,
                bands=here,
                share=share,
                table_lines=table_lines,
            ),
            out_shape=out_shape,
            in_specs=[smem()] + vmem(spaces + 4 + len(extra)),
            out_specs=vmem(len(out_shape)),
            scratch_shapes=[pltpu.VMEM((part, rows, width), f32)],
            compiler_params=params(20),
            name="correct",
        )(gains, *strips[q], *matrices, *extra)
        if q == 0:
            placer = results[1:]
        pixels.append(
            lax.all_to_all(
                results[0], ("space", "date", "band"), split_axis=0, concat_axis=0, tiled=True
            )
        )

    full, weights = pl.pallas_call(
        functools.partial(
            columns_kernel, spaces=spaces, dates=dates, cores=cores, local_dates=local_dates
        ),
        out_shape=[
            jax.ShapeDtypeStruct((sources, part, share, BCOLS), f32),
            jax.ShapeDtypeStruct((dates * local_dates, tile, BCOLS), f32),
        ],
        in_specs=vmem(2),
        out_specs=vmem(2),
        compiler_params=params(8),
        name="columns",
    )(pixels[0], resample_columns)
    shares = pl.pallas_call(
        functools.partial(
            median_kernel,
            spaces=spaces,
            dates=dates,
            cores=cores,
            bands=bands,
            local_dates=local_dates,
        ),
        out_shape=[jax.ShapeDtypeStruct((bands, share, BCOLS), f32)] * cores,
        in_specs=vmem(2 + chunks),
        out_specs=vmem(cores),
        scratch_shapes=[pltpu.VMEM((sources, part, share, BCOLS), f32)] * (chunks - 1)
        + [pltpu.VMEM((cores, bands, share, BCOLS), f32)],
        compiler_params=params(12),
        name="median",
    )(weights, resample_columns, full, *pixels[1:])

    pieces = []
    for dx in range(dates):
        for dc in range(cores):
            piece = shares[dc]
            if dx or dc:
                pairs = [
                    (x * cores + c, (x + dx) % dates * cores + (c + dc) % cores)
                    for x in range(dates)
                    for c in range(cores)
                ]
                piece = lax.ppermute(piece, ("date", "band"), pairs)
            pieces.append(piece)
    return pl.pallas_call(
        functools.partial(place_kernel, dates=dates, cores=cores),
        out_shape=jax.ShapeDtypeStruct((bands, tile_rows, BCOLS), f32),
        in_specs=vmem(dates * cores),
        out_specs=pl.BlockSpec(memory_space=pltpu.VMEM),
        compiler_params=params(4),
        name="place",
    )(*pieces)


def solution(mesh):
    in_specs = (
        P("date", "band", ("groups", "space"), None),
        P(None, "band", None),
        P(None, "band"),
        P(("groups", "space"), None),
        P(("groups", "space")),
        P("date", ("groups", "space")),
        P(("groups", "space"), None, None),
        P(("groups", "space"), None, None),
    )
    out_specs = P("band", ("groups", "space"), None)
    return jax.shard_map(local, mesh=mesh, in_specs=in_specs, out_specs=out_specs, check_vma=False)
```

```python
import functools

import jax
import jax.numpy as jnp
from jax import lax
from jax.experimental import pallas as pl
from jax.experimental.pallas import tpu as pltpu
from jax.sharding import PartitionSpec as P


BROWS = 4
BCOLS = 128
ITERS = 4
LANES = 128
SUBLANES = 8


smooth_sq = 0.01
f32 = jnp.float32
bf16 = jnp.bfloat16


def split(x):
    high = x.astype(bf16)
    return high, (x - high.astype(f32)).astype(bf16)


def mm(a, b):
    return jnp.dot(a, b, preferred_element_type=f32)


def total(terms):
    terms = list(terms)
    while len(terms) > 1:
        terms = [a + b for a, b in zip(terms[::2], terms[1::2])] + terms[len(terms) & ~1 :]
    return terms[0]


def round_up(value, unit):
    return -(-value // unit) * unit


def vmem(count):
    return [pl.BlockSpec(memory_space=pltpu.VMEM)] * count


def hbm(count):
    return [pl.BlockSpec(memory_space=pltpu.HBM)] * count


def fetch(pairs, sem):
    copies = [pltpu.make_async_copy(src, dst, sem.at[k]) for k, (src, dst) in enumerate(pairs)]
    for copy in copies:
        copy.start()
    return copies


def params(mib):
    return pltpu.CompilerParams(vmem_limit_bytes=mib << 20)


def upright(line):
    size = line.shape[1]
    eye = lax.broadcasted_iota(jnp.int32, (size, size), 0) == lax.broadcasted_iota(
        jnp.int32, (size, size), 1
    )
    spread = jnp.broadcast_to(line, (size, size))
    return jnp.sum(jnp.where(eye, spread, 0.0), axis=1, keepdims=True)


def pack_kernel(
    target_hbm, start_hbm, rows_hbm, images_ref, *refs, spaces, chunks, part, halves, table_lines
):
    params_refs = (target_hbm, start_hbm, rows_hbm)
    outs, (target_ref, start_ref, rows_ref, small_sem, sem) = refs[:-5], refs[-5:]
    tables = fetch(zip(params_refs, (target_ref, start_ref, rows_ref)), small_sem)
    width = images_ref.shape[1]
    size = images_ref.shape[0] // spaces // chunks
    strip = size // part
    own = lax.axis_index("space")
    copies = []
    for q in range(chunks):
        for d in range(spaces):
            to = lax.rem(own + d, spaces)
            out = outs[q * spaces + d]
            copy = pltpu.make_async_copy(
                images_ref.at[pl.ds(pl.multiple_of((to * chunks + q) * size, size), size)],
                out.at[pl.ds(0, size)],
                sem.at[q * spaces + d],
            )
            copy.start()
            copies.append(copy)
    for table in tables:
        table.wait()
    blocks = target_ref.shape[1]
    rows = spaces * strip
    matrix = rows_ref[0]
    lane = lax.broadcasted_iota(jnp.int32, (BROWS, width), 1) & (BROWS - 1)
    spread = jnp.zeros((BROWS, width), f32)
    for k in range(BROWS):
        spread = jnp.where(lane == k, jnp.broadcast_to(matrix[:, k : k + 1], spread.shape), spread)
    target = upright(target_ref[...].astype(f32))
    start = target * f32(blocks * BROWS) + upright(start_ref[...].astype(f32))
    length = halves * rows
    place = lax.broadcasted_iota(jnp.int32, (blocks, length), 1)
    block = lax.broadcasted_iota(jnp.int32, (blocks, length), 0)
    first = own * strip
    shift = halves.bit_length() - 1
    low = (block & (halves - 1)) * rows + (block >> shift) * BROWS + first
    inside = (place >= low) & (place < low + BROWS)
    lines = [
        jnp.sum(jnp.where(inside, table, 0.0), axis=0, keepdims=True) for table in (start, target)
    ]
    for d in range(spaces):
        out = outs[d]
        out[size:, :] = jnp.zeros((out.shape[0] - size, width), f32)
        out[size : size + BROWS, :] = spread
        for t, line in enumerate(lines):
            for k in range(table_lines):
                at = size + BROWS + t * table_lines + k
                used = min(width, length - k * width)
                out[at : at + 1, 0:used] = line[:, k * width : k * width + used]
    for copy in copies:
        copy.wait()


def taps_kernel(kernels_hbm, strength_hbm, line_ref, gain_ref, kernels_ref, strength_ref, sem):
    for copy in fetch(((kernels_hbm, kernels_ref), (strength_hbm, strength_ref)), sem):
        copy.wait()
    passes, bands, taps_count = kernels_ref.shape
    wide = line_ref.shape[2]
    pad = jnp.zeros((bands, LANES - taps_count), f32)
    mirror = lax.broadcasted_iota(jnp.int32, (LANES, LANES), 0) + lax.broadcasted_iota(
        jnp.int32, (LANES, LANES), 1
    )
    mirror = jnp.where(mirror == taps_count - 1, 1.0, 0.0).astype(f32)
    rest = jnp.zeros((bands, wide - LANES), f32)
    for p in range(passes):
        taps = kernels_ref[p]
        taps = taps / jnp.sum(taps, axis=1, keepdims=True)
        taps = jnp.concatenate([taps, pad], axis=1)
        strength = upright(strength_ref[p : p + 1, :])
        turned = jnp.dot(taps, mirror, precision=lax.Precision.HIGHEST)
        at = slice(p * bands, (p + 1) * bands)
        line_ref[0, at, :] = jnp.concatenate([taps * strength, rest], axis=1)
        line_ref[1, at, :] = jnp.concatenate([turned, rest], axis=1)
        gain_ref[at, :] = jnp.broadcast_to(1.0 + strength, (bands, gain_ref.shape[1]))


def banded(line, size, radius):
    wide = line.shape[1]
    spread = jnp.broadcast_to(line, (size, wide))
    return split(pltpu.roll(spread, wide - radius, 1, stride=1, stride_axis=0)[:, :size])


def correct_kernel(
    line_ref, gain_ref, *refs, spaces, part, first, passes, bands, radius, share, table_lines
):
    x_refs, refs = refs[:spaces], refs[spaces:]
    if first == 0:
        count_hbm, out_ref, ah_ref, al_ref, state, count_ref, sem = refs
        counted = fetch(((count_hbm, count_ref),), sem)
    else:
        ah_ref, al_ref, out_ref, state = refs
    rows, width = state.shape[1:]
    strip = rows // spaces
    tables = part * strip
    halves = width // BCOLS
    length = halves * rows
    own = lax.axis_index("space")
    for d in range(spaces):
        src = lax.rem(own + (spaces - d), spaces)
        at = pl.ds(pl.multiple_of(src * strip, strip), strip)
        for i in range(part):
            state[i, at, :] = x_refs[d][i * strip : (i + 1) * strip, :]
    if first == 0:
        def table(t):
            lines = []
            for k in range(table_lines):
                at = tables + BROWS + t * table_lines + k
                used = min(width, length - k * width)
                lines.append(total(x[at : at + 1, 0:used] for x in x_refs))
            return jnp.concatenate(lines, axis=1)

        start, target = table(0), table(1)
        entries = jnp.zeros((BROWS, length), f32)
        for d in range(spaces):
            src = lax.rem(own + (spaces - d), spaces).astype(f32)
            matrix = x_refs[d][tables : tables + BROWS, :]
            matrix = jnp.concatenate([matrix] * (length // width), axis=1)
            entries = jnp.where(target == src, matrix, entries)
        map_rows = ah_ref.shape[0]
        line = lax.broadcasted_iota(jnp.int32, (map_rows, length), 0)
        offset = line - start.astype(jnp.int32)
        placer = jnp.zeros((map_rows, length), f32)
        for i in range(BROWS):
            placer = jnp.where(offset == i, entries[i : i + 1, :], placer)
        ah, al = split(placer)
        ah_ref[...] = ah
        al_ref[...] = al
    slots = [(first + i) % bands for i in range(part)]
    for step in range(passes):
        middle = []
        for i, slot in enumerate(slots):
            k = step * bands + slot
            xh, xl = split(state[i])
            rh, rl = banded(line_ref[0, k : k + 1, :], rows, radius)
            both = mm(jnp.concatenate([rh, rh], axis=1), jnp.concatenate([xh, xl], axis=0))
            middle.append(split(both + mm(rl, xh)))
        for i, slot in enumerate(slots):
            k = step * bands + slot
            yh, yl = middle[i]
            ch, cl = banded(line_ref[1, k : k + 1, :], width, radius)
            both = mm(jnp.concatenate([yh, yl], axis=0), ch)
            blurred = both[:rows] + both[rows:] + mm(yh, cl)
            state[i] = gain_ref[k : k + 1, :] * state[i] - blurred
    ah, al = ah_ref[...], al_ref[...]
    map_rows = ah.shape[0]
    stacked = jnp.concatenate([ah, al], axis=0)
    for i in range(0, part, 2):
        pair = range(i, min(i + 2, part))
        z = jnp.concatenate(
            [
                jnp.concatenate(
                    [state[j, :, h * BCOLS : (h + 1) * BCOLS] for h in range(halves)], axis=0
                )
                for j in pair
            ],
            axis=1,
        )
        zh, zl = split(z)
        both = mm(stacked, zh)
        laid = both[:map_rows] + both[map_rows:] + mm(ah, zl)
        for p, j in enumerate(pair):
            for d in range(out_ref.shape[0]):
                out_ref[d, j * share : (j + 1) * share, :] = laid[
                    d * share : (d + 1) * share, p * BCOLS : (p + 1) * BCOLS
                ]
    if first == 0:
        counted[0].wait()
        dates = count_ref.shape[1]
        counted = count_ref[...].astype(f32)
        for d in range(out_ref.shape[0]):
            out_ref[d, part * share :, :] = jnp.zeros((SUBLANES, BCOLS), f32)
            out_ref[d, part * share : part * share + 1, 0:dates] = counted


def columns_of(block, kh, kl):
    bh, bl = split(block)
    both = mm(jnp.concatenate([bh, bl], axis=0), kh)
    size = block.shape[0]
    return both[:size] + both[size:] + mm(bh, kl)


def columns_kernel(
    y_ref, cols_hbm, full_ref, weight_ref, kh_ref, kl_ref, cols_ref, sem, *, spaces, dates, cores, local_dates
):
    fetch(((cols_hbm, cols_ref),), sem)[0].wait()
    sources, part, share, width = full_ref.shape
    kh, kl = split(cols_ref[0])
    kh_ref[...] = kh
    kl_ref[...] = kl
    for s in range(sources):
        full = columns_of(y_ref[s, : part * share, :], kh, kl)
        full_ref[s] = full.reshape(part, share, width)
    at = slice(part * share, part * share + 1)
    summed = total(y_ref[s, at, :] for s in range(0, sources, cores))
    mean_count = jnp.sum(summed, axis=1, keepdims=True) / f32(spaces * dates * local_dates)
    own = lax.axis_index("space")
    for x in range(dates):
        counted = y_ref[(own * dates + x) * cores, at, :]
        weight = counted / (counted + mean_count)
        for t in range(local_dates):
            weight_ref[x * local_dates + t] = jnp.broadcast_to(
                weight[:, t : t + 1], weight_ref.shape[1:]
            )


def median_kernel(
    weight_ref, kh_ref, kl_ref, first_ref, *refs, spaces, dates, cores, bands, local_dates
):
    sources, part, share, width = first_ref.shape
    chunks = local_dates * bands // spaces // part
    y_refs, refs = refs[: chunks - 1], refs[chunks - 1 :]
    out_refs, refs = refs[:cores], refs[cores:]
    full_refs = [first_ref] + list(refs[: chunks - 1])
    result = refs[-1]
    kh, kl = kh_ref[...], kl_ref[...]
    for y_ref, full_ref in zip(y_refs, full_refs[1:]):
        for s in range(sources):
            full_ref[s] = columns_of(y_ref[s], kh, kl).reshape(part, share, width)
    total_bands = cores * bands
    where = [[None] * total_bands for _ in range(dates * local_dates)]
    for z in range(spaces):
        for x in range(dates):
            for c in range(cores):
                for i in range(part * chunks):
                    t, b = divmod(z * part * chunks + i, bands)
                    where[x * local_dates + t][c * bands + b] = (
                        i // part,
                        (z * dates + x) * cores + c,
                        i % part,
                    )
    tile = weight_ref.shape[1]
    for start in range(0, share, tile):
        rows = pl.ds(start, tile)

        def load(t):
            return [full_refs[q][s, i, rows, :] for q, s, i in where[t]]

        number = [jnp.zeros((tile, width), f32)] * total_bands
        below = jnp.zeros((tile, width), f32)
        for t, _ in enumerate(where):
            w = weight_ref[t]
            below = below + w
            number = [n + w * v for n, v in zip(number, load(t))]
        estimate = [n / below for n in number]
        for _ in range(ITERS):
            number = [jnp.zeros((tile, width), f32)] * total_bands
            below = jnp.zeros((tile, width), f32)
            for t, _ in enumerate(where):
                values = load(t)
                squares = []
                for v, e in zip(values, estimate):
                    d = v - e
                    squares.append(d * d)
                scaled = weight_ref[t] / jnp.sqrt(total(squares) + smooth_sq)
                below = below + scaled
                number = [n + scaled * v for n, v in zip(number, values)]
            estimate = [n / below for n in number]
        for b in range(total_bands):
            result[b // bands, b % bands, rows, :] = estimate[b]
    own = lax.axis_index("band")
    for k in range(cores):
        out_refs[k][...] = result[lax.rem(own + k, cores)]


def place_kernel(*refs, dates, cores):
    out_ref = refs[-1]
    share = refs[0].shape[1]
    x, c = lax.axis_index("date"), lax.axis_index("band")
    for dx in range(dates):
        for dc in range(cores):
            j = lax.rem(x + (dates - dx), dates) * cores + lax.rem(c + (cores - dc), cores)
            at = pl.ds(pl.multiple_of(j * share, share), share)
            out_ref[:, at, :] = refs[dx * cores + dc][...]


def local(
    reflect, kernels, strength, destinations, offsets, counts, resample_rows, resample_columns
):
    spaces, dates, cores = (lax.axis_size(a) for a in ("space", "date", "band"))
    local_dates, bands, strip, width = reflect.shape
    passes = kernels.shape[0]
    blocks = offsets.shape[0]
    rows = spaces * strip
    halves = width // BCOLS
    length = halves * rows
    table_lines = -(-length // width)
    tile_rows = blocks * BROWS
    sources = spaces * dates * cores
    share = tile_rows // (dates * cores)
    tile = min(share, SUBLANES)
    per = local_dates * bands // spaces
    chunks = 2 if per % 2 == 0 else 1
    part = per // chunks

    images = reflect.reshape(local_dates * bands * strip, width)
    extra_lines = round_up(BROWS + 2 * table_lines, SUBLANES)
    packed = pl.pallas_call(
        functools.partial(
            pack_kernel,
            spaces=spaces,
            chunks=chunks,
            part=part,
            halves=halves,
            table_lines=table_lines,
        ),
        out_shape=[
            jax.ShapeDtypeStruct((part * strip + (extra_lines if q == 0 else 0), width), f32)
            for q in range(chunks)
            for _ in range(spaces)
        ],
        in_specs=hbm(4),
        out_specs=vmem(chunks * spaces),
        scratch_shapes=[
            pltpu.VMEM((1, blocks), jnp.int32),
            pltpu.VMEM((1, blocks), jnp.int32),
            pltpu.VMEM((1, BROWS, BROWS), f32),
            pltpu.SemaphoreType.DMA((3,)),
            pltpu.SemaphoreType.DMA((chunks * spaces,)),
        ],
        compiler_params=params(8),
        name="pack",
    )(destinations.reshape(1, blocks), offsets.reshape(1, blocks), resample_rows, images)
    strips = []
    for q in range(chunks):
        mine = list(packed[q * spaces : (q + 1) * spaces])
        for d in range(1, spaces):
            pairs = [(i, (i + d) % spaces) for i in range(spaces)]
            mine[d] = lax.ppermute(mine[d], "space", pairs)
        strips.append(mine)

    here = bands if per % bands == 0 else per
    if here != bands:
        first_band = (lax.axis_index("space") * per) % bands
        kernels = lax.dynamic_slice_in_dim(kernels, first_band, here, axis=1)
        strength = lax.dynamic_slice_in_dim(strength, first_band, here, axis=1)
    wide = max(rows, width) + LANES
    count = passes * here
    lines, gains = pl.pallas_call(
        taps_kernel,
        out_shape=[
            jax.ShapeDtypeStruct((2, count, wide), f32),
            jax.ShapeDtypeStruct((count, width), f32),
        ],
        in_specs=hbm(2),
        out_specs=vmem(2),
        scratch_shapes=[
            pltpu.VMEM(kernels.shape, f32),
            pltpu.VMEM(strength.shape, f32),
            pltpu.SemaphoreType.DMA((2,)),
        ],
        compiler_params=params(4),
        name="taps",
    )(kernels, strength)

    pixels = []
    placer = None
    for q in range(chunks):
        out_shape = [
            jax.ShapeDtypeStruct((sources, part * share + (SUBLANES if q == 0 else 0), BCOLS), f32)
        ]
        if q == 0:
            out_shape += [jax.ShapeDtypeStruct((spaces * tile_rows, length), bf16)] * 2
            extra = [counts.reshape(1, local_dates)]
            extra_specs = hbm(1)
            extra_scratch = [
                pltpu.VMEM((1, local_dates), jnp.int32),
                pltpu.SemaphoreType.DMA((1,)),
            ]
        else:
            extra, extra_specs, extra_scratch = placer, vmem(2), []
        correct = pl.pallas_call(
            functools.partial(
                correct_kernel,
                spaces=spaces,
                part=part,
                first=q * part,
                passes=passes,
                bands=here,
                radius=kernels.shape[2] // 2,
                share=share,
                table_lines=table_lines,
            ),
            out_shape=out_shape,
            in_specs=vmem(2 + spaces) + extra_specs,
            out_specs=vmem(len(out_shape)),
            scratch_shapes=[pltpu.VMEM((part, rows, width), f32)] + extra_scratch,
            compiler_params=params(20),
        )
        results = correct(lines, gains, *strips[q], *extra)
        if q == 0:
            placer = results[1:]
        pixels.append(
            lax.all_to_all(
                results[0], ("space", "date", "band"), split_axis=0, concat_axis=0, tiled=True
            )
        )

    full, weights, *columns = pl.pallas_call(
        functools.partial(
            columns_kernel, spaces=spaces, dates=dates, cores=cores, local_dates=local_dates
        ),
        out_shape=[
            jax.ShapeDtypeStruct((sources, part, share, BCOLS), f32),
            jax.ShapeDtypeStruct((dates * local_dates, tile, BCOLS), f32),
        ]
        + [jax.ShapeDtypeStruct((BCOLS, BCOLS), bf16)] * 2,
        in_specs=vmem(1) + hbm(1),
        out_specs=vmem(4),
        scratch_shapes=[pltpu.VMEM((1, BCOLS, BCOLS), f32), pltpu.SemaphoreType.DMA((1,))],
        compiler_params=params(8),
        name="columns",
    )(pixels[0], resample_columns)
    shares = pl.pallas_call(
        functools.partial(
            median_kernel,
            spaces=spaces,
            dates=dates,
            cores=cores,
            bands=bands,
            local_dates=local_dates,
        ),
        out_shape=[jax.ShapeDtypeStruct((bands, share, BCOLS), f32)] * cores,
        in_specs=vmem(3 + chunks),
        out_specs=vmem(cores),
        scratch_shapes=[pltpu.VMEM((sources, part, share, BCOLS), f32)] * (chunks - 1)
        + [pltpu.VMEM((cores, bands, share, BCOLS), f32)],
        compiler_params=params(12),
        name="median",
    )(weights, *columns, full, *pixels[1:])

    pieces = []
    for dx in range(dates):
        for dc in range(cores):
            piece = shares[dc]
            if dx or dc:
                pairs = [
                    (x * cores + c, (x + dx) % dates * cores + (c + dc) % cores)
                    for x in range(dates)
                    for c in range(cores)
                ]
                piece = lax.ppermute(piece, ("date", "band"), pairs)
            pieces.append(piece)
    return pl.pallas_call(
        functools.partial(place_kernel, dates=dates, cores=cores),
        out_shape=jax.ShapeDtypeStruct((bands, tile_rows, BCOLS), f32),
        in_specs=vmem(dates * cores),
        out_specs=pl.BlockSpec(memory_space=pltpu.VMEM),
        compiler_params=params(4),
        name="place",
    )(*pieces)


def solution(mesh):
    in_specs = (
        P("date", "band", ("groups", "space"), None),
        P(None, "band", None),
        P(None, "band"),
        P(("groups", "space"), None),
        P(("groups", "space")),
        P("date", ("groups", "space")),
        P(("groups", "space"), None, None),
        P(("groups", "space"), None, None),
    )
    out_specs = P("band", ("groups", "space"), None)

    return jax.shard_map(local, mesh=mesh, in_specs=in_specs, out_specs=out_specs, check_vma=False)
```

```python
import functools

import jax
import jax.numpy as jnp
from jax import lax
from jax.experimental import pallas as pl
from jax.experimental.pallas import tpu as pltpu
from jax.sharding import PartitionSpec as P


BROWS = 4
BCOLS = 128
ITERS = 4
LANES = 128
SUBLANES = 8


smooth_sq = 0.01
f32 = jnp.float32
bf16 = jnp.bfloat16


def split(x):
    high = x.astype(bf16)
    return high, (x - high.astype(f32)).astype(bf16)


def mm(a, b):
    return jnp.dot(a, b, preferred_element_type=f32)


def total(terms):
    terms = list(terms)
    while len(terms) > 1:
        terms = [a + b for a, b in zip(terms[::2], terms[1::2])] + terms[len(terms) & ~1 :]
    return terms[0]


def round_up(value, unit):
    return -(-value // unit) * unit


def vmem(count):
    return [pl.BlockSpec(memory_space=pltpu.VMEM)] * count


def hbm(count):
    return [pl.BlockSpec(memory_space=pltpu.HBM)] * count


def send_order(spaces):
    middle = spaces // 2
    return list(range(middle, spaces)) + list(range(1, middle))


def fetch(pairs, sem):
    copies = [pltpu.make_async_copy(src, dst, sem.at[k]) for k, (src, dst) in enumerate(pairs)]
    for copy in copies:
        copy.start()
    return copies


def params(mib):
    return pltpu.CompilerParams(vmem_limit_bytes=mib << 20)


def upright(line):
    size = line.shape[1]
    eye = lax.broadcasted_iota(jnp.int32, (size, size), 0) == lax.broadcasted_iota(
        jnp.int32, (size, size), 1
    )
    spread = jnp.broadcast_to(line, (size, size))
    return jnp.sum(jnp.where(eye, spread, 0.0), axis=1, keepdims=True)


def pack_kernel(
    target_hbm, start_hbm, rows_hbm, images_ref, *refs, spaces, parts, strip, halves, table_lines
):
    params_refs = (target_hbm, start_hbm, rows_hbm)
    outs, (target_ref, start_ref, rows_ref, small_sem, sem) = refs[:-5], refs[-5:]
    tables = fetch(zip(params_refs, (target_ref, start_ref, rows_ref)), small_sem)
    width = images_ref.shape[1]
    step = images_ref.shape[0] // spaces
    own = lax.axis_index("space")
    copies = []
    for q, part in enumerate(parts):
        size, ahead = part * strip, sum(parts[:q]) * strip
        for d in range(spaces):
            to = own ^ d
            out = outs[q * spaces + d]
            copy = pltpu.make_async_copy(
                images_ref.at[pl.ds(pl.multiple_of(to * step + ahead, strip), size)],
                out.at[pl.ds(0, size)],
                sem.at[q * spaces + d],
            )
            copy.start()
            copies.append(copy)
    for table in tables:
        table.wait()
    blocks = target_ref.shape[1]
    rows = spaces * strip
    matrix = rows_ref[0]
    lane = lax.broadcasted_iota(jnp.int32, (BROWS, width), 1) & (BROWS - 1)
    spread = jnp.zeros((BROWS, width), f32)
    for k in range(BROWS):
        spread = jnp.where(lane == k, jnp.broadcast_to(matrix[:, k : k + 1], spread.shape), spread)
    target = upright(target_ref[...].astype(f32))
    start = target * f32(blocks * BROWS) + upright(start_ref[...].astype(f32))
    length = halves * rows
    place = lax.broadcasted_iota(jnp.int32, (blocks, length), 1)
    block = lax.broadcasted_iota(jnp.int32, (blocks, length), 0)
    first = own * strip
    shift = halves.bit_length() - 1
    low = (block & (halves - 1)) * rows + (block >> shift) * BROWS + first
    inside = (place >= low) & (place < low + BROWS)
    lines = [
        jnp.sum(jnp.where(inside, table, 0.0), axis=0, keepdims=True) for table in (start, target)
    ]
    size = parts[0] * strip
    for d in range(spaces):
        out = outs[d]
        out[size:, :] = jnp.zeros((out.shape[0] - size, width), f32)
        out[size : size + BROWS, :] = spread
        for t, line in enumerate(lines):
            for k in range(table_lines):
                at = size + BROWS + t * table_lines + k
                used = min(width, length - k * width)
                out[at : at + 1, 0:used] = line[:, k * width : k * width + used]
    for copy in copies:
        copy.wait()


def taps_kernel(kernels_hbm, strength_hbm, line_ref, gain_ref, kernels_ref, strength_ref, sem):
    for copy in fetch(((kernels_hbm, kernels_ref), (strength_hbm, strength_ref)), sem):
        copy.wait()
    passes, bands, taps_count = kernels_ref.shape
    wide = line_ref.shape[2]
    pad = jnp.zeros((bands, LANES - taps_count), f32)
    mirror = lax.broadcasted_iota(jnp.int32, (LANES, LANES), 0) + lax.broadcasted_iota(
        jnp.int32, (LANES, LANES), 1
    )
    mirror = jnp.where(mirror == taps_count - 1, 1.0, 0.0).astype(f32)
    rest = jnp.zeros((bands, wide - LANES), f32)
    for p in range(passes):
        taps = kernels_ref[p]
        taps = taps / jnp.sum(taps, axis=1, keepdims=True)
        taps = jnp.concatenate([taps, pad], axis=1)
        strength = upright(strength_ref[p : p + 1, :])
        turned = jnp.dot(taps, mirror, precision=lax.Precision.HIGHEST)
        at = slice(p * bands, (p + 1) * bands)
        line_ref[0, at, :] = jnp.concatenate([taps * strength, rest], axis=1)
        line_ref[1, at, :] = jnp.concatenate([turned, rest], axis=1)
        gain_ref[at, :] = jnp.broadcast_to(1.0 + strength, (bands, gain_ref.shape[1]))


def banded(line, size, radius):
    wide = line.shape[1]
    spread = jnp.broadcast_to(line, (size, wide))
    return split(pltpu.roll(spread, wide - radius, 1, stride=1, stride_axis=0)[:, :size])


def correct_kernel(
    line_ref, gain_ref, *refs, spaces, cores, part, first, passes, bands, radius, share, table_lines
):
    x_refs, refs = refs[:spaces], refs[spaces:]
    if first == 0:
        count_hbm, out_ref, ah_ref, al_ref, state, count_ref, sem = refs
        counted = fetch(((count_hbm, count_ref),), sem)
    else:
        ah_ref, al_ref, *out_refs, state, laid_ref = refs
    rows, width = state.shape[1:]
    strip = rows // spaces
    tables = part * strip
    halves = width // BCOLS
    length = halves * rows
    own = lax.axis_index("space")
    for d in range(spaces):
        src = own ^ d
        at = pl.ds(pl.multiple_of(src * strip, strip), strip)
        for i in range(part):
            state[i, at, :] = x_refs[d][i * strip : (i + 1) * strip, :]
    if first == 0:
        def table(t):
            lines = []
            for k in range(table_lines):
                at = tables + BROWS + t * table_lines + k
                used = min(width, length - k * width)
                lines.append(total(x[at : at + 1, 0:used] for x in x_refs))
            return jnp.concatenate(lines, axis=1)

        start, target = table(0), table(1)
        entries = jnp.zeros((BROWS, length), f32)
        for d in range(spaces):
            src = (own ^ d).astype(f32)
            matrix = x_refs[d][tables : tables + BROWS, :]
            matrix = jnp.concatenate([matrix] * (length // width), axis=1)
            entries = jnp.where(target == src, matrix, entries)
        map_rows = ah_ref.shape[0]
        line = lax.broadcasted_iota(jnp.int32, (map_rows, length), 0)
        offset = line - start.astype(jnp.int32)
        placer = jnp.zeros((map_rows, length), f32)
        for i in range(BROWS):
            placer = jnp.where(offset == i, entries[i : i + 1, :], placer)
        ah, al = split(placer)
        ah_ref[...] = ah
        al_ref[...] = al
    slots = [(first + i) % bands for i in range(part)]
    for step in range(passes):
        middle = []
        for i, slot in enumerate(slots):
            k = step * bands + slot
            xh, xl = split(state[i])
            rh, rl = banded(line_ref[0, k : k + 1, :], rows, radius)
            both = mm(jnp.concatenate([rh, rh], axis=1), jnp.concatenate([xh, xl], axis=0))
            middle.append(split(both + mm(rl, xh)))
        for i, slot in enumerate(slots):
            k = step * bands + slot
            yh, yl = middle[i]
            ch, cl = banded(line_ref[1, k : k + 1, :], width, radius)
            both = mm(jnp.concatenate([yh, yl], axis=0), ch)
            blurred = both[:rows] + both[rows:] + mm(yh, cl)
            state[i] = gain_ref[k : k + 1, :] * state[i] - blurred
    ah, al = ah_ref[...], al_ref[...]
    map_rows = ah.shape[0]
    stacked = jnp.concatenate([ah, al], axis=0)
    for i in range(0, part, 2):
        pair = range(i, min(i + 2, part))
        z = jnp.concatenate(
            [
                jnp.concatenate(
                    [state[j, :, h * BCOLS : (h + 1) * BCOLS] for h in range(halves)], axis=0
                )
                for j in pair
            ],
            axis=1,
        )
        zh, zl = split(z)
        both = mm(stacked, zh)
        laid = both[:map_rows] + both[map_rows:] + mm(ah, zl)
        if first == 0:
            for p, j in enumerate(pair):
                for d in range(out_ref.shape[0]):
                    out_ref[d, j * share : (j + 1) * share, :] = laid[
                        d * share : (d + 1) * share, p * BCOLS : (p + 1) * BCOLS
                    ]
            continue
        groups = laid_ref.shape[0]
        for m in range(groups):
            laid_ref[m, :, : laid.shape[1]] = laid[m * share : (m + 1) * share]
        x, c = lax.axis_index("date"), lax.axis_index("band")
        for k, out in enumerate(out_refs):
            mine = (x ^ (k // cores)) * cores + (c ^ (k % cores))
            for g in range(spaces):
                rows_of = laid_ref[g * (groups // spaces) + mine]
                for p, j in enumerate(pair):
                    out[g, j * share : (j + 1) * share, :] = rows_of[
                        :, p * BCOLS : (p + 1) * BCOLS
                    ]
    if first == 0:
        counted[0].wait()
        dates = count_ref.shape[1]
        counted = count_ref[...].astype(f32)
        for d in range(out_ref.shape[0]):
            out_ref[d, part * share :, :] = jnp.zeros((SUBLANES, BCOLS), f32)
            out_ref[d, part * share : part * share + 1, 0:dates] = counted


def columns_of(block, kh, kl):
    bh, bl = split(block)
    both = mm(jnp.concatenate([bh, bl], axis=0), kh)
    size = block.shape[0]
    return both[:size] + both[size:] + mm(bh, kl)


def halve_kernel(cols_ref, kh_ref, kl_ref):
    kh_ref[...], kl_ref[...] = split(cols_ref[0])


def columns_kernel(
    y_ref, kh_ref, kl_ref, full_ref, weight_ref, *, spaces, dates, cores, local_dates
):
    sources, part, share, width = full_ref.shape
    kh, kl = kh_ref[...], kl_ref[...]
    for s in range(sources):
        full = columns_of(y_ref[s, : part * share, :], kh, kl)
        full_ref[s] = full.reshape(part, share, width)
    at = slice(part * share, part * share + 1)
    summed = total(y_ref[s, at, :] for s in range(0, sources, cores))
    mean_count = jnp.sum(summed, axis=1, keepdims=True) / f32(spaces * dates * local_dates)
    own = lax.axis_index("space")
    for x in range(dates):
        counted = y_ref[(own * dates + x) * cores, at, :]
        weight = counted / (counted + mean_count)
        for t in range(local_dates):
            weight_ref[x * local_dates + t] = jnp.broadcast_to(
                weight[:, t : t + 1], weight_ref.shape[1:]
            )


def regroup_kernel(*refs, spaces):
    groups = len(refs) - spaces
    own = lax.axis_index("space")
    for d in range(spaces):
        for k in range(groups):
            refs[groups + d][k] = refs[k][own ^ d]


def median_kernel(
    weight_ref, kh_ref, kl_ref, first_ref, *refs, spaces, dates, cores, bands, per, local_dates
):
    share, width = first_ref.shape[2:]
    part = first_ref.shape[1]
    rest = per - part
    y_refs, refs = refs[:spaces], refs[spaces:]
    out_refs, (full_ref, result) = refs[:cores], refs[cores:]
    kh, kl = kh_ref[...], kl_ref[...]
    for d in range(spaces):
        block = y_refs[d][...].reshape(dates * cores * rest * share, width)
        full_ref[d] = columns_of(block, kh, kl).reshape(dates * cores, rest, share, width)
    z, x, c = (lax.axis_index(a) for a in ("space", "date", "band"))
    across = max(1, bands // per)
    inside = max(1, per // bands)
    span = bands // across
    tile = weight_ref.shape[1]
    slots = [(dc, b) for dc in range(cores) for b in range(bands)]
    order = [
        (d, dx, t) for d in range(0, spaces, across) for dx in range(dates) for t in range(inside)
    ]
    for start in range(0, share, tile):
        rows = pl.ds(start, tile)

        def load(d, dx, t):
            values = []
            for dc, b in slots:
                far = d ^ (b // span)
                image = t * bands + b % span
                if image < part:
                    source = ((z ^ far) * dates + (x ^ dx)) * cores + (c ^ dc)
                    values.append(first_ref[source, image, rows, :])
                else:
                    values.append(full_ref[far, dx * cores + dc, image - part, rows, :])
            return values

        def weight(d, dx, t):
            return weight_ref[(x ^ dx) * local_dates + (z ^ d) // across * inside + t]

        number = [jnp.zeros((tile, width), f32)] * len(slots)
        below = jnp.zeros((tile, width), f32)
        for key in order:
            w = weight(*key)
            below = below + w
            number = [n + w * v for n, v in zip(number, load(*key))]
        estimate = [n / below for n in number]
        for _ in range(ITERS):
            number = [jnp.zeros((tile, width), f32)] * len(slots)
            below = jnp.zeros((tile, width), f32)
            for key in order:
                values = load(*key)
                squares = []
                for v, e in zip(values, estimate):
                    gap = v - e
                    squares.append(gap * gap)
                scaled = weight(*key) / jnp.sqrt(total(squares) + smooth_sq)
                below = below + scaled
                number = [n + scaled * v for n, v in zip(number, values)]
            estimate = [n / below for n in number]
        for (dc, b), value in zip(slots, estimate):
            if across == 1:
                out_refs[dc][b, rows, :] = value
            else:
                result[dc, ((z % across) ^ (b // span)) * span + b % span, rows, :] = value
    if across > 1:
        for dc in range(cores):
            out_refs[dc][...] = result[dc]


def place_kernel(*refs, dates, cores):
    out_ref = refs[-1]
    share = refs[0].shape[1]
    x, c = lax.axis_index("date"), lax.axis_index("band")
    for dx in range(dates):
        for dc in range(cores):
            j = (x ^ dx) * cores + (c ^ dc)
            at = pl.ds(pl.multiple_of(j * share, share), share)
            out_ref[:, at, :] = refs[dx * cores + dc][...]


def across_sides(pieces, dates, cores):
    received = [pieces[0]]
    for k in range(1, dates * cores):
        pairs = [
            (x * cores + c, (x ^ (k // cores)) * cores + (c ^ (k % cores)))
            for x in range(dates)
            for c in range(cores)
        ]
        received.append(lax.ppermute(pieces[k], ("date", "band"), pairs))
    return received


def local(
    reflect, kernels, strength, destinations, offsets, counts, resample_rows, resample_columns
):
    spaces, dates, cores = (lax.axis_size(a) for a in ("space", "date", "band"))
    local_dates, bands, strip, width = reflect.shape
    passes = kernels.shape[0]
    blocks = offsets.shape[0]
    rows = spaces * strip
    halves = width // BCOLS
    length = halves * rows
    table_lines = -(-length // width)
    tile_rows = blocks * BROWS
    sources = spaces * dates * cores
    share = tile_rows // (dates * cores)
    tile = min(share, SUBLANES)
    per = local_dates * bands // spaces
    late = max(1, per // 4)
    parts = (per - late, late)

    images = reflect.reshape(local_dates * bands * strip, width)
    extra_lines = round_up(BROWS + 2 * table_lines, SUBLANES)
    packed = pl.pallas_call(
        functools.partial(
            pack_kernel,
            spaces=spaces,
            parts=parts,
            strip=strip,
            halves=halves,
            table_lines=table_lines,
        ),
        out_shape=[
            jax.ShapeDtypeStruct((part * strip + (extra_lines if q == 0 else 0), width), f32)
            for q, part in enumerate(parts)
            for _ in range(spaces)
        ],
        in_specs=hbm(4),
        out_specs=vmem(len(parts) * spaces),
        scratch_shapes=[
            pltpu.VMEM((1, blocks), jnp.int32),
            pltpu.VMEM((1, blocks), jnp.int32),
            pltpu.VMEM((1, BROWS, BROWS), f32),
            pltpu.SemaphoreType.DMA((3,)),
            pltpu.SemaphoreType.DMA((len(parts) * spaces,)),
        ],
        compiler_params=params(8),
        name="pack",
    )(destinations.reshape(1, blocks), offsets.reshape(1, blocks), resample_rows, images)
    strips = []
    for q in range(len(parts)):
        mine = list(packed[q * spaces : (q + 1) * spaces])
        for d in send_order(spaces):
            pairs = [(i, i ^ d) for i in range(spaces)]
            mine[d] = lax.ppermute(mine[d], "space", pairs)
        strips.append(mine)

    here = bands if per % bands == 0 else per
    if here != bands:
        first_band = (lax.axis_index("space") * per) % bands
        kernels = lax.dynamic_slice_in_dim(kernels, first_band, here, axis=1)
        strength = lax.dynamic_slice_in_dim(strength, first_band, here, axis=1)
    wide = max(rows, width) + LANES
    count = passes * here
    lines, gains = pl.pallas_call(
        taps_kernel,
        out_shape=[
            jax.ShapeDtypeStruct((2, count, wide), f32),
            jax.ShapeDtypeStruct((count, width), f32),
        ],
        in_specs=hbm(2),
        out_specs=vmem(2),
        scratch_shapes=[
            pltpu.VMEM(kernels.shape, f32),
            pltpu.VMEM(strength.shape, f32),
            pltpu.SemaphoreType.DMA((2,)),
        ],
        compiler_params=params(4),
        name="taps",
    )(kernels, strength)

    def correct(q, out_shape, extra, extra_specs, extra_scratch):
        return pl.pallas_call(
            functools.partial(
                correct_kernel,
                spaces=spaces,
                cores=cores,
                part=parts[q],
                first=sum(parts[:q]),
                passes=passes,
                bands=here,
                radius=kernels.shape[2] // 2,
                share=share,
                table_lines=table_lines,
            ),
            out_shape=out_shape,
            in_specs=vmem(2 + spaces) + extra_specs,
            out_specs=vmem(len(out_shape)),
            scratch_shapes=[pltpu.VMEM((parts[q], rows, width), f32)] + extra_scratch,
            compiler_params=params(20),
        )(lines, gains, *strips[q], *extra)

    laid, *placer = correct(
        0,
        [jax.ShapeDtypeStruct((sources, parts[0] * share + SUBLANES, BCOLS), f32)]
        + [jax.ShapeDtypeStruct((spaces * tile_rows, length), bf16)] * 2,
        [counts.reshape(1, local_dates)],
        hbm(1),
        [pltpu.VMEM((1, local_dates), jnp.int32), pltpu.SemaphoreType.DMA((1,))],
    )
    pixels = lax.all_to_all(
        laid, ("space", "date", "band"), split_axis=0, concat_axis=0, tiled=True
    )
    late_rows = parts[1] * share
    sides = correct(
        1,
        [jax.ShapeDtypeStruct((spaces, late_rows, BCOLS), f32)] * (dates * cores),
        placer,
        vmem(2),
        [pltpu.VMEM((spaces * tile_rows // share, share, 2 * BCOLS), f32)],
    )
    sides = across_sides(sides, dates, cores)
    regroup = pl.pallas_call(
        functools.partial(regroup_kernel, spaces=spaces),
        out_shape=[jax.ShapeDtypeStruct((dates * cores, late_rows, BCOLS), f32)] * spaces,
        in_specs=vmem(dates * cores),
        out_specs=vmem(spaces),
        compiler_params=params(4),
        name="regroup",
    )
    late_pixels = list(regroup(*sides))
    for d in send_order(spaces):
        pairs = [(i, i ^ d) for i in range(spaces)]
        late_pixels[d] = lax.ppermute(late_pixels[d], "space", pairs)

    halve = pl.pallas_call(
        halve_kernel,
        out_shape=[jax.ShapeDtypeStruct((BCOLS, BCOLS), bf16)] * 2,
        in_specs=vmem(1),
        out_specs=vmem(2),
        compiler_params=params(2),
        name="halve",
    )
    columns = halve(resample_columns)
    columns_call = pl.pallas_call(
        functools.partial(
            columns_kernel, spaces=spaces, dates=dates, cores=cores, local_dates=local_dates
        ),
        out_shape=[
            jax.ShapeDtypeStruct((sources, parts[0], share, BCOLS), f32),
            jax.ShapeDtypeStruct((dates * local_dates, tile, BCOLS), f32),
        ],
        in_specs=vmem(3),
        out_specs=vmem(2),
        compiler_params=params(8),
        name="columns",
    )
    full, weights = columns_call(pixels, *columns)
    shares = pl.pallas_call(
        functools.partial(
            median_kernel,
            spaces=spaces,
            dates=dates,
            cores=cores,
            bands=bands,
            per=per,
            local_dates=local_dates,
        ),
        out_shape=[jax.ShapeDtypeStruct((bands, share, BCOLS), f32)] * cores,
        in_specs=vmem(4 + spaces),
        out_specs=vmem(cores),
        scratch_shapes=[
            pltpu.VMEM((spaces, dates * cores, parts[1], share, BCOLS), f32),
            pltpu.VMEM((cores, bands, share, BCOLS), f32),
        ],
        compiler_params=params(12),
        name="median",
    )(weights, *columns, full, *late_pixels)

    pieces = across_sides([shares[k % cores] for k in range(dates * cores)], dates, cores)
    return pl.pallas_call(
        functools.partial(place_kernel, dates=dates, cores=cores),
        out_shape=jax.ShapeDtypeStruct((bands, tile_rows, BCOLS), f32),
        in_specs=vmem(dates * cores),
        out_specs=pl.BlockSpec(memory_space=pltpu.VMEM),
        compiler_params=params(4),
        name="place",
    )(*pieces)


def solution(mesh):
    in_specs = (
        P("date", "band", ("groups", "space"), None),
        P(None, "band", None),
        P(None, "band"),
        P(("groups", "space"), None),
        P(("groups", "space")),
        P("date", ("groups", "space")),
        P(("groups", "space"), None, None),
        P(("groups", "space"), None, None),
    )
    out_specs = P("band", ("groups", "space"), None)

    return jax.shard_map(local, mesh=mesh, in_specs=in_specs, out_specs=out_specs, check_vma=False)
```

```python
import functools

import jax
import jax.numpy as jnp
from jax import lax
from jax.experimental import pallas as pl
from jax.experimental.pallas import tpu as pltpu
from jax.sharding import PartitionSpec as P


BROWS = 4
BCOLS = 128
ITERS = 4
LANES = 128
SUBLANES = 8


smooth_sq = 0.01
f32 = jnp.float32
bf16 = jnp.bfloat16


def split(x):
    high = x.astype(bf16)
    return high, (x - high.astype(f32)).astype(bf16)


def mm(a, b):
    return jnp.dot(a, b, preferred_element_type=f32)


def total(terms):
    terms = list(terms)
    while len(terms) > 1:
        terms = [a + b for a, b in zip(terms[::2], terms[1::2])] + terms[len(terms) & ~1 :]
    return terms[0]


def round_up(value, unit):
    return -(-value // unit) * unit


def vmem(count):
    return [pl.BlockSpec(memory_space=pltpu.VMEM)] * count


def hbm(count):
    return [pl.BlockSpec(memory_space=pltpu.HBM)] * count


def fetch(pairs, sem):
    copies = [pltpu.make_async_copy(src, dst, sem.at[k]) for k, (src, dst) in enumerate(pairs)]
    for copy in copies:
        copy.start()
    return copies


def params(mib):
    return pltpu.CompilerParams(vmem_limit_bytes=mib << 20)


def upright(line):
    size = line.shape[1]
    eye = lax.broadcasted_iota(jnp.int32, (size, size), 0) == lax.broadcasted_iota(
        jnp.int32, (size, size), 1
    )
    spread = jnp.broadcast_to(line, (size, size))
    return jnp.sum(jnp.where(eye, spread, 0.0), axis=1, keepdims=True)


def tables_kernel(
    target_hbm,
    start_hbm,
    rows_hbm,
    count_hbm,
    out_ref,
    counted_ref,
    target_ref,
    start_ref,
    rows_ref,
    count_ref,
    sem,
    *,
    spaces,
    strip,
    halves,
    table_lines,
):
    tables = fetch(
        zip(
            (target_hbm, start_hbm, rows_hbm, count_hbm),
            (target_ref, start_ref, rows_ref, count_ref),
        ),
        sem,
    )
    width = out_ref.shape[1]
    own = lax.axis_index("space")
    for table in tables:
        table.wait()
    blocks = target_ref.shape[1]
    rows = spaces * strip
    matrix = rows_ref[0]
    lane = lax.broadcasted_iota(jnp.int32, (BROWS, width), 1) & (BROWS - 1)
    spread = jnp.zeros((BROWS, width), f32)
    for k in range(BROWS):
        spread = jnp.where(lane == k, jnp.broadcast_to(matrix[:, k : k + 1], spread.shape), spread)
    target = upright(target_ref[...].astype(f32))
    start = target * f32(blocks * BROWS) + upright(start_ref[...].astype(f32))
    length = halves * rows
    place = lax.broadcasted_iota(jnp.int32, (blocks, length), 1)
    block = lax.broadcasted_iota(jnp.int32, (blocks, length), 0)
    first = own * strip
    shift = halves.bit_length() - 1
    low = (block & (halves - 1)) * rows + (block >> shift) * BROWS + first
    inside = (place >= low) & (place < low + BROWS)
    lines = [
        jnp.sum(jnp.where(inside, table, 0.0), axis=0, keepdims=True) for table in (start, target)
    ]
    out_ref[...] = jnp.zeros(out_ref.shape, f32)
    out_ref[0:BROWS, :] = spread
    for t, line in enumerate(lines):
        for k in range(table_lines):
            at = BROWS + t * table_lines + k
            used = min(width, length - k * width)
            out_ref[at : at + 1, 0:used] = line[:, k * width : k * width + used]
    counted_ref[...] = jnp.zeros(counted_ref.shape, f32)
    counted_ref[0:1, 0 : count_ref.shape[1]] = count_ref[...].astype(f32)


def taps_kernel(kernels_hbm, strength_hbm, line_ref, gain_ref, kernels_ref, strength_ref, sem):
    for copy in fetch(((kernels_hbm, kernels_ref), (strength_hbm, strength_ref)), sem):
        copy.wait()
    passes, bands, taps_count = kernels_ref.shape
    wide = line_ref.shape[2]
    pad = jnp.zeros((bands, LANES - taps_count), f32)
    mirror = lax.broadcasted_iota(jnp.int32, (LANES, LANES), 0) + lax.broadcasted_iota(
        jnp.int32, (LANES, LANES), 1
    )
    mirror = jnp.where(mirror == taps_count - 1, 1.0, 0.0).astype(f32)
    rest = jnp.zeros((bands, wide - LANES), f32)
    for p in range(passes):
        taps = kernels_ref[p]
        taps = taps / jnp.sum(taps, axis=1, keepdims=True)
        taps = jnp.concatenate([taps, pad], axis=1)
        strength = upright(strength_ref[p : p + 1, :])
        turned = jnp.dot(taps, mirror, precision=lax.Precision.HIGHEST)
        at = slice(p * bands, (p + 1) * bands)
        line_ref[0, at, :] = jnp.concatenate([taps * strength, rest], axis=1)
        line_ref[1, at, :] = jnp.concatenate([turned, rest], axis=1)
        gain_ref[at, :] = jnp.broadcast_to(1.0 + strength, (bands, gain_ref.shape[1]))


def banded(line, size, radius):
    wide = line.shape[1]
    spread = jnp.broadcast_to(line, (size, wide))
    return split(pltpu.roll(spread, wide - radius, 1, stride=1, stride_axis=0)[:, :size])


def correct_kernel(
    x_ref, line_ref, gain_ref, counted_ref, *refs, passes, bands, radius, table_lines
):
    spaces, per, strip, width = x_ref.shape
    table_refs, (out_ref, state) = refs[:spaces], refs[spaces:]
    rows = spaces * strip
    halves = width // BCOLS
    length = halves * rows
    own = lax.axis_index("space")

    def table(t):
        lines = []
        for k in range(table_lines):
            at = BROWS + t * table_lines + k
            used = min(width, length - k * width)
            lines.append(total(ref[at : at + 1, 0:used] for ref in table_refs))
        return jnp.concatenate(lines, axis=1)

    start, target = table(0), table(1)
    entries = jnp.zeros((BROWS, length), f32)
    for d in range(spaces):
        matrix = jnp.concatenate([table_refs[d][0:BROWS, :]] * (length // width), axis=1)
        entries = jnp.where(target == (own ^ d).astype(f32), matrix, entries)
    share = (out_ref.shape[1] - SUBLANES) // per
    map_rows = out_ref.shape[0] * share
    line = lax.broadcasted_iota(jnp.int32, (map_rows, length), 0)
    offset = line - start.astype(jnp.int32)
    placer = jnp.zeros((map_rows, length), f32)
    for i in range(BROWS):
        placer = jnp.where(offset == i, entries[i : i + 1, :], placer)
    ah, al = split(placer)
    stacked = jnp.concatenate([ah, al], axis=0)

    for step in range(passes):
        middle = []
        for slot in range(bands):
            k = step * bands + slot
            rh, rl = banded(line_ref[0, k : k + 1, :], rows, radius)
            left = jnp.concatenate([rh, rh], axis=1)
            for i in range(slot, per, bands):
                if step == 0:
                    image = jnp.concatenate([x_ref[s, i] for s in range(spaces)], axis=0)
                    state[i] = image
                else:
                    image = state[i]
                xh, xl = split(image)
                both = mm(left, jnp.concatenate([xh, xl], axis=0))
                middle.append(split(both + mm(rl, xh)))
        for slot in range(bands):
            k = step * bands + slot
            ch, cl = banded(line_ref[1, k : k + 1, :], width, radius)
            group = range(slot, per, bands)
            mine = middle[slot * len(group) : (slot + 1) * len(group)]
            high = jnp.concatenate([yh for yh, _ in mine], axis=0)
            low = jnp.concatenate([yl for _, yl in mine], axis=0)
            both = mm(jnp.concatenate([high, low], axis=0), ch)
            size = high.shape[0]
            blurred = both[:size] + both[size:] + mm(high, cl)
            gain = gain_ref[k : k + 1, :]
            for q, i in enumerate(group):
                state[i] = gain * state[i] - blurred[q * rows : (q + 1) * rows]
    for i in range(0, per, 2):
        pair = range(i, min(i + 2, per))
        z = jnp.concatenate(
            [
                jnp.concatenate(
                    [state[j, :, h * BCOLS : (h + 1) * BCOLS] for h in range(halves)], axis=0
                )
                for j in pair
            ],
            axis=1,
        )
        zh, zl = split(z)
        both = mm(stacked, zh)
        laid = both[:map_rows] + both[map_rows:] + mm(ah, zl)
        for p, j in enumerate(pair):
            at = SUBLANES + j * share
            for d in range(out_ref.shape[0]):
                out_ref[d, at : at + share, :] = laid[
                    d * share : (d + 1) * share, p * BCOLS : (p + 1) * BCOLS
                ]
    for d in range(out_ref.shape[0]):
        out_ref[d, :SUBLANES, :] = counted_ref[...]


def columns_of(block, kh, kl):
    bh, bl = split(block)
    both = mm(jnp.concatenate([bh, bl], axis=0), kh)
    size = block.shape[0]
    return both[:size] + both[size:] + mm(bh, kl)


def halve_kernel(cols_ref, kh_ref, kl_ref):
    kh_ref[...], kl_ref[...] = split(cols_ref[0])


def median_kernel(
    y_ref, kh_ref, kl_ref, *refs, spaces, dates, cores, bands, local_dates
):
    out_refs, (full_ref, weight_ref, result) = refs[:cores], refs[cores:]
    sources, per, share, width = full_ref.shape
    kh, kl = kh_ref[...], kl_ref[...]
    for s in range(sources):
        full = columns_of(y_ref[s, SUBLANES:, :], kh, kl)
        full_ref[s] = full.reshape(per, share, width)
    summed = total(y_ref[s, 0:1, :] for s in range(0, sources, cores))
    mean_count = jnp.sum(summed, axis=1, keepdims=True) / f32(spaces * dates * local_dates)
    own = lax.axis_index("space")
    for x in range(dates):
        counted = y_ref[(own * dates + x) * cores, 0:1, :]
        weight = counted / (counted + mean_count)
        for t in range(local_dates):
            weight_ref[x * local_dates + t] = jnp.broadcast_to(
                weight[:, t : t + 1], weight_ref.shape[1:]
            )
    total_bands = cores * bands
    where = [[None] * total_bands for _ in range(dates * local_dates)]
    for z in range(spaces):
        for x in range(dates):
            for c in range(cores):
                for i in range(per):
                    t, b = divmod(z * per + i, bands)
                    where[x * local_dates + t][c * bands + b] = ((z * dates + x) * cores + c, i)
    tile = weight_ref.shape[1]
    for start in range(0, share, tile):
        rows = pl.ds(start, tile)

        def load(t):
            return [full_ref[s, i, rows, :] for s, i in where[t]]

        number = [jnp.zeros((tile, width), f32)] * total_bands
        below = jnp.zeros((tile, width), f32)
        for t, _ in enumerate(where):
            w = weight_ref[t]
            below = below + w
            number = [n + w * v for n, v in zip(number, load(t))]
        estimate = [n / below for n in number]
        for _ in range(ITERS):
            number = [jnp.zeros((tile, width), f32)] * total_bands
            below = jnp.zeros((tile, width), f32)
            for t, _ in enumerate(where):
                values = load(t)
                squares = []
                for v, e in zip(values, estimate):
                    gap = v - e
                    squares.append(gap * gap)
                scaled = weight_ref[t] / jnp.sqrt(total(squares) + smooth_sq)
                below = below + scaled
                number = [n + scaled * v for n, v in zip(number, values)]
            estimate = [n / below for n in number]
        for b in range(total_bands):
            result[b // bands, b % bands, rows, :] = estimate[b]
    core = lax.axis_index("band")
    for k in range(cores):
        out_refs[k][...] = result[core ^ k]


def place_kernel(*refs, dates, cores):
    out_ref = refs[-1]
    share = refs[0].shape[1]
    x, c = lax.axis_index("date"), lax.axis_index("band")
    for dx in range(dates):
        for dc in range(cores):
            j = (x ^ dx) * cores + (c ^ dc)
            at = pl.ds(pl.multiple_of(j * share, share), share)
            out_ref[:, at, :] = refs[dx * cores + dc][...]


def across_sides(pieces, dates, cores):
    received = [pieces[0]]
    for k in range(1, dates * cores):
        pairs = [
            (x * cores + c, (x ^ (k // cores)) * cores + (c ^ (k % cores)))
            for x in range(dates)
            for c in range(cores)
        ]
        received.append(lax.ppermute(pieces[k], ("date", "band"), pairs))
    return received


def local(
    reflect, kernels, strength, destinations, offsets, counts, resample_rows, resample_columns
):
    spaces, dates, cores = (lax.axis_size(a) for a in ("space", "date", "band"))
    local_dates, bands, strip, width = reflect.shape
    passes = kernels.shape[0]
    blocks = offsets.shape[0]
    rows = spaces * strip
    halves = width // BCOLS
    length = halves * rows
    table_lines = -(-length // width)
    tile_rows = blocks * BROWS
    sources = spaces * dates * cores
    share = tile_rows // (dates * cores)
    tile = min(share, SUBLANES)
    per = local_dates * bands // spaces
    images = reflect.reshape(local_dates * bands, strip, width)
    whole = lax.all_to_all(images, "space", split_axis=0, concat_axis=0, tiled=True)

    make_tables = pl.pallas_call(
        functools.partial(
            tables_kernel, spaces=spaces, strip=strip, halves=halves, table_lines=table_lines
        ),
        out_shape=[
            jax.ShapeDtypeStruct((round_up(BROWS + 2 * table_lines, SUBLANES), width), f32),
            jax.ShapeDtypeStruct((SUBLANES, BCOLS), f32),
        ],
        in_specs=hbm(4),
        out_specs=vmem(2),
        scratch_shapes=[
            pltpu.VMEM((1, blocks), jnp.int32),
            pltpu.VMEM((1, blocks), jnp.int32),
            pltpu.VMEM((1, BROWS, BROWS), f32),
            pltpu.VMEM((1, local_dates), jnp.int32),
            pltpu.SemaphoreType.DMA((4,)),
        ],
        compiler_params=params(4),
        name="tables",
    )
    table, counted = make_tables(
        destinations.reshape(1, blocks),
        offsets.reshape(1, blocks),
        resample_rows,
        counts.reshape(1, local_dates),
    )
    tables = [table]
    for d in range(1, spaces):
        tables.append(lax.ppermute(table, "space", [(i, i ^ d) for i in range(spaces)]))

    here = bands if per % bands == 0 else per
    if here != bands:
        first_band = (lax.axis_index("space") * per) % bands
        kernels = lax.dynamic_slice_in_dim(kernels, first_band, here, axis=1)
        strength = lax.dynamic_slice_in_dim(strength, first_band, here, axis=1)
    wide = max(rows, width) + LANES
    count = passes * here
    make_lines = pl.pallas_call(
        taps_kernel,
        out_shape=[
            jax.ShapeDtypeStruct((2, count, wide), f32),
            jax.ShapeDtypeStruct((count, width), f32),
        ],
        in_specs=hbm(2),
        out_specs=vmem(2),
        scratch_shapes=[
            pltpu.VMEM(kernels.shape, f32),
            pltpu.VMEM(strength.shape, f32),
            pltpu.SemaphoreType.DMA((2,)),
        ],
        compiler_params=params(4),
        name="taps",
    )
    lines, gains = make_lines(kernels, strength)

    laid = pl.pallas_call(
        functools.partial(
            correct_kernel,
            passes=passes,
            bands=here,
            radius=kernels.shape[2] // 2,
            table_lines=table_lines,
        ),
        out_shape=jax.ShapeDtypeStruct((sources, SUBLANES + per * share, BCOLS), f32),
        in_specs=vmem(4 + spaces),
        out_specs=pl.BlockSpec(memory_space=pltpu.VMEM),
        scratch_shapes=[pltpu.VMEM((per, rows, width), f32)],
        compiler_params=params(24),
        name="correct",
    )(whole.reshape(spaces, per, strip, width), lines, gains, counted, *tables)
    pixels = lax.all_to_all(
        laid, ("space", "date", "band"), split_axis=0, concat_axis=0, tiled=True
    )

    halve = pl.pallas_call(
        halve_kernel,
        out_shape=[jax.ShapeDtypeStruct((BCOLS, BCOLS), bf16)] * 2,
        in_specs=vmem(1),
        out_specs=vmem(2),
        compiler_params=params(2),
        name="halve",
    )
    columns = halve(resample_columns)
    shares = pl.pallas_call(
        functools.partial(
            median_kernel,
            spaces=spaces,
            dates=dates,
            cores=cores,
            bands=bands,
            local_dates=local_dates,
        ),
        out_shape=[jax.ShapeDtypeStruct((bands, share, BCOLS), f32)] * cores,
        in_specs=vmem(3),
        out_specs=vmem(cores),
        scratch_shapes=[
            pltpu.VMEM((sources, per, share, BCOLS), f32),
            pltpu.VMEM((dates * local_dates, tile, BCOLS), f32),
            pltpu.VMEM((cores, bands, share, BCOLS), f32),
        ],
        compiler_params=params(12),
        name="median",
    )(pixels, *columns)

    pieces = across_sides([shares[k % cores] for k in range(dates * cores)], dates, cores)
    return pl.pallas_call(
        functools.partial(place_kernel, dates=dates, cores=cores),
        out_shape=jax.ShapeDtypeStruct((bands, tile_rows, BCOLS), f32),
        in_specs=vmem(dates * cores),
        out_specs=pl.BlockSpec(memory_space=pltpu.VMEM),
        compiler_params=params(4),
        name="place",
    )(*pieces)


def solution(mesh):
    in_specs = (
        P("date", "band", ("groups", "space"), None),
        P(None, "band", None),
        P(None, "band"),
        P(("groups", "space"), None),
        P(("groups", "space")),
        P("date", ("groups", "space")),
        P(("groups", "space"), None, None),
        P(("groups", "space"), None, None),
    )
    out_specs = P("band", ("groups", "space"), None)

    return jax.shard_map(local, mesh=mesh, in_specs=in_specs, out_specs=out_specs, check_vma=False)
```

```python
import functools

import jax
import jax.numpy as jnp
from jax import lax
from jax.experimental import pallas as pl
from jax.experimental.pallas import tpu as pltpu
from jax.sharding import PartitionSpec as P


BROWS = 4
BCOLS = 128
ITERS = 4
LANES = 128
SUBLANES = 8


smooth_sq = 0.01
f32 = jnp.float32
bf16 = jnp.bfloat16


def split(x):
    high = x.astype(bf16)
    return high, (x - high.astype(f32)).astype(bf16)


def mm(a, b):
    return jnp.dot(a, b, preferred_element_type=f32)


def total(terms):
    terms = list(terms)
    while len(terms) > 1:
        terms = [a + b for a, b in zip(terms[::2], terms[1::2])] + terms[len(terms) & ~1 :]
    return terms[0]


def round_up(value, unit):
    return -(-value // unit) * unit


def vmem(count):
    return [pl.BlockSpec(memory_space=pltpu.VMEM)] * count


def hbm(count):
    return [pl.BlockSpec(memory_space=pltpu.HBM)] * count


def fetch(pairs, sem):
    copies = [pltpu.make_async_copy(src, dst, sem.at[k]) for k, (src, dst) in enumerate(pairs)]
    for copy in copies:
        copy.start()
    return copies


def params(mib):
    return pltpu.CompilerParams(vmem_limit_bytes=mib << 20)


def upright(line):
    size = line.shape[1]
    eye = lax.broadcasted_iota(jnp.int32, (size, size), 0) == lax.broadcasted_iota(
        jnp.int32, (size, size), 1
    )
    spread = jnp.broadcast_to(line, (size, size))
    return jnp.sum(jnp.where(eye, spread, 0.0), axis=1, keepdims=True)


def pack_kernel(
    target_hbm,
    start_hbm,
    rows_hbm,
    images_ref,
    *refs,
    halves,
    table_lines,
):
    spaces, part, strip, width = images_ref.shape
    outs, (target_ref, start_ref, rows_ref, sem) = refs[:spaces], refs[spaces:]
    tables = fetch(
        zip(
            (target_hbm, start_hbm, rows_hbm),
            (target_ref, start_ref, rows_ref),
        ),
        sem,
    )
    own = lax.axis_index("space")
    size = part * strip
    for d in range(spaces):
        outs[d][:size, :] = images_ref[own ^ d].reshape(size, width)
    for table in tables:
        table.wait()
    blocks = target_ref.shape[1]
    rows = spaces * strip
    matrix = rows_ref[0]
    lane = lax.broadcasted_iota(jnp.int32, (BROWS, width), 1) & (BROWS - 1)
    spread = jnp.zeros((BROWS, width), f32)
    for k in range(BROWS):
        spread = jnp.where(lane == k, jnp.broadcast_to(matrix[:, k : k + 1], spread.shape), spread)
    target = upright(target_ref[...].astype(f32))
    start = target * f32(blocks * BROWS) + upright(start_ref[...].astype(f32))
    length = halves * rows
    place = lax.broadcasted_iota(jnp.int32, (blocks, length), 1)
    block = lax.broadcasted_iota(jnp.int32, (blocks, length), 0)
    first = own * strip
    shift = halves.bit_length() - 1
    low = (block & (halves - 1)) * rows + (block >> shift) * BROWS + first
    inside = (place >= low) & (place < low + BROWS)
    lines = [
        jnp.sum(jnp.where(inside, table, 0.0), axis=0, keepdims=True) for table in (start, target)
    ]
    for out in outs:
        out[size:, :] = jnp.zeros((out.shape[0] - size, width), f32)
        out[size : size + BROWS, :] = spread
        for t, line in enumerate(lines):
            for k in range(table_lines):
                at = size + BROWS + t * table_lines + k
                used = min(width, length - k * width)
                out[at : at + 1, 0:used] = line[:, k * width : k * width + used]


def taps_kernel(kernels_hbm, strength_hbm, line_ref, gain_ref, kernels_ref, strength_ref, sem):
    for copy in fetch(((kernels_hbm, kernels_ref), (strength_hbm, strength_ref)), sem):
        copy.wait()
    passes, bands, taps_count = kernels_ref.shape
    wide = line_ref.shape[2]
    pad = jnp.zeros((bands, LANES - taps_count), f32)
    mirror = lax.broadcasted_iota(jnp.int32, (LANES, LANES), 0) + lax.broadcasted_iota(
        jnp.int32, (LANES, LANES), 1
    )
    mirror = jnp.where(mirror == taps_count - 1, 1.0, 0.0).astype(f32)
    rest = jnp.zeros((bands, wide - LANES), f32)
    for p in range(passes):
        taps = kernels_ref[p]
        taps = taps / jnp.sum(taps, axis=1, keepdims=True)
        taps = jnp.concatenate([taps, pad], axis=1)
        strength = upright(strength_ref[p : p + 1, :])
        turned = jnp.dot(taps, mirror, precision=lax.Precision.HIGHEST)
        at = slice(p * bands, (p + 1) * bands)
        line_ref[0, at, :] = jnp.concatenate([taps * strength, rest], axis=1)
        line_ref[1, at, :] = jnp.concatenate([turned, rest], axis=1)
        gain_ref[at, :] = jnp.broadcast_to(1.0 + strength, (bands, gain_ref.shape[1]))


def banded(line, size, radius):
    wide = line.shape[1]
    spread = jnp.broadcast_to(line, (size, wide))
    return split(pltpu.roll(spread, wide - radius, 1, stride=1, stride_axis=0)[:, :size])


def corrections(state, line_ref, gain_ref, first, passes, bands, radius):
    part, rows, width = state.shape
    groups = [[i for i in range(part) if (first + i) % bands == slot] for slot in range(bands)]
    for step in range(passes):
        middle = {}
        for slot, group in enumerate(groups):
            if group:
                k = step * bands + slot
                rh, rl = banded(line_ref[0, k : k + 1, :], rows, radius)
                left = jnp.concatenate([rh, rh], axis=1)
            for i in group:
                xh, xl = split(state[i])
                both = mm(left, jnp.concatenate([xh, xl], axis=0))
                middle[i] = split(both + mm(rl, xh))
        for slot, group in enumerate(groups):
            if not group:
                continue
            k = step * bands + slot
            ch, cl = banded(line_ref[1, k : k + 1, :], width, radius)
            high = jnp.concatenate([middle[i][0] for i in group], axis=0)
            low = jnp.concatenate([middle[i][1] for i in group], axis=0)
            both = mm(jnp.concatenate([high, low], axis=0), ch)
            size = high.shape[0]
            blurred = both[:size] + both[size:] + mm(high, cl)
            gain = gain_ref[k : k + 1, :]
            for q, i in enumerate(group):
                state[i] = gain * state[i] - blurred[q * rows : (q + 1) * rows]


def laid_pairs(state, ah, al):
    part, _, width = state.shape
    map_rows = ah.shape[0]
    stacked = jnp.concatenate([ah, al], axis=0)
    for i in range(0, part, 2):
        pair = range(i, min(i + 2, part))
        z = jnp.concatenate(
            [
                jnp.concatenate(
                    [state[j, :, h : h + BCOLS] for h in range(0, width, BCOLS)], axis=0
                )
                for j in pair
            ],
            axis=1,
        )
        zh, zl = split(z)
        both = mm(stacked, zh)
        yield pair, both[:map_rows] + both[map_rows:] + mm(ah, zl)


def small_kernel(
    line_ref, gain_ref, count_ref, *refs, spaces, cores, passes, bands, radius, share, table_lines
):
    x_refs, (*out_refs, ah_ref, al_ref, state, laid_ref) = refs[:spaces], refs[spaces:]
    part, rows, width = state.shape
    strip = rows // spaces
    tables = part * strip
    length = width // BCOLS * rows
    own = lax.axis_index("space")
    for d in range(spaces):
        at = pl.ds(pl.multiple_of((own ^ d) * strip, strip), strip)
        for i in range(part):
            state[i, at, :] = x_refs[d][i * strip : (i + 1) * strip, :]

    def table(t):
        lines = []
        for k in range(table_lines):
            at = tables + BROWS + t * table_lines + k
            used = min(width, length - k * width)
            lines.append(total(ref[at : at + 1, 0:used] for ref in x_refs))
        return jnp.concatenate(lines, axis=1)

    start, target = table(0), table(1)
    entries = jnp.zeros((BROWS, length), f32)
    for d in range(spaces):
        matrix = x_refs[d][tables : tables + BROWS, :]
        matrix = jnp.concatenate([matrix] * (length // width), axis=1)
        entries = jnp.where(target == (own ^ d).astype(f32), matrix, entries)
    line = lax.broadcasted_iota(jnp.int32, ah_ref.shape, 0)
    offset = line - start.astype(jnp.int32)
    placer = jnp.zeros(ah_ref.shape, f32)
    for i in range(BROWS):
        placer = jnp.where(offset == i, entries[i : i + 1, :], placer)
    ah, al = split(placer)
    ah_ref[...] = ah
    al_ref[...] = al
    corrections(state, line_ref, gain_ref, 0, passes, bands, radius)
    x, c = lax.axis_index("date"), lax.axis_index("band")
    groups = laid_ref.shape[0]
    for pair, laid in laid_pairs(state, ah, al):
        for m in range(groups):
            laid_ref[m, :, : laid.shape[1]] = laid[m * share : (m + 1) * share]
        for k, out in enumerate(out_refs):
            mine = (x ^ (k // cores)) * cores + (c ^ (k % cores))
            for g in range(spaces):
                lines = laid_ref[g * (groups // spaces) + mine]
                for p, j in enumerate(pair):
                    out[g, j * share : (j + 1) * share, :] = lines[
                        :, p * BCOLS : (p + 1) * BCOLS
                    ]
    counts = count_ref[...].astype(f32)
    for out in out_refs:
        for g in range(spaces):
            out[g, part * share :, :] = jnp.zeros((SUBLANES, BCOLS), f32)
            out[g, part * share : part * share + 1, 0 : counts.shape[1]] = counts


def large_kernel(
    x_ref, line_ref, gain_ref, ah_ref, al_ref, out_ref, state, *, first, passes, bands, radius
):
    spaces, part = x_ref.shape[:2]
    for i in range(part):
        state[i] = jnp.concatenate([x_ref[s, i] for s in range(spaces)], axis=0)
    corrections(state, line_ref, gain_ref, first, passes, bands, radius)
    share = out_ref.shape[1] // part
    for pair, laid in laid_pairs(state, ah_ref[...], al_ref[...]):
        for p, j in enumerate(pair):
            for d in range(out_ref.shape[0]):
                out_ref[d, j * share : (j + 1) * share, :] = laid[
                    d * share : (d + 1) * share, p * BCOLS : (p + 1) * BCOLS
                ]


def columns_of(block, kh, kl):
    bh, bl = split(block)
    both = mm(jnp.concatenate([bh, bl], axis=0), kh)
    size = block.shape[0]
    return both[:size] + both[size:] + mm(bh, kl)


def halve_kernel(cols_ref, kh_ref, kl_ref):
    kh_ref[...], kl_ref[...] = split(cols_ref[0])


def regroup_kernel(*refs, spaces):
    groups = len(refs) - spaces
    own = lax.axis_index("space")
    for d in range(spaces):
        for k in range(groups):
            refs[groups + d][k] = refs[k][own ^ d]


def columns_kernel(
    kh_ref, kl_ref, *refs, spaces, dates, cores, local_dates
):
    y_refs, (full_ref, weight_ref) = refs[:spaces], refs[spaces:]
    sides, part, share, width = full_ref.shape[1:]
    size = part * share
    kh, kl = kh_ref[...], kl_ref[...]
    for d in range(spaces):
        block = y_refs[d][:, :size, :].reshape(sides * size, width)
        full_ref[d] = columns_of(block, kh, kl).reshape(sides, part, share, width)
    counted = [y[dx * cores, size : size + 1, :] for y in y_refs for dx in range(dates)]
    summed = jnp.sum(total(counted), axis=1, keepdims=True)
    mean_count = summed / f32(spaces * dates * local_dates)
    for dx in range(dates):
        own = y_refs[0][dx * cores, size : size + 1, :]
        weight = own / (own + mean_count)
        for t in range(local_dates):
            weight_ref[dx * local_dates + t] = jnp.broadcast_to(
                weight[:, t : t + 1], weight_ref.shape[1:]
            )


def median_kernel(
    weight_ref,
    kh_ref,
    kl_ref,
    small_ref,
    y_ref,
    *refs,
    spaces,
    dates,
    cores,
    bands,
    per,
    local_dates,
):
    out_refs, (large_ref, result) = refs[:cores], refs[cores:]
    share, width = small_ref.shape[3:]
    part = small_ref.shape[2]
    kh, kl = kh_ref[...], kl_ref[...]
    for s in range(y_ref.shape[0]):
        large_ref[s] = columns_of(y_ref[s], kh, kl).reshape(per - part, share, width)
    z, x, c = (lax.axis_index(a) for a in ("space", "date", "band"))
    across = max(1, bands // per)
    inside = max(1, per // bands)
    span = bands // across
    tile = weight_ref.shape[1]
    slots = [(dc, b) for dc in range(cores) for b in range(bands)]
    order = [
        (d, dx, t) for d in range(0, spaces, across) for dx in range(dates) for t in range(inside)
    ]
    for start in range(0, share, tile):
        rows = pl.ds(start, tile)

        def load(d, dx, t):
            values = []
            for dc, b in slots:
                far = d ^ (b // span)
                image = t * bands + b % span
                if image < part:
                    values.append(small_ref[far, dx * cores + dc, image, rows, :])
                else:
                    source = ((z ^ far) * dates + (x ^ dx)) * cores + (c ^ dc)
                    values.append(large_ref[source, image - part, rows, :])
            return values

        def weight(d, dx, t):
            return weight_ref[dx * local_dates + (z ^ d) // across * inside + t]

        number = [jnp.zeros((tile, width), f32)] * len(slots)
        below = jnp.zeros((tile, width), f32)
        for key in order:
            w = weight(*key)
            below = below + w
            number = [n + w * v for n, v in zip(number, load(*key))]
        estimate = [n / below for n in number]
        for _ in range(ITERS):
            number = [jnp.zeros((tile, width), f32)] * len(slots)
            below = jnp.zeros((tile, width), f32)
            for key in order:
                values = load(*key)
                squares = []
                for v, e in zip(values, estimate):
                    gap = v - e
                    squares.append(gap * gap)
                scaled = weight(*key) / jnp.sqrt(total(squares) + smooth_sq)
                below = below + scaled
                number = [n + scaled * v for n, v in zip(number, values)]
            estimate = [n / below for n in number]
        for (dc, b), value in zip(slots, estimate):
            if across == 1:
                out_refs[dc][b, rows, :] = value
            else:
                result[dc, ((z % across) ^ (b // span)) * span + b % span, rows, :] = value
    if across > 1:
        for dc in range(cores):
            out_refs[dc][...] = result[dc]


def place_kernel(*refs, dates, cores):
    out_ref = refs[-1]
    share = refs[0].shape[1]
    x, c = lax.axis_index("date"), lax.axis_index("band")
    for dx in range(dates):
        for dc in range(cores):
            j = (x ^ dx) * cores + (c ^ dc)
            at = pl.ds(pl.multiple_of(j * share, share), share)
            out_ref[:, at, :] = refs[dx * cores + dc][...]


def across_sides(pieces, dates, cores):
    received = [pieces[0]]
    for k in range(1, dates * cores):
        pairs = [
            (x * cores + c, (x ^ (k // cores)) * cores + (c ^ (k % cores)))
            for x in range(dates)
            for c in range(cores)
        ]
        received.append(lax.ppermute(pieces[k], ("date", "band"), pairs))
    return received


def local(
    reflect, kernels, strength, destinations, offsets, counts, resample_rows, resample_columns
):
    spaces, dates, cores = (lax.axis_size(a) for a in ("space", "date", "band"))
    local_dates, bands, strip, width = reflect.shape
    passes = kernels.shape[0]
    blocks = offsets.shape[0]
    rows = spaces * strip
    halves = width // BCOLS
    length = halves * rows
    table_lines = -(-length // width)
    tile_rows = blocks * BROWS
    sources = spaces * dates * cores
    share = tile_rows // (dates * cores)
    tile = min(share, SUBLANES)
    per = local_dates * bands // spaces
    part = max(1, per // 4)
    images = reflect.reshape(spaces, per, strip, width)
    pack = pl.pallas_call(
        functools.partial(pack_kernel, halves=halves, table_lines=table_lines),
        out_shape=[
            jax.ShapeDtypeStruct(
                (part * strip + round_up(BROWS + 2 * table_lines, SUBLANES), width), f32
            )
        ]
        * spaces,
        in_specs=hbm(3) + vmem(1),
        out_specs=vmem(spaces),
        scratch_shapes=[
            pltpu.VMEM((1, blocks), jnp.int32),
            pltpu.VMEM((1, blocks), jnp.int32),
            pltpu.VMEM((1, BROWS, BROWS), f32),
            pltpu.SemaphoreType.DMA((3,)),
        ],
        compiler_params=params(4),
        name="pack",
    )
    small = list(
        pack(
            destinations.reshape(1, blocks),
            offsets.reshape(1, blocks),
            resample_rows,
            images[:, :part],
        )
    )
    for d in range(spaces - 1, 0, -1):
        small[d] = lax.ppermute(small[d], "space", [(i, i ^ d) for i in range(spaces)])
    large = lax.all_to_all(images[:, part:], "space", split_axis=0, concat_axis=0, tiled=True)

    here = bands if per % bands == 0 else per
    if here != bands:
        first_band = (lax.axis_index("space") * per) % bands
        kernels = lax.dynamic_slice_in_dim(kernels, first_band, here, axis=1)
        strength = lax.dynamic_slice_in_dim(strength, first_band, here, axis=1)
    wide = max(rows, width) + LANES
    count = passes * here
    make_lines = pl.pallas_call(
        taps_kernel,
        out_shape=[
            jax.ShapeDtypeStruct((2, count, wide), f32),
            jax.ShapeDtypeStruct((count, width), f32),
        ],
        in_specs=hbm(2),
        out_specs=vmem(2),
        scratch_shapes=[
            pltpu.VMEM(kernels.shape, f32),
            pltpu.VMEM(strength.shape, f32),
            pltpu.SemaphoreType.DMA((2,)),
        ],
        compiler_params=params(4),
        name="taps",
    )
    lines, gains = make_lines(kernels, strength)

    settings = dict(passes=passes, bands=here, radius=kernels.shape[2] // 2)
    small_rows = part * share + SUBLANES
    correct_small = pl.pallas_call(
        functools.partial(
            small_kernel,
            spaces=spaces,
            cores=cores,
            share=share,
            table_lines=table_lines,
            **settings,
        ),
        out_shape=[jax.ShapeDtypeStruct((spaces, small_rows, BCOLS), f32)] * (dates * cores)
        + [jax.ShapeDtypeStruct((spaces * tile_rows, length), bf16)] * 2,
        in_specs=vmem(3 + spaces),
        out_specs=vmem(dates * cores + 2),
        scratch_shapes=[
            pltpu.VMEM((part, rows, width), f32),
            pltpu.VMEM((spaces * tile_rows // share, share, 2 * BCOLS), f32),
        ],
        compiler_params=params(20),
        name="correct0",
    )
    *sides, ah, al = correct_small(lines, gains, counts.reshape(1, local_dates), *small)
    sides = across_sides(sides, dates, cores)
    regroup = pl.pallas_call(
        functools.partial(regroup_kernel, spaces=spaces),
        out_shape=[jax.ShapeDtypeStruct((dates * cores, small_rows, BCOLS), f32)] * spaces,
        in_specs=vmem(dates * cores),
        out_specs=vmem(spaces),
        compiler_params=params(4),
        name="regroup",
    )
    small = list(regroup(*sides))
    for d in range(spaces - 1, 0, -1):
        small[d] = lax.ppermute(small[d], "space", [(i, i ^ d) for i in range(spaces)])

    correct_large = pl.pallas_call(
        functools.partial(large_kernel, first=part, **settings),
        out_shape=jax.ShapeDtypeStruct((sources, (per - part) * share, BCOLS), f32),
        in_specs=vmem(5),
        out_specs=pl.BlockSpec(memory_space=pltpu.VMEM),
        scratch_shapes=[pltpu.VMEM((per - part, rows, width), f32)],
        compiler_params=params(20),
        name="correct1",
    )
    laid = correct_large(large, lines, gains, ah, al)
    pixels = lax.all_to_all(
        laid, ("space", "date", "band"), split_axis=0, concat_axis=0, tiled=True
    )

    halve = pl.pallas_call(
        halve_kernel,
        out_shape=[jax.ShapeDtypeStruct((BCOLS, BCOLS), bf16)] * 2,
        in_specs=vmem(1),
        out_specs=vmem(2),
        compiler_params=params(2),
        name="halve",
    )
    columns = halve(resample_columns)
    columns_call = pl.pallas_call(
        functools.partial(
            columns_kernel, spaces=spaces, dates=dates, cores=cores, local_dates=local_dates
        ),
        out_shape=[
            jax.ShapeDtypeStruct((spaces, dates * cores, part, share, BCOLS), f32),
            jax.ShapeDtypeStruct((dates * local_dates, tile, BCOLS), f32),
        ],
        in_specs=vmem(2 + spaces),
        out_specs=vmem(2),
        compiler_params=params(8),
        name="columns",
    )
    full, weights = columns_call(*columns, *small)
    shares = pl.pallas_call(
        functools.partial(
            median_kernel,
            spaces=spaces,
            dates=dates,
            cores=cores,
            bands=bands,
            per=per,
            local_dates=local_dates,
        ),
        out_shape=[jax.ShapeDtypeStruct((bands, share, BCOLS), f32)] * cores,
        in_specs=vmem(5),
        out_specs=vmem(cores),
        scratch_shapes=[
            pltpu.VMEM((sources, per - part, share, BCOLS), f32),
            pltpu.VMEM((cores, bands, share, BCOLS), f32),
        ],
        compiler_params=params(12),
        name="median",
    )(weights, *columns, full, pixels)

    pieces = across_sides([shares[k % cores] for k in range(dates * cores)], dates, cores)
    return pl.pallas_call(
        functools.partial(place_kernel, dates=dates, cores=cores),
        out_shape=jax.ShapeDtypeStruct((bands, tile_rows, BCOLS), f32),
        in_specs=vmem(dates * cores),
        out_specs=pl.BlockSpec(memory_space=pltpu.VMEM),
        compiler_params=params(4),
        name="place",
    )(*pieces)


def solution(mesh):
    in_specs = (
        P("date", "band", ("groups", "space"), None),
        P(None, "band", None),
        P(None, "band"),
        P(("groups", "space"), None),
        P(("groups", "space")),
        P("date", ("groups", "space")),
        P(("groups", "space"), None, None),
        P(("groups", "space"), None, None),
    )
    out_specs = P("band", ("groups", "space"), None)

    return jax.shard_map(local, mesh=mesh, in_specs=in_specs, out_specs=out_specs, check_vma=False)
```

```python
import functools

import jax
import jax.numpy as jnp
from jax import lax
from jax.experimental import pallas as pl
from jax.experimental.pallas import tpu as pltpu
from jax.sharding import PartitionSpec as P


BROWS = 4
BCOLS = 128
ITERS = 4
LANES = 128
SUBLANES = 8


smooth_sq = 0.01
f32 = jnp.float32
bf16 = jnp.bfloat16


def split(x):
    high = x.astype(bf16)
    return high, (x - high.astype(f32)).astype(bf16)


def mm(a, b):
    return jnp.dot(a, b, preferred_element_type=f32)


def total(terms):
    terms = list(terms)
    while len(terms) > 1:
        terms = [a + b for a, b in zip(terms[::2], terms[1::2])] + terms[len(terms) & ~1 :]
    return terms[0]


def round_up(value, unit):
    return -(-value // unit) * unit


def vmem(count):
    return [pl.BlockSpec(memory_space=pltpu.VMEM)] * count


def hbm(count):
    return [pl.BlockSpec(memory_space=pltpu.HBM)] * count


def fetch(pairs, sem):
    copies = [pltpu.make_async_copy(src, dst, sem.at[k]) for k, (src, dst) in enumerate(pairs)]
    for copy in copies:
        copy.start()
    return copies


def params(mib):
    return pltpu.CompilerParams(vmem_limit_bytes=mib << 20)


def upright(line):
    size = line.shape[1]
    eye = lax.broadcasted_iota(jnp.int32, (size, size), 0) == lax.broadcasted_iota(
        jnp.int32, (size, size), 1
    )
    spread = jnp.broadcast_to(line, (size, size))
    return jnp.sum(jnp.where(eye, spread, 0.0), axis=1, keepdims=True)


def pack_kernel(
    target_hbm,
    start_hbm,
    rows_hbm,
    images_ref,
    *refs,
    part,
    halves,
    table_lines,
):
    spaces, _, strip, width = images_ref.shape
    outs, (target_ref, start_ref, rows_ref, sem) = refs[:spaces], refs[spaces:]
    tables = fetch(
        zip(
            (target_hbm, start_hbm, rows_hbm),
            (target_ref, start_ref, rows_ref),
        ),
        sem,
    )
    own = lax.axis_index("space")
    size = part * strip
    for d in range(spaces):
        outs[d][:size, :] = images_ref[own ^ d, 0:part].reshape(size, width)
    for table in tables:
        table.wait()
    blocks = target_ref.shape[1]
    rows = spaces * strip
    matrix = rows_ref[0]
    lane = lax.broadcasted_iota(jnp.int32, (BROWS, width), 1) & (BROWS - 1)
    spread = jnp.zeros((BROWS, width), f32)
    for k in range(BROWS):
        spread = jnp.where(lane == k, jnp.broadcast_to(matrix[:, k : k + 1], spread.shape), spread)
    target = upright(target_ref[...].astype(f32))
    start = target * f32(blocks * BROWS) + upright(start_ref[...].astype(f32))
    length = halves * rows
    place = lax.broadcasted_iota(jnp.int32, (blocks, length), 1)
    block = lax.broadcasted_iota(jnp.int32, (blocks, length), 0)
    first = own * strip
    shift = halves.bit_length() - 1
    low = (block & (halves - 1)) * rows + (block >> shift) * BROWS + first
    inside = (place >= low) & (place < low + BROWS)
    lines = [
        jnp.sum(jnp.where(inside, table, 0.0), axis=0, keepdims=True) for table in (start, target)
    ]
    for out in outs:
        out[size:, :] = jnp.zeros((out.shape[0] - size, width), f32)
        out[size : size + BROWS, :] = spread
        for t, line in enumerate(lines):
            for k in range(table_lines):
                at = size + BROWS + t * table_lines + k
                used = min(width, length - k * width)
                out[at : at + 1, 0:used] = line[:, k * width : k * width + used]


def cut_kernel(images_ref, out_ref):
    part = images_ref.shape[1] - out_ref.shape[1]
    for s in range(out_ref.shape[0]):
        out_ref[s] = images_ref[s, part:]


def taps_kernel(kernels_hbm, strength_hbm, line_ref, gain_ref, kernels_ref, strength_ref, sem):
    for copy in fetch(((kernels_hbm, kernels_ref), (strength_hbm, strength_ref)), sem):
        copy.wait()
    passes, bands, taps_count = kernels_ref.shape
    wide = line_ref.shape[2]
    pad = jnp.zeros((bands, LANES - taps_count), f32)
    mirror = lax.broadcasted_iota(jnp.int32, (LANES, LANES), 0) + lax.broadcasted_iota(
        jnp.int32, (LANES, LANES), 1
    )
    mirror = jnp.where(mirror == taps_count - 1, 1.0, 0.0).astype(f32)
    rest = jnp.zeros((bands, wide - LANES), f32)
    for p in range(passes):
        taps = kernels_ref[p]
        taps = taps / jnp.sum(taps, axis=1, keepdims=True)
        taps = jnp.concatenate([taps, pad], axis=1)
        strength = upright(strength_ref[p : p + 1, :])
        turned = jnp.dot(taps, mirror, precision=lax.Precision.HIGHEST)
        at = slice(p * bands, (p + 1) * bands)
        line_ref[0, at, :] = jnp.concatenate([taps * strength, rest], axis=1)
        line_ref[1, at, :] = jnp.concatenate([turned, rest], axis=1)
        gain_ref[at, :] = jnp.broadcast_to(1.0 + strength, (bands, gain_ref.shape[1]))


def banded(line, size, radius):
    wide = line.shape[1]
    spread = jnp.broadcast_to(line, (size, wide))
    return split(pltpu.roll(spread, wide - radius, 1, stride=1, stride_axis=0)[:, :size])


def corrections(state, line_ref, gain_ref, first, passes, bands, radius):
    part, rows, width = state.shape
    groups = [[i for i in range(part) if (first + i) % bands == slot] for slot in range(bands)]
    for step in range(passes):
        middle = {}
        for slot, group in enumerate(groups):
            if group:
                k = step * bands + slot
                rh, rl = banded(line_ref[0, k : k + 1, :], rows, radius)
                left = jnp.concatenate([rh, rh], axis=1)
            for i in group:
                xh, xl = split(state[i])
                both = mm(left, jnp.concatenate([xh, xl], axis=0))
                middle[i] = split(both + mm(rl, xh))
        for slot, group in enumerate(groups):
            if not group:
                continue
            k = step * bands + slot
            ch, cl = banded(line_ref[1, k : k + 1, :], width, radius)
            high = jnp.concatenate([middle[i][0] for i in group], axis=0)
            low = jnp.concatenate([middle[i][1] for i in group], axis=0)
            both = mm(jnp.concatenate([high, low], axis=0), ch)
            size = high.shape[0]
            blurred = both[:size] + both[size:] + mm(high, cl)
            gain = gain_ref[k : k + 1, :]
            for q, i in enumerate(group):
                state[i] = gain * state[i] - blurred[q * rows : (q + 1) * rows]


def laid_pairs(state, ah, al):
    part, _, width = state.shape
    map_rows = ah.shape[0]
    stacked = jnp.concatenate([ah, al], axis=0)
    for i in range(0, part, 2):
        pair = range(i, min(i + 2, part))
        z = jnp.concatenate(
            [
                jnp.concatenate(
                    [state[j, :, h : h + BCOLS] for h in range(0, width, BCOLS)], axis=0
                )
                for j in pair
            ],
            axis=1,
        )
        zh, zl = split(z)
        both = mm(stacked, zh)
        yield pair, both[:map_rows] + both[map_rows:] + mm(ah, zl)


def small_kernel(
    line_ref, gain_ref, count_ref, *refs, spaces, cores, passes, bands, radius, share, table_lines
):
    x_refs, (*out_refs, ah_ref, al_ref, state, laid_ref) = refs[:spaces], refs[spaces:]
    part, rows, width = state.shape
    strip = rows // spaces
    tables = part * strip
    length = width // BCOLS * rows
    own = lax.axis_index("space")
    for d in range(spaces):
        at = pl.ds(pl.multiple_of((own ^ d) * strip, strip), strip)
        for i in range(part):
            state[i, at, :] = x_refs[d][i * strip : (i + 1) * strip, :]

    def table(t):
        lines = []
        for k in range(table_lines):
            at = tables + BROWS + t * table_lines + k
            used = min(width, length - k * width)
            lines.append(total(ref[at : at + 1, 0:used] for ref in x_refs))
        return jnp.concatenate(lines, axis=1)

    start, target = table(0), table(1)
    entries = jnp.zeros((BROWS, length), f32)
    for d in range(spaces):
        matrix = x_refs[d][tables : tables + BROWS, :]
        matrix = jnp.concatenate([matrix] * (length // width), axis=1)
        entries = jnp.where(target == (own ^ d).astype(f32), matrix, entries)
    line = lax.broadcasted_iota(jnp.int32, ah_ref.shape, 0)
    offset = line - start.astype(jnp.int32)
    placer = jnp.zeros(ah_ref.shape, f32)
    for i in range(BROWS):
        placer = jnp.where(offset == i, entries[i : i + 1, :], placer)
    ah, al = split(placer)
    ah_ref[...] = ah
    al_ref[...] = al
    corrections(state, line_ref, gain_ref, 0, passes, bands, radius)
    x, c = lax.axis_index("date"), lax.axis_index("band")
    groups = laid_ref.shape[0]
    for pair, laid in laid_pairs(state, ah, al):
        for m in range(groups):
            laid_ref[m, :, : laid.shape[1]] = laid[m * share : (m + 1) * share]
        for k, out in enumerate(out_refs):
            mine = (x ^ (k // cores)) * cores + (c ^ (k % cores))
            for g in range(spaces):
                lines = laid_ref[g * (groups // spaces) + mine]
                for p, j in enumerate(pair):
                    out[g, j * share : (j + 1) * share, :] = lines[
                        :, p * BCOLS : (p + 1) * BCOLS
                    ]
    counts = count_ref[...].astype(f32)
    for out in out_refs:
        for g in range(spaces):
            out[g, part * share :, :] = jnp.zeros((SUBLANES, BCOLS), f32)
            out[g, part * share : part * share + 1, 0 : counts.shape[1]] = counts


def large_kernel(
    x_ref, line_ref, gain_ref, ah_ref, al_ref, out_ref, state, *, first, passes, bands, radius
):
    spaces, part = x_ref.shape[:2]
    for i in range(part):
        state[i] = jnp.concatenate([x_ref[s, i] for s in range(spaces)], axis=0)
    corrections(state, line_ref, gain_ref, first, passes, bands, radius)
    share = out_ref.shape[1] // part
    for pair, laid in laid_pairs(state, ah_ref[...], al_ref[...]):
        for p, j in enumerate(pair):
            for d in range(out_ref.shape[0]):
                out_ref[d, j * share : (j + 1) * share, :] = laid[
                    d * share : (d + 1) * share, p * BCOLS : (p + 1) * BCOLS
                ]


def columns_of(block, kh, kl):
    bh, bl = split(block)
    both = mm(jnp.concatenate([bh, bl], axis=0), kh)
    size = block.shape[0]
    return both[:size] + both[size:] + mm(bh, kl)


def halve_kernel(cols_ref, kh_ref, kl_ref):
    kh_ref[...], kl_ref[...] = split(cols_ref[0])


def regroup_kernel(*refs, spaces):
    groups = len(refs) - spaces
    own = lax.axis_index("space")
    for d in range(spaces):
        for k in range(groups):
            refs[groups + d][k] = refs[k][own ^ d]


def columns_kernel(
    kh_ref, kl_ref, *refs, spaces, dates, cores, local_dates
):
    y_refs, (full_ref, weight_ref) = refs[:spaces], refs[spaces:]
    sides, part, share, width = full_ref.shape[1:]
    size = part * share
    kh, kl = kh_ref[...], kl_ref[...]
    for d in range(spaces):
        block = y_refs[d][:, :size, :].reshape(sides * size, width)
        full_ref[d] = columns_of(block, kh, kl).reshape(sides, part, share, width)
    counted = [y[dx * cores, size : size + 1, :] for y in y_refs for dx in range(dates)]
    summed = jnp.sum(total(counted), axis=1, keepdims=True)
    mean_count = summed / f32(spaces * dates * local_dates)
    for dx in range(dates):
        own = y_refs[0][dx * cores, size : size + 1, :]
        weight = own / (own + mean_count)
        for t in range(local_dates):
            weight_ref[dx * local_dates + t] = jnp.broadcast_to(
                weight[:, t : t + 1], weight_ref.shape[1:]
            )


def median_kernel(
    weight_ref,
    kh_ref,
    kl_ref,
    small_ref,
    y_ref,
    *refs,
    spaces,
    dates,
    cores,
    bands,
    per,
    local_dates,
):
    out_refs, (large_ref, result) = refs[:cores], refs[cores:]
    share, width = small_ref.shape[3:]
    part = small_ref.shape[2]
    kh, kl = kh_ref[...], kl_ref[...]
    for s in range(y_ref.shape[0]):
        large_ref[s] = columns_of(y_ref[s], kh, kl).reshape(per - part, share, width)
    z, x, c = (lax.axis_index(a) for a in ("space", "date", "band"))
    across = max(1, bands // per)
    inside = max(1, per // bands)
    span = bands // across
    tile = weight_ref.shape[1]
    slots = [(dc, b) for dc in range(cores) for b in range(bands)]
    order = [
        (d, dx, t) for d in range(0, spaces, across) for dx in range(dates) for t in range(inside)
    ]
    for start in range(0, share, tile):
        rows = pl.ds(start, tile)

        def load(d, dx, t):
            values = []
            for dc, b in slots:
                far = d ^ (b // span)
                image = t * bands + b % span
                if image < part:
                    values.append(small_ref[far, dx * cores + dc, image, rows, :])
                else:
                    source = ((z ^ far) * dates + (x ^ dx)) * cores + (c ^ dc)
                    values.append(large_ref[source, image - part, rows, :])
            return values

        def weight(d, dx, t):
            return weight_ref[dx * local_dates + (z ^ d) // across * inside + t]

        number = [jnp.zeros((tile, width), f32)] * len(slots)
        below = jnp.zeros((tile, width), f32)
        for key in order:
            w = weight(*key)
            below = below + w
            number = [n + w * v for n, v in zip(number, load(*key))]
        estimate = [n / below for n in number]
        for _ in range(ITERS):
            number = [jnp.zeros((tile, width), f32)] * len(slots)
            below = jnp.zeros((tile, width), f32)
            for key in order:
                values = load(*key)
                squares = []
                for v, e in zip(values, estimate):
                    gap = v - e
                    squares.append(gap * gap)
                scaled = weight(*key) / jnp.sqrt(total(squares) + smooth_sq)
                below = below + scaled
                number = [n + scaled * v for n, v in zip(number, values)]
            estimate = [n / below for n in number]
        for (dc, b), value in zip(slots, estimate):
            if across == 1:
                out_refs[dc][b, rows, :] = value
            else:
                result[dc, ((z % across) ^ (b // span)) * span + b % span, rows, :] = value
    if across > 1:
        for dc in range(cores):
            out_refs[dc][...] = result[dc]


def place_kernel(*refs, dates, cores):
    out_ref = refs[-1]
    share = refs[0].shape[1]
    x, c = lax.axis_index("date"), lax.axis_index("band")
    for dx in range(dates):
        for dc in range(cores):
            j = (x ^ dx) * cores + (c ^ dc)
            at = pl.ds(pl.multiple_of(j * share, share), share)
            out_ref[:, at, :] = refs[dx * cores + dc][...]


def across_sides(pieces, dates, cores):
    received = [pieces[0]]
    for k in range(1, dates * cores):
        pairs = [
            (x * cores + c, (x ^ (k // cores)) * cores + (c ^ (k % cores)))
            for x in range(dates)
            for c in range(cores)
        ]
        received.append(lax.ppermute(pieces[k], ("date", "band"), pairs))
    return received


def local(
    reflect, kernels, strength, destinations, offsets, counts, resample_rows, resample_columns
):
    spaces, dates, cores = (lax.axis_size(a) for a in ("space", "date", "band"))
    local_dates, bands, strip, width = reflect.shape
    passes = kernels.shape[0]
    blocks = offsets.shape[0]
    rows = spaces * strip
    halves = width // BCOLS
    length = halves * rows
    table_lines = -(-length // width)
    tile_rows = blocks * BROWS
    sources = spaces * dates * cores
    share = tile_rows // (dates * cores)
    tile = min(share, SUBLANES)
    per = local_dates * bands // spaces
    part = max(1, per // 2)
    images = reflect.reshape(spaces, per, strip, width)
    pack = pl.pallas_call(
        functools.partial(pack_kernel, part=part, halves=halves, table_lines=table_lines),
        out_shape=[
            jax.ShapeDtypeStruct(
                (part * strip + round_up(BROWS + 2 * table_lines, SUBLANES), width), f32
            )
        ]
        * spaces,
        in_specs=hbm(3) + vmem(1),
        out_specs=vmem(spaces),
        scratch_shapes=[
            pltpu.VMEM((1, blocks), jnp.int32),
            pltpu.VMEM((1, blocks), jnp.int32),
            pltpu.VMEM((1, BROWS, BROWS), f32),
            pltpu.SemaphoreType.DMA((3,)),
        ],
        compiler_params=params(4),
        name="pack",
    )
    small = list(
        pack(
            destinations.reshape(1, blocks),
            offsets.reshape(1, blocks),
            resample_rows,
            images,
        )
    )
    for d in range(spaces - 1, 0, -1):
        small[d] = lax.ppermute(small[d], "space", [(i, i ^ d) for i in range(spaces)])
    cut = pl.pallas_call(
        cut_kernel,
        out_shape=jax.ShapeDtypeStruct((spaces, per - part, strip, width), f32),
        in_specs=vmem(1),
        out_specs=pl.BlockSpec(memory_space=pltpu.VMEM),
        compiler_params=params(4),
        name="cut",
    )
    rest = cut(images)
    large = lax.all_to_all(rest, "space", split_axis=0, concat_axis=0, tiled=True)

    here = bands if per % bands == 0 else per
    if here != bands:
        first_band = (lax.axis_index("space") * per) % bands
        kernels = lax.dynamic_slice_in_dim(kernels, first_band, here, axis=1)
        strength = lax.dynamic_slice_in_dim(strength, first_band, here, axis=1)
    wide = max(rows, width) + LANES
    count = passes * here
    make_lines = pl.pallas_call(
        taps_kernel,
        out_shape=[
            jax.ShapeDtypeStruct((2, count, wide), f32),
            jax.ShapeDtypeStruct((count, width), f32),
        ],
        in_specs=hbm(2),
        out_specs=vmem(2),
        scratch_shapes=[
            pltpu.VMEM(kernels.shape, f32),
            pltpu.VMEM(strength.shape, f32),
            pltpu.SemaphoreType.DMA((2,)),
        ],
        compiler_params=params(4),
        name="taps",
    )
    lines, gains = make_lines(kernels, strength)

    settings = dict(passes=passes, bands=here, radius=kernels.shape[2] // 2)
    small_rows = part * share + SUBLANES
    correct_small = pl.pallas_call(
        functools.partial(
            small_kernel,
            spaces=spaces,
            cores=cores,
            share=share,
            table_lines=table_lines,
            **settings,
        ),
        out_shape=[jax.ShapeDtypeStruct((spaces, small_rows, BCOLS), f32)] * (dates * cores)
        + [jax.ShapeDtypeStruct((spaces * tile_rows, length), bf16)] * 2,
        in_specs=vmem(3 + spaces),
        out_specs=vmem(dates * cores + 2),
        scratch_shapes=[
            pltpu.VMEM((part, rows, width), f32),
            pltpu.VMEM((spaces * tile_rows // share, share, 2 * BCOLS), f32),
        ],
        compiler_params=params(20),
        name="correct0",
    )
    *sides, ah, al = correct_small(lines, gains, counts.reshape(1, local_dates), *small)
    sides = across_sides(sides, dates, cores)
    regroup = pl.pallas_call(
        functools.partial(regroup_kernel, spaces=spaces),
        out_shape=[jax.ShapeDtypeStruct((dates * cores, small_rows, BCOLS), f32)] * spaces,
        in_specs=vmem(dates * cores),
        out_specs=vmem(spaces),
        compiler_params=params(4),
        name="regroup",
    )
    small = list(regroup(*sides))
    for d in range(spaces - 1, 0, -1):
        small[d] = lax.ppermute(small[d], "space", [(i, i ^ d) for i in range(spaces)])

    correct_large = pl.pallas_call(
        functools.partial(large_kernel, first=part, **settings),
        out_shape=jax.ShapeDtypeStruct((sources, (per - part) * share, BCOLS), f32),
        in_specs=vmem(5),
        out_specs=pl.BlockSpec(memory_space=pltpu.VMEM),
        scratch_shapes=[pltpu.VMEM((per - part, rows, width), f32)],
        compiler_params=params(20),
        name="correct1",
    )
    laid = correct_large(large, lines, gains, ah, al)
    pixels = lax.all_to_all(
        laid, ("space", "date", "band"), split_axis=0, concat_axis=0, tiled=True
    )

    halve = pl.pallas_call(
        halve_kernel,
        out_shape=[jax.ShapeDtypeStruct((BCOLS, BCOLS), bf16)] * 2,
        in_specs=vmem(1),
        out_specs=vmem(2),
        compiler_params=params(2),
        name="halve",
    )
    columns = halve(resample_columns)
    columns_call = pl.pallas_call(
        functools.partial(
            columns_kernel, spaces=spaces, dates=dates, cores=cores, local_dates=local_dates
        ),
        out_shape=[
            jax.ShapeDtypeStruct((spaces, dates * cores, part, share, BCOLS), f32),
            jax.ShapeDtypeStruct((dates * local_dates, tile, BCOLS), f32),
        ],
        in_specs=vmem(2 + spaces),
        out_specs=vmem(2),
        compiler_params=params(8),
        name="columns",
    )
    full, weights = columns_call(*columns, *small)
    shares = pl.pallas_call(
        functools.partial(
            median_kernel,
            spaces=spaces,
            dates=dates,
            cores=cores,
            bands=bands,
            per=per,
            local_dates=local_dates,
        ),
        out_shape=[jax.ShapeDtypeStruct((bands, share, BCOLS), f32)] * cores,
        in_specs=vmem(5),
        out_specs=vmem(cores),
        scratch_shapes=[
            pltpu.VMEM((sources, per - part, share, BCOLS), f32),
            pltpu.VMEM((cores, bands, share, BCOLS), f32),
        ],
        compiler_params=params(12),
        name="median",
    )(weights, *columns, full, pixels)

    pieces = across_sides([shares[k % cores] for k in range(dates * cores)], dates, cores)
    return pl.pallas_call(
        functools.partial(place_kernel, dates=dates, cores=cores),
        out_shape=jax.ShapeDtypeStruct((bands, tile_rows, BCOLS), f32),
        in_specs=vmem(dates * cores),
        out_specs=pl.BlockSpec(memory_space=pltpu.VMEM),
        compiler_params=params(4),
        name="place",
    )(*pieces)


def solution(mesh):
    in_specs = (
        P("date", "band", ("groups", "space"), None),
        P(None, "band", None),
        P(None, "band"),
        P(("groups", "space"), None),
        P(("groups", "space")),
        P("date", ("groups", "space")),
        P(("groups", "space"), None, None),
        P(("groups", "space"), None, None),
    )
    out_specs = P("band", ("groups", "space"), None)

    return jax.shard_map(local, mesh=mesh, in_specs=in_specs, out_specs=out_specs, check_vma=False)
```

```python
import functools

import jax
import jax.numpy as jnp
from jax import lax
from jax.experimental import pallas as pl
from jax.experimental.pallas import tpu as pltpu
from jax.sharding import PartitionSpec as P


BROWS = 4
BCOLS = 128
ITERS = 4
LANES = 128
SUBLANES = 8


smooth_sq = 0.01
f32 = jnp.float32
bf16 = jnp.bfloat16


def split(x):
    high = x.astype(bf16)
    return high, (x - high.astype(f32)).astype(bf16)


def mm(a, b):
    return jnp.dot(a, b, preferred_element_type=f32)


def total(terms):
    terms = list(terms)
    while len(terms) > 1:
        terms = [a + b for a, b in zip(terms[::2], terms[1::2])] + terms[len(terms) & ~1 :]
    return terms[0]


def round_up(value, unit):
    return -(-value // unit) * unit


def vmem(count):
    return [pl.BlockSpec(memory_space=pltpu.VMEM)] * count


def hbm(count):
    return [pl.BlockSpec(memory_space=pltpu.HBM)] * count


def fetch(pairs, sem):
    copies = [pltpu.make_async_copy(src, dst, sem.at[k]) for k, (src, dst) in enumerate(pairs)]
    for copy in copies:
        copy.start()
    return copies


def params(mib):
    return pltpu.CompilerParams(vmem_limit_bytes=mib << 20)


def upright(line):
    size = line.shape[1]
    eye = lax.broadcasted_iota(jnp.int32, (size, size), 0) == lax.broadcasted_iota(
        jnp.int32, (size, size), 1
    )
    spread = jnp.broadcast_to(line, (size, size))
    return jnp.sum(jnp.where(eye, spread, 0.0), axis=1, keepdims=True)


def pack_kernel(
    target_hbm,
    start_hbm,
    rows_hbm,
    count_hbm,
    images_ref,
    *refs,
    part,
    halves,
    table_lines,
):
    spaces, _, strip, width = images_ref.shape
    outs, (target_ref, start_ref, rows_ref, count_ref, sem) = refs[:spaces], refs[spaces:]
    tables = fetch(
        zip(
            (target_hbm, start_hbm, rows_hbm, count_hbm),
            (target_ref, start_ref, rows_ref, count_ref),
        ),
        sem,
    )
    own = lax.axis_index("space")
    size = part * strip
    for d in range(spaces):
        outs[d][:size, :] = images_ref[own ^ d, 0:part].reshape(size, width)
    for table in tables:
        table.wait()
    blocks = target_ref.shape[1]
    rows = spaces * strip
    matrix = rows_ref[0]
    lane = lax.broadcasted_iota(jnp.int32, (BROWS, width), 1) & (BROWS - 1)
    spread = jnp.zeros((BROWS, width), f32)
    for k in range(BROWS):
        spread = jnp.where(lane == k, jnp.broadcast_to(matrix[:, k : k + 1], spread.shape), spread)
    target = upright(target_ref[...].astype(f32))
    start = target * f32(blocks * BROWS) + upright(start_ref[...].astype(f32))
    length = halves * rows
    place = lax.broadcasted_iota(jnp.int32, (blocks, length), 1)
    block = lax.broadcasted_iota(jnp.int32, (blocks, length), 0)
    first = own * strip
    shift = halves.bit_length() - 1
    low = (block & (halves - 1)) * rows + (block >> shift) * BROWS + first
    inside = (place >= low) & (place < low + BROWS)
    lines = [
        jnp.sum(jnp.where(inside, table, 0.0), axis=0, keepdims=True) for table in (start, target)
    ]
    for out in outs:
        out[size:, :] = jnp.zeros((out.shape[0] - size, width), f32)
        out[size : size + BROWS, :] = spread
        for t, line in enumerate(lines):
            for k in range(table_lines):
                at = size + BROWS + t * table_lines + k
                used = min(width, length - k * width)
                out[at : at + 1, 0:used] = line[:, k * width : k * width + used]
        at = size + BROWS + 2 * table_lines
        out[at : at + 1, 0 : count_ref.shape[1]] = count_ref[...].astype(f32)


def cut_kernel(images_ref, out_ref):
    part = images_ref.shape[1] - out_ref.shape[1]
    for s in range(out_ref.shape[0]):
        out_ref[s] = images_ref[s, part:]


def taps_kernel(kernels_hbm, strength_hbm, line_ref, gain_ref, kernels_ref, strength_ref, sem):
    for copy in fetch(((kernels_hbm, kernels_ref), (strength_hbm, strength_ref)), sem):
        copy.wait()
    passes, bands, taps_count = kernels_ref.shape
    wide = line_ref.shape[2]
    pad = jnp.zeros((bands, LANES - taps_count), f32)
    mirror = lax.broadcasted_iota(jnp.int32, (LANES, LANES), 0) + lax.broadcasted_iota(
        jnp.int32, (LANES, LANES), 1
    )
    mirror = jnp.where(mirror == taps_count - 1, 1.0, 0.0).astype(f32)
    rest = jnp.zeros((bands, wide - LANES), f32)
    for p in range(passes):
        taps = kernels_ref[p]
        taps = taps / jnp.sum(taps, axis=1, keepdims=True)
        taps = jnp.concatenate([taps, pad], axis=1)
        strength = upright(strength_ref[p : p + 1, :])
        turned = jnp.dot(taps, mirror, precision=lax.Precision.HIGHEST)
        at = slice(p * bands, (p + 1) * bands)
        line_ref[0, at, :] = jnp.concatenate([taps * strength, rest], axis=1)
        line_ref[1, at, :] = jnp.concatenate([turned, rest], axis=1)
        gain_ref[at, :] = jnp.broadcast_to(1.0 + strength, (bands, gain_ref.shape[1]))


def banded(line, size, radius):
    wide = line.shape[1]
    spread = jnp.broadcast_to(line, (size, wide))
    return split(pltpu.roll(spread, wide - radius, 1, stride=1, stride_axis=0)[:, :size])


def corrections(state, line_ref, gain_ref, first, passes, bands, radius):
    part, rows, width = state.shape
    groups = [[i for i in range(part) if (first + i) % bands == slot] for slot in range(bands)]
    for step in range(passes):
        middle = {}
        for slot, group in enumerate(groups):
            if group:
                k = step * bands + slot
                rh, rl = banded(line_ref[0, k : k + 1, :], rows, radius)
                left = jnp.concatenate([rh, rh], axis=1)
            for i in group:
                xh, xl = split(state[i])
                both = mm(left, jnp.concatenate([xh, xl], axis=0))
                middle[i] = split(both + mm(rl, xh))
        for slot, group in enumerate(groups):
            if not group:
                continue
            k = step * bands + slot
            ch, cl = banded(line_ref[1, k : k + 1, :], width, radius)
            high = jnp.concatenate([middle[i][0] for i in group], axis=0)
            low = jnp.concatenate([middle[i][1] for i in group], axis=0)
            both = mm(jnp.concatenate([high, low], axis=0), ch)
            size = high.shape[0]
            blurred = both[:size] + both[size:] + mm(high, cl)
            gain = gain_ref[k : k + 1, :]
            for q, i in enumerate(group):
                state[i] = gain * state[i] - blurred[q * rows : (q + 1) * rows]


def laid_pairs(state, ah, al):
    part, _, width = state.shape
    map_rows = ah.shape[0]
    stacked = jnp.concatenate([ah, al], axis=0)
    for i in range(0, part, 2):
        pair = range(i, min(i + 2, part))
        z = jnp.concatenate(
            [
                jnp.concatenate(
                    [state[j, :, h : h + BCOLS] for h in range(0, width, BCOLS)], axis=0
                )
                for j in pair
            ],
            axis=1,
        )
        zh, zl = split(z)
        both = mm(stacked, zh)
        yield pair, both[:map_rows] + both[map_rows:] + mm(ah, zl)


def small_kernel(
    line_ref, gain_ref, *refs, spaces, cores, passes, bands, radius, share, table_lines
):
    x_refs, (*out_refs, ah_ref, al_ref, state, laid_ref) = refs[:spaces], refs[spaces:]
    part, rows, width = state.shape
    strip = rows // spaces
    tables = part * strip
    length = width // BCOLS * rows
    own = lax.axis_index("space")
    for d in range(spaces):
        at = pl.ds(pl.multiple_of((own ^ d) * strip, strip), strip)
        for i in range(part):
            state[i, at, :] = x_refs[d][i * strip : (i + 1) * strip, :]

    def table(t):
        lines = []
        for k in range(table_lines):
            at = tables + BROWS + t * table_lines + k
            used = min(width, length - k * width)
            lines.append(total(ref[at : at + 1, 0:used] for ref in x_refs))
        return jnp.concatenate(lines, axis=1)

    start, target = table(0), table(1)
    entries = jnp.zeros((BROWS, length), f32)
    for d in range(spaces):
        matrix = x_refs[d][tables : tables + BROWS, :]
        matrix = jnp.concatenate([matrix] * (length // width), axis=1)
        entries = jnp.where(target == (own ^ d).astype(f32), matrix, entries)
    line = lax.broadcasted_iota(jnp.int32, ah_ref.shape, 0)
    offset = line - start.astype(jnp.int32)
    placer = jnp.zeros(ah_ref.shape, f32)
    for i in range(BROWS):
        placer = jnp.where(offset == i, entries[i : i + 1, :], placer)
    ah, al = split(placer)
    ah_ref[...] = ah
    al_ref[...] = al
    corrections(state, line_ref, gain_ref, 0, passes, bands, radius)
    x, c = lax.axis_index("date"), lax.axis_index("band")
    groups = laid_ref.shape[0]
    for pair, laid in laid_pairs(state, ah, al):
        for m in range(groups):
            laid_ref[m, :, : laid.shape[1]] = laid[m * share : (m + 1) * share]
        for k, out in enumerate(out_refs):
            mine = (x ^ (k // cores)) * cores + (c ^ (k % cores))
            for g in range(spaces):
                lines = laid_ref[g * (groups // spaces) + mine]
                for p, j in enumerate(pair):
                    out[g, j * share : (j + 1) * share, :] = lines[
                        :, p * BCOLS : (p + 1) * BCOLS
                    ]
    at = tables + BROWS + 2 * table_lines
    counted = [ref[at : at + 1, 0:BCOLS] for ref in x_refs]
    for out in out_refs:
        out[0, part * share : part * share + 1, :] = counted[0]
        out[0, part * share + 1 : part * share + 2, :] = total(counted)


def large_kernel(
    x_ref, line_ref, gain_ref, ah_ref, al_ref, out_ref, state, *, first, passes, bands, radius
):
    spaces, part = x_ref.shape[:2]
    for i in range(part):
        state[i] = jnp.concatenate([x_ref[s, i] for s in range(spaces)], axis=0)
    corrections(state, line_ref, gain_ref, first, passes, bands, radius)
    share = out_ref.shape[1] // part
    for pair, laid in laid_pairs(state, ah_ref[...], al_ref[...]):
        for p, j in enumerate(pair):
            for d in range(out_ref.shape[0]):
                out_ref[d, j * share : (j + 1) * share, :] = laid[
                    d * share : (d + 1) * share, p * BCOLS : (p + 1) * BCOLS
                ]


def columns_of(block, kh, kl):
    bh, bl = split(block)
    both = mm(jnp.concatenate([bh, bl], axis=0), kh)
    size = block.shape[0]
    return both[:size] + both[size:] + mm(bh, kl)


def halve_kernel(cols_ref, kh_ref, kl_ref):
    kh_ref[...], kl_ref[...] = split(cols_ref[0])


def regroup_kernel(*refs, spaces):
    groups, size = refs[-2].shape[:2]
    own = lax.axis_index("space")
    for k in range(groups):
        for d in range(spaces):
            refs[groups + d][k] = refs[k][own ^ d, :size, :]
        refs[-1][k] = refs[k][0, size:, :]


def columns_kernel(
    kh_ref, kl_ref, count_ref, *refs, spaces, dates, cores, local_dates
):
    y_refs, (full_ref, weight_ref) = refs[:spaces], refs[spaces:]
    sides, part, share, width = full_ref.shape[1:]
    size = part * share
    kh, kl = kh_ref[...], kl_ref[...]
    for d in range(spaces):
        block = y_refs[d][...].reshape(sides * size, width)
        full_ref[d] = columns_of(block, kh, kl).reshape(sides, part, share, width)
    counted = total(count_ref[dx * cores, 1:2, :] for dx in range(dates))
    summed = jnp.sum(counted, axis=1, keepdims=True)
    mean_count = summed / f32(spaces * dates * local_dates)
    for dx in range(dates):
        own = count_ref[dx * cores, 0:1, :]
        weight = own / (own + mean_count)
        for t in range(local_dates):
            weight_ref[dx * local_dates + t] = jnp.broadcast_to(
                weight[:, t : t + 1], weight_ref.shape[1:]
            )


def median_kernel(
    weight_ref,
    kh_ref,
    kl_ref,
    small_ref,
    y_ref,
    *refs,
    spaces,
    dates,
    cores,
    bands,
    per,
    local_dates,
):
    out_refs, (large_ref, result) = refs[:cores], refs[cores:]
    share, width = small_ref.shape[3:]
    part = small_ref.shape[2]
    kh, kl = kh_ref[...], kl_ref[...]
    for s in range(y_ref.shape[0]):
        large_ref[s] = columns_of(y_ref[s], kh, kl).reshape(per - part, share, width)
    z, x, c = (lax.axis_index(a) for a in ("space", "date", "band"))
    across = max(1, bands // per)
    inside = max(1, per // bands)
    span = bands // across
    tile = weight_ref.shape[1]
    slots = [(dc, b) for dc in range(cores) for b in range(bands)]
    order = [
        (d, dx, t) for d in range(0, spaces, across) for dx in range(dates) for t in range(inside)
    ]
    for start in range(0, share, tile):
        rows = pl.ds(start, tile)

        def load(d, dx, t):
            values = []
            for dc, b in slots:
                far = d ^ (b // span)
                image = t * bands + b % span
                if image < part:
                    values.append(small_ref[far, dx * cores + dc, image, rows, :])
                else:
                    source = ((z ^ far) * dates + (x ^ dx)) * cores + (c ^ dc)
                    values.append(large_ref[source, image - part, rows, :])
            return values

        def weight(d, dx, t):
            return weight_ref[dx * local_dates + (z ^ d) // across * inside + t]

        number = [jnp.zeros((tile, width), f32)] * len(slots)
        below = jnp.zeros((tile, width), f32)
        for key in order:
            w = weight(*key)
            below = below + w
            number = [n + w * v for n, v in zip(number, load(*key))]
        estimate = [n / below for n in number]
        for _ in range(ITERS):
            number = [jnp.zeros((tile, width), f32)] * len(slots)
            below = jnp.zeros((tile, width), f32)
            for key in order:
                values = load(*key)
                squares = []
                for v, e in zip(values, estimate):
                    gap = v - e
                    squares.append(gap * gap)
                scaled = weight(*key) / jnp.sqrt(total(squares) + smooth_sq)
                below = below + scaled
                number = [n + scaled * v for n, v in zip(number, values)]
            estimate = [n / below for n in number]
        for (dc, b), value in zip(slots, estimate):
            if across == 1:
                out_refs[dc][b, rows, :] = value
            else:
                result[dc, ((z % across) ^ (b // span)) * span + b % span, rows, :] = value
    if across > 1:
        for dc in range(cores):
            out_refs[dc][...] = result[dc]


def place_kernel(*refs, dates, cores):
    out_ref = refs[-1]
    share = refs[0].shape[1]
    x, c = lax.axis_index("date"), lax.axis_index("band")
    for dx in range(dates):
        for dc in range(cores):
            j = (x ^ dx) * cores + (c ^ dc)
            at = pl.ds(pl.multiple_of(j * share, share), share)
            out_ref[:, at, :] = refs[dx * cores + dc][...]


def across_sides(pieces, dates, cores):
    received = [pieces[0]]
    for k in range(1, dates * cores):
        pairs = [
            (x * cores + c, (x ^ (k // cores)) * cores + (c ^ (k % cores)))
            for x in range(dates)
            for c in range(cores)
        ]
        received.append(lax.ppermute(pieces[k], ("date", "band"), pairs))
    return received


def local(
    reflect, kernels, strength, destinations, offsets, counts, resample_rows, resample_columns
):
    spaces, dates, cores = (lax.axis_size(a) for a in ("space", "date", "band"))
    local_dates, bands, strip, width = reflect.shape
    passes = kernels.shape[0]
    blocks = offsets.shape[0]
    rows = spaces * strip
    halves = width // BCOLS
    length = halves * rows
    table_lines = -(-length // width)
    tile_rows = blocks * BROWS
    sources = spaces * dates * cores
    share = tile_rows // (dates * cores)
    tile = min(share, SUBLANES)
    per = local_dates * bands // spaces
    part = max(1, per // 2)
    images = reflect.reshape(spaces, per, strip, width)
    pack = pl.pallas_call(
        functools.partial(pack_kernel, part=part, halves=halves, table_lines=table_lines),
        out_shape=[
            jax.ShapeDtypeStruct(
                (part * strip + round_up(BROWS + 2 * table_lines + 1, SUBLANES), width), f32
            )
        ]
        * spaces,
        in_specs=hbm(4) + vmem(1),
        out_specs=vmem(spaces),
        scratch_shapes=[
            pltpu.VMEM((1, blocks), jnp.int32),
            pltpu.VMEM((1, blocks), jnp.int32),
            pltpu.VMEM((1, BROWS, BROWS), f32),
            pltpu.VMEM((1, local_dates), jnp.int32),
            pltpu.SemaphoreType.DMA((4,)),
        ],
        compiler_params=params(4),
        name="pack",
    )
    small = list(
        pack(
            destinations.reshape(1, blocks),
            offsets.reshape(1, blocks),
            resample_rows,
            counts.reshape(1, local_dates),
            images,
        )
    )
    for d in range(spaces - 1, 0, -1):
        small[d] = lax.ppermute(small[d], "space", [(i, i ^ d) for i in range(spaces)])
    cut = pl.pallas_call(
        cut_kernel,
        out_shape=jax.ShapeDtypeStruct((spaces, per - part, strip, width), f32),
        in_specs=vmem(1),
        out_specs=pl.BlockSpec(memory_space=pltpu.VMEM),
        compiler_params=params(4),
        name="cut",
    )
    rest = cut(images)
    large = lax.all_to_all(rest, "space", split_axis=0, concat_axis=0, tiled=True)

    here = bands if per % bands == 0 else per
    if here != bands:
        first_band = (lax.axis_index("space") * per) % bands
        kernels = lax.dynamic_slice_in_dim(kernels, first_band, here, axis=1)
        strength = lax.dynamic_slice_in_dim(strength, first_band, here, axis=1)
    wide = max(rows, width) + LANES
    count = passes * here
    make_lines = pl.pallas_call(
        taps_kernel,
        out_shape=[
            jax.ShapeDtypeStruct((2, count, wide), f32),
            jax.ShapeDtypeStruct((count, width), f32),
        ],
        in_specs=hbm(2),
        out_specs=vmem(2),
        scratch_shapes=[
            pltpu.VMEM(kernels.shape, f32),
            pltpu.VMEM(strength.shape, f32),
            pltpu.SemaphoreType.DMA((2,)),
        ],
        compiler_params=params(4),
        name="taps",
    )
    lines, gains = make_lines(kernels, strength)

    settings = dict(passes=passes, bands=here, radius=kernels.shape[2] // 2)
    small_rows = part * share + SUBLANES
    correct_small = pl.pallas_call(
        functools.partial(
            small_kernel,
            spaces=spaces,
            cores=cores,
            share=share,
            table_lines=table_lines,
            **settings,
        ),
        out_shape=[jax.ShapeDtypeStruct((spaces, small_rows, BCOLS), f32)] * (dates * cores)
        + [jax.ShapeDtypeStruct((spaces * tile_rows, length), bf16)] * 2,
        in_specs=vmem(2 + spaces),
        out_specs=vmem(dates * cores + 2),
        scratch_shapes=[
            pltpu.VMEM((part, rows, width), f32),
            pltpu.VMEM((spaces * tile_rows // share, share, 2 * BCOLS), f32),
        ],
        compiler_params=params(20),
        name="correct0",
    )
    *sides, ah, al = correct_small(lines, gains, *small)
    sides = across_sides(sides, dates, cores)
    regroup = pl.pallas_call(
        functools.partial(regroup_kernel, spaces=spaces),
        out_shape=[jax.ShapeDtypeStruct((dates * cores, part * share, BCOLS), f32)] * spaces
        + [jax.ShapeDtypeStruct((dates * cores, SUBLANES, BCOLS), f32)],
        in_specs=vmem(dates * cores),
        out_specs=vmem(spaces + 1),
        compiler_params=params(4),
        name="regroup",
    )
    *small, counted = regroup(*sides)
    for d in range(spaces - 1, 0, -1):
        small[d] = lax.ppermute(small[d], "space", [(i, i ^ d) for i in range(spaces)])

    correct_large = pl.pallas_call(
        functools.partial(large_kernel, first=part, **settings),
        out_shape=jax.ShapeDtypeStruct((sources, (per - part) * share, BCOLS), f32),
        in_specs=vmem(5),
        out_specs=pl.BlockSpec(memory_space=pltpu.VMEM),
        scratch_shapes=[pltpu.VMEM((per - part, rows, width), f32)],
        compiler_params=params(20),
        name="correct1",
    )
    laid = correct_large(large, lines, gains, ah, al)
    pixels = lax.all_to_all(
        laid, ("space", "date", "band"), split_axis=0, concat_axis=0, tiled=True
    )

    halve = pl.pallas_call(
        halve_kernel,
        out_shape=[jax.ShapeDtypeStruct((BCOLS, BCOLS), bf16)] * 2,
        in_specs=vmem(1),
        out_specs=vmem(2),
        compiler_params=params(2),
        name="halve",
    )
    columns = halve(resample_columns)
    columns_call = pl.pallas_call(
        functools.partial(
            columns_kernel, spaces=spaces, dates=dates, cores=cores, local_dates=local_dates
        ),
        out_shape=[
            jax.ShapeDtypeStruct((spaces, dates * cores, part, share, BCOLS), f32),
            jax.ShapeDtypeStruct((dates * local_dates, tile, BCOLS), f32),
        ],
        in_specs=vmem(3 + spaces),
        out_specs=vmem(2),
        compiler_params=params(8),
        name="columns",
    )
    full, weights = columns_call(*columns, counted, *small)
    shares = pl.pallas_call(
        functools.partial(
            median_kernel,
            spaces=spaces,
            dates=dates,
            cores=cores,
            bands=bands,
            per=per,
            local_dates=local_dates,
        ),
        out_shape=[jax.ShapeDtypeStruct((bands, share, BCOLS), f32)] * cores,
        in_specs=vmem(5),
        out_specs=vmem(cores),
        scratch_shapes=[
            pltpu.VMEM((sources, per - part, share, BCOLS), f32),
            pltpu.VMEM((cores, bands, share, BCOLS), f32),
        ],
        compiler_params=params(12),
        name="median",
    )(weights, *columns, full, pixels)

    pieces = across_sides([shares[k % cores] for k in range(dates * cores)], dates, cores)
    return pl.pallas_call(
        functools.partial(place_kernel, dates=dates, cores=cores),
        out_shape=jax.ShapeDtypeStruct((bands, tile_rows, BCOLS), f32),
        in_specs=vmem(dates * cores),
        out_specs=pl.BlockSpec(memory_space=pltpu.VMEM),
        compiler_params=params(4),
        name="place",
    )(*pieces)


def solution(mesh):
    in_specs = (
        P("date", "band", ("groups", "space"), None),
        P(None, "band", None),
        P(None, "band"),
        P(("groups", "space"), None),
        P(("groups", "space")),
        P("date", ("groups", "space")),
        P(("groups", "space"), None, None),
        P(("groups", "space"), None, None),
    )
    out_specs = P("band", ("groups", "space"), None)

    return jax.shard_map(local, mesh=mesh, in_specs=in_specs, out_specs=out_specs, check_vma=False)
```

```python
import functools

import jax
import jax.numpy as jnp
from jax import lax
from jax.experimental import pallas as pl
from jax.experimental.pallas import tpu as pltpu
from jax.sharding import PartitionSpec as P


BROWS = 4
BCOLS = 128
ITERS = 4
LANES = 128
SUBLANES = 8


smooth_sq = 0.01
f32 = jnp.float32
bf16 = jnp.bfloat16


def split(x):
    high = x.astype(bf16)
    return high, (x - high.astype(f32)).astype(bf16)


def mm(a, b):
    return jnp.dot(a, b, preferred_element_type=f32)


def total(terms):
    terms = list(terms)
    while len(terms) > 1:
        terms = [a + b for a, b in zip(terms[::2], terms[1::2])] + terms[len(terms) & ~1 :]
    return terms[0]


def round_up(value, unit):
    return -(-value // unit) * unit


def vmem(count):
    return [pl.BlockSpec(memory_space=pltpu.VMEM)] * count


def hbm(count):
    return [pl.BlockSpec(memory_space=pltpu.HBM)] * count


def fetch(pairs, sem):
    copies = [pltpu.make_async_copy(src, dst, sem.at[k]) for k, (src, dst) in enumerate(pairs)]
    for copy in copies:
        copy.start()
    return copies


def params(mib):
    return pltpu.CompilerParams(vmem_limit_bytes=mib << 20)


def upright(line):
    size = line.shape[1]
    eye = lax.broadcasted_iota(jnp.int32, (size, size), 0) == lax.broadcasted_iota(
        jnp.int32, (size, size), 1
    )
    spread = jnp.broadcast_to(line, (size, size))
    return jnp.sum(jnp.where(eye, spread, 0.0), axis=1, keepdims=True)


def pack_kernel(
    target_hbm,
    start_hbm,
    rows_hbm,
    count_hbm,
    images_ref,
    *refs,
    part,
    halves,
    table_lines,
):
    spaces, _, strip, width = images_ref.shape
    outs, (target_ref, start_ref, rows_ref, count_ref, sem) = refs[:spaces], refs[spaces:]
    tables = fetch(
        zip(
            (target_hbm, start_hbm, rows_hbm, count_hbm),
            (target_ref, start_ref, rows_ref, count_ref),
        ),
        sem,
    )
    own = lax.axis_index("space")
    size = part * strip
    for d in range(spaces):
        outs[d][:size, :] = images_ref[own ^ d, 0:part].reshape(size, width)
    for table in tables:
        table.wait()
    blocks = target_ref.shape[1]
    rows = spaces * strip
    matrix = rows_ref[0]
    lane = lax.broadcasted_iota(jnp.int32, (BROWS, width), 1) & (BROWS - 1)
    spread = jnp.zeros((BROWS, width), f32)
    for k in range(BROWS):
        spread = jnp.where(lane == k, jnp.broadcast_to(matrix[:, k : k + 1], spread.shape), spread)
    target = upright(target_ref[...].astype(f32))
    start = target * f32(blocks * BROWS) + upright(start_ref[...].astype(f32))
    length = halves * rows
    place = lax.broadcasted_iota(jnp.int32, (blocks, length), 1)
    block = lax.broadcasted_iota(jnp.int32, (blocks, length), 0)
    first = own * strip
    shift = halves.bit_length() - 1
    low = (block & (halves - 1)) * rows + (block >> shift) * BROWS + first
    inside = (place >= low) & (place < low + BROWS)
    lines = [
        jnp.sum(jnp.where(inside, table, 0.0), axis=0, keepdims=True) for table in (start, target)
    ]
    for out in outs:
        out[size:, :] = jnp.zeros((out.shape[0] - size, width), f32)
        out[size : size + BROWS, :] = spread
        for t, line in enumerate(lines):
            for k in range(table_lines):
                at = size + BROWS + t * table_lines + k
                used = min(width, length - k * width)
                out[at : at + 1, 0:used] = line[:, k * width : k * width + used]
        at = size + BROWS + 2 * table_lines
        out[at : at + 1, 0 : count_ref.shape[1]] = count_ref[...].astype(f32)


def cut_kernel(images_ref, out_ref):
    part = images_ref.shape[1] - out_ref.shape[1]
    for s in range(out_ref.shape[0]):
        out_ref[s] = images_ref[s, part:]


def taps_kernel(kernels_hbm, strength_hbm, line_ref, gain_ref, kernels_ref, strength_ref, sem):
    for copy in fetch(((kernels_hbm, kernels_ref), (strength_hbm, strength_ref)), sem):
        copy.wait()
    passes, bands, taps_count = kernels_ref.shape
    wide = line_ref.shape[2]
    pad = jnp.zeros((bands, LANES - taps_count), f32)
    mirror = lax.broadcasted_iota(jnp.int32, (LANES, LANES), 0) + lax.broadcasted_iota(
        jnp.int32, (LANES, LANES), 1
    )
    mirror = jnp.where(mirror == taps_count - 1, 1.0, 0.0).astype(f32)
    rest = jnp.zeros((bands, wide - LANES), f32)
    for p in range(passes):
        taps = kernels_ref[p]
        taps = taps / jnp.sum(taps, axis=1, keepdims=True)
        taps = jnp.concatenate([taps, pad], axis=1)
        strength = upright(strength_ref[p : p + 1, :])
        turned = jnp.dot(taps, mirror, precision=lax.Precision.HIGHEST)
        at = slice(p * bands, (p + 1) * bands)
        line_ref[0, at, :] = jnp.concatenate([taps * strength, rest], axis=1)
        line_ref[1, at, :] = jnp.concatenate([turned, rest], axis=1)
        gain_ref[at, :] = jnp.broadcast_to(1.0 + strength, (bands, gain_ref.shape[1]))


def banded(line, size, radius):
    wide = line.shape[1]
    spread = jnp.broadcast_to(line, (size, wide))
    return split(pltpu.roll(spread, wide - radius, 1, stride=1, stride_axis=0)[:, :size])


def corrections(state, line_ref, gain_ref, first, passes, bands, radius):
    part, rows, width = state.shape
    groups = [[i for i in range(part) if (first + i) % bands == slot] for slot in range(bands)]
    for step in range(passes):
        middle = {}
        for slot, group in enumerate(groups):
            if group:
                k = step * bands + slot
                rh, rl = banded(line_ref[0, k : k + 1, :], rows, radius)
                left = jnp.concatenate([rh, rh], axis=1)
            for i in group:
                xh, xl = split(state[i])
                both = mm(left, jnp.concatenate([xh, xl], axis=0))
                middle[i] = split(both + mm(rl, xh))
        for slot, group in enumerate(groups):
            if not group:
                continue
            k = step * bands + slot
            ch, cl = banded(line_ref[1, k : k + 1, :], width, radius)
            high = jnp.concatenate([middle[i][0] for i in group], axis=0)
            low = jnp.concatenate([middle[i][1] for i in group], axis=0)
            both = mm(jnp.concatenate([high, low], axis=0), ch)
            size = high.shape[0]
            blurred = both[:size] + both[size:] + mm(high, cl)
            gain = gain_ref[k : k + 1, :]
            for q, i in enumerate(group):
                state[i] = gain * state[i] - blurred[q * rows : (q + 1) * rows]


def laid_pairs(state, ah, al):
    part, _, width = state.shape
    map_rows = ah.shape[0]
    stacked = jnp.concatenate([ah, al], axis=0)
    for i in range(0, part, 2):
        pair = range(i, min(i + 2, part))
        z = jnp.concatenate(
            [
                jnp.concatenate(
                    [state[j, :, h : h + BCOLS] for h in range(0, width, BCOLS)], axis=0
                )
                for j in pair
            ],
            axis=1,
        )
        zh, zl = split(z)
        both = mm(stacked, zh)
        yield pair, both[:map_rows] + both[map_rows:] + mm(ah, zl)


def small_kernel(
    line_ref, gain_ref, *refs, spaces, cores, passes, bands, radius, share, table_lines
):
    x_refs, (*out_refs, ah_ref, al_ref, state, laid_ref) = refs[:spaces], refs[spaces:]
    part, rows, width = state.shape
    strip = rows // spaces
    tables = part * strip
    length = width // BCOLS * rows
    own = lax.axis_index("space")
    for d in range(spaces):
        at = pl.ds(pl.multiple_of((own ^ d) * strip, strip), strip)
        for i in range(part):
            state[i, at, :] = x_refs[d][i * strip : (i + 1) * strip, :]

    def table(t):
        lines = []
        for k in range(table_lines):
            at = tables + BROWS + t * table_lines + k
            used = min(width, length - k * width)
            lines.append(total(ref[at : at + 1, 0:used] for ref in x_refs))
        return jnp.concatenate(lines, axis=1)

    start, target = table(0), table(1)
    entries = jnp.zeros((BROWS, length), f32)
    for d in range(spaces):
        matrix = x_refs[d][tables : tables + BROWS, :]
        matrix = jnp.concatenate([matrix] * (length // width), axis=1)
        entries = jnp.where(target == (own ^ d).astype(f32), matrix, entries)
    line = lax.broadcasted_iota(jnp.int32, ah_ref.shape, 0)
    offset = line - start.astype(jnp.int32)
    placer = jnp.zeros(ah_ref.shape, f32)
    for i in range(BROWS):
        placer = jnp.where(offset == i, entries[i : i + 1, :], placer)
    ah, al = split(placer)
    ah_ref[...] = ah
    al_ref[...] = al
    corrections(state, line_ref, gain_ref, 0, passes, bands, radius)
    x, c = lax.axis_index("date"), lax.axis_index("band")
    groups = laid_ref.shape[0]
    for pair, laid in laid_pairs(state, ah, al):
        for m in range(groups):
            laid_ref[m, :, : laid.shape[1]] = laid[m * share : (m + 1) * share]
        for k, out in enumerate(out_refs):
            mine = (x ^ (k // cores)) * cores + (c ^ (k % cores))
            for g in range(spaces):
                lines = laid_ref[g * (groups // spaces) + mine]
                for p, j in enumerate(pair):
                    out[g, j * share : (j + 1) * share, :] = lines[
                        :, p * BCOLS : (p + 1) * BCOLS
                    ]
    at = tables + BROWS + 2 * table_lines
    counted = [ref[at : at + 1, 0:BCOLS] for ref in x_refs]
    for out in out_refs:
        out[0, part * share : part * share + 1, :] = counted[0]
        out[0, part * share + 1 : part * share + 2, :] = total(counted)


def large_kernel(
    x_ref, line_ref, gain_ref, ah_ref, al_ref, out_ref, state, piece, sem, *, first, passes, bands, radius
):
    spaces, part = x_ref.shape[:2]
    for i in range(part):
        state[i] = jnp.concatenate([x_ref[s, i] for s in range(spaces)], axis=0)
    corrections(state, line_ref, gain_ref, first, passes, bands, radius)
    share = out_ref.shape[1] // part
    copies = []
    for pair, laid in laid_pairs(state, ah_ref[...], al_ref[...]):
        for p, j in enumerate(pair):
            for d in range(out_ref.shape[0]):
                piece[d, j * share : (j + 1) * share, :] = laid[
                    d * share : (d + 1) * share, p * BCOLS : (p + 1) * BCOLS
                ]
        at = slice(pair[0] * share, (pair[-1] + 1) * share)
        copies.append(
            pltpu.make_async_copy(piece.at[:, at], out_ref.at[:, at], sem.at[len(copies)])
        )
        copies[-1].start()
    for copy in copies:
        copy.wait()


def columns_of(block, kh, kl):
    bh, bl = split(block)
    both = mm(jnp.concatenate([bh, bl], axis=0), kh)
    size = block.shape[0]
    return both[:size] + both[size:] + mm(bh, kl)


def halve_kernel(cols_ref, kh_ref, kl_ref):
    kh_ref[...], kl_ref[...] = split(cols_ref[0])


def regroup_kernel(*refs, spaces):
    groups, size = refs[-2].shape[:2]
    own = lax.axis_index("space")
    for k in range(groups):
        for d in range(spaces):
            refs[groups + d][k] = refs[k][own ^ d, :size, :]
        refs[-1][k] = refs[k][0, size:, :]


def columns_kernel(
    kh_ref, kl_ref, count_ref, *refs, spaces, dates, cores, local_dates
):
    y_refs, (full_ref, weight_ref) = refs[:spaces], refs[spaces:]
    sides, part, share, width = full_ref.shape[1:]
    size = part * share
    kh, kl = kh_ref[...], kl_ref[...]
    for d in range(spaces):
        block = y_refs[d][...].reshape(sides * size, width)
        full_ref[d] = columns_of(block, kh, kl).reshape(sides, part, share, width)
    counted = total(count_ref[dx * cores, 1:2, :] for dx in range(dates))
    summed = jnp.sum(counted, axis=1, keepdims=True)
    mean_count = summed / f32(spaces * dates * local_dates)
    for dx in range(dates):
        own = count_ref[dx * cores, 0:1, :]
        weight = own / (own + mean_count)
        for t in range(local_dates):
            weight_ref[dx * local_dates + t] = jnp.broadcast_to(
                weight[:, t : t + 1], weight_ref.shape[1:]
            )


def median_kernel(
    weight_ref,
    kh_ref,
    kl_ref,
    small_ref,
    y_ref,
    *refs,
    spaces,
    dates,
    cores,
    bands,
    per,
    local_dates,
):
    out_refs, (large_ref, result) = refs[:cores], refs[cores:]
    share, width = small_ref.shape[3:]
    part = small_ref.shape[2]
    kh, kl = kh_ref[...], kl_ref[...]
    for s in range(y_ref.shape[0]):
        large_ref[s] = columns_of(y_ref[s], kh, kl).reshape(per - part, share, width)
    z, x, c = (lax.axis_index(a) for a in ("space", "date", "band"))
    across = max(1, bands // per)
    inside = max(1, per // bands)
    span = bands // across
    tile = weight_ref.shape[1]
    slots = [(dc, b) for dc in range(cores) for b in range(bands)]
    order = [
        (d, dx, t) for d in range(0, spaces, across) for dx in range(dates) for t in range(inside)
    ]
    for start in range(0, share, tile):
        rows = pl.ds(start, tile)

        def load(d, dx, t):
            values = []
            for dc, b in slots:
                far = d ^ (b // span)
                image = t * bands + b % span
                if image < part:
                    values.append(small_ref[far, dx * cores + dc, image, rows, :])
                else:
                    source = ((z ^ far) * dates + (x ^ dx)) * cores + (c ^ dc)
                    values.append(large_ref[source, image - part, rows, :])
            return values

        def weight(d, dx, t):
            return weight_ref[dx * local_dates + (z ^ d) // across * inside + t]

        number = [jnp.zeros((tile, width), f32)] * len(slots)
        below = jnp.zeros((tile, width), f32)
        for key in order:
            w = weight(*key)
            below = below + w
            number = [n + w * v for n, v in zip(number, load(*key))]
        estimate = [n / below for n in number]
        for _ in range(ITERS):
            number = [jnp.zeros((tile, width), f32)] * len(slots)
            below = jnp.zeros((tile, width), f32)
            for key in order:
                values = load(*key)
                squares = []
                for v, e in zip(values, estimate):
                    gap = v - e
                    squares.append(gap * gap)
                scaled = weight(*key) / jnp.sqrt(total(squares) + smooth_sq)
                below = below + scaled
                number = [n + scaled * v for n, v in zip(number, values)]
            estimate = [n / below for n in number]
        for (dc, b), value in zip(slots, estimate):
            if across == 1:
                out_refs[dc][b, rows, :] = value
            else:
                result[dc, ((z % across) ^ (b // span)) * span + b % span, rows, :] = value
    if across > 1:
        for dc in range(cores):
            out_refs[dc][...] = result[dc]


def place_kernel(*refs, dates, cores):
    out_ref = refs[-1]
    share = refs[0].shape[1]
    x, c = lax.axis_index("date"), lax.axis_index("band")
    for dx in range(dates):
        for dc in range(cores):
            j = (x ^ dx) * cores + (c ^ dc)
            at = pl.ds(pl.multiple_of(j * share, share), share)
            out_ref[:, at, :] = refs[dx * cores + dc][...]


def across_sides(pieces, dates, cores):
    received = [pieces[0]]
    for k in range(1, dates * cores):
        pairs = [
            (x * cores + c, (x ^ (k // cores)) * cores + (c ^ (k % cores)))
            for x in range(dates)
            for c in range(cores)
        ]
        received.append(lax.ppermute(pieces[k], ("date", "band"), pairs))
    return received


def local(
    reflect, kernels, strength, destinations, offsets, counts, resample_rows, resample_columns
):
    spaces, dates, cores = (lax.axis_size(a) for a in ("space", "date", "band"))
    local_dates, bands, strip, width = reflect.shape
    passes = kernels.shape[0]
    blocks = offsets.shape[0]
    rows = spaces * strip
    halves = width // BCOLS
    length = halves * rows
    table_lines = -(-length // width)
    tile_rows = blocks * BROWS
    sources = spaces * dates * cores
    share = tile_rows // (dates * cores)
    tile = min(share, SUBLANES)
    per = local_dates * bands // spaces
    part = max(1, per // 2)
    images = reflect.reshape(spaces, per, strip, width)
    pack = pl.pallas_call(
        functools.partial(pack_kernel, part=part, halves=halves, table_lines=table_lines),
        out_shape=[
            jax.ShapeDtypeStruct(
                (part * strip + round_up(BROWS + 2 * table_lines + 1, SUBLANES), width), f32
            )
        ]
        * spaces,
        in_specs=hbm(4) + vmem(1),
        out_specs=vmem(spaces),
        scratch_shapes=[
            pltpu.VMEM((1, blocks), jnp.int32),
            pltpu.VMEM((1, blocks), jnp.int32),
            pltpu.VMEM((1, BROWS, BROWS), f32),
            pltpu.VMEM((1, local_dates), jnp.int32),
            pltpu.SemaphoreType.DMA((4,)),
        ],
        compiler_params=params(4),
        name="pack",
    )
    small = list(
        pack(
            destinations.reshape(1, blocks),
            offsets.reshape(1, blocks),
            resample_rows,
            counts.reshape(1, local_dates),
            images,
        )
    )
    for d in range(spaces - 1, 0, -1):
        small[d] = lax.ppermute(small[d], "space", [(i, i ^ d) for i in range(spaces)])
    cut = pl.pallas_call(
        cut_kernel,
        out_shape=jax.ShapeDtypeStruct((spaces, per - part, strip, width), f32),
        in_specs=vmem(1),
        out_specs=pl.BlockSpec(memory_space=pltpu.VMEM),
        compiler_params=params(4),
        name="cut",
    )
    rest = cut(images)
    large = lax.all_to_all(rest, "space", split_axis=0, concat_axis=0, tiled=True)

    here = bands if per % bands == 0 else per
    if here != bands:
        first_band = (lax.axis_index("space") * per) % bands
        kernels = lax.dynamic_slice_in_dim(kernels, first_band, here, axis=1)
        strength = lax.dynamic_slice_in_dim(strength, first_band, here, axis=1)
    wide = max(rows, width) + LANES
    count = passes * here
    make_lines = pl.pallas_call(
        taps_kernel,
        out_shape=[
            jax.ShapeDtypeStruct((2, count, wide), f32),
            jax.ShapeDtypeStruct((count, width), f32),
        ],
        in_specs=hbm(2),
        out_specs=vmem(2),
        scratch_shapes=[
            pltpu.VMEM(kernels.shape, f32),
            pltpu.VMEM(strength.shape, f32),
            pltpu.SemaphoreType.DMA((2,)),
        ],
        compiler_params=params(4),
        name="taps",
    )
    lines, gains = make_lines(kernels, strength)

    settings = dict(passes=passes, bands=here, radius=kernels.shape[2] // 2)
    small_rows = part * share + SUBLANES
    correct_small = pl.pallas_call(
        functools.partial(
            small_kernel,
            spaces=spaces,
            cores=cores,
            share=share,
            table_lines=table_lines,
            **settings,
        ),
        out_shape=[jax.ShapeDtypeStruct((spaces, small_rows, BCOLS), f32)] * (dates * cores)
        + [jax.ShapeDtypeStruct((spaces * tile_rows, length), bf16)] * 2,
        in_specs=vmem(2 + spaces),
        out_specs=vmem(dates * cores + 2),
        scratch_shapes=[
            pltpu.VMEM((part, rows, width), f32),
            pltpu.VMEM((spaces * tile_rows // share, share, 2 * BCOLS), f32),
        ],
        compiler_params=params(20),
        name="correct0",
    )
    *sides, ah, al = correct_small(lines, gains, *small)
    sides = across_sides(sides, dates, cores)
    regroup = pl.pallas_call(
        functools.partial(regroup_kernel, spaces=spaces),
        out_shape=[jax.ShapeDtypeStruct((dates * cores, part * share, BCOLS), f32)] * spaces
        + [jax.ShapeDtypeStruct((dates * cores, SUBLANES, BCOLS), f32)],
        in_specs=vmem(dates * cores),
        out_specs=vmem(spaces + 1),
        compiler_params=params(4),
        name="regroup",
    )
    *small, counted = regroup(*sides)
    for d in range(spaces - 1, 0, -1):
        small[d] = lax.ppermute(small[d], "space", [(i, i ^ d) for i in range(spaces)])

    correct_large = pl.pallas_call(
        functools.partial(large_kernel, first=part, **settings),
        out_shape=jax.ShapeDtypeStruct((sources, (per - part) * share, BCOLS), f32),
        in_specs=vmem(5),
        out_specs=pl.BlockSpec(memory_space=pltpu.HBM),
        scratch_shapes=[
            pltpu.VMEM((per - part, rows, width), f32),
            pltpu.VMEM((sources, (per - part) * share, BCOLS), f32),
            pltpu.SemaphoreType.DMA((per - part,)),
        ],
        compiler_params=params(20),
        name="correct1",
    )
    laid = correct_large(large, lines, gains, ah, al)
    pixels = lax.all_to_all(
        laid, ("space", "date", "band"), split_axis=0, concat_axis=0, tiled=True
    )

    halve = pl.pallas_call(
        halve_kernel,
        out_shape=[jax.ShapeDtypeStruct((BCOLS, BCOLS), bf16)] * 2,
        in_specs=vmem(1),
        out_specs=vmem(2),
        compiler_params=params(2),
        name="halve",
    )
    columns = halve(resample_columns)
    columns_call = pl.pallas_call(
        functools.partial(
            columns_kernel, spaces=spaces, dates=dates, cores=cores, local_dates=local_dates
        ),
        out_shape=[
            jax.ShapeDtypeStruct((spaces, dates * cores, part, share, BCOLS), f32),
            jax.ShapeDtypeStruct((dates * local_dates, tile, BCOLS), f32),
        ],
        in_specs=vmem(3 + spaces),
        out_specs=vmem(2),
        compiler_params=params(8),
        name="columns",
    )
    full, weights = columns_call(*columns, counted, *small)
    shares = pl.pallas_call(
        functools.partial(
            median_kernel,
            spaces=spaces,
            dates=dates,
            cores=cores,
            bands=bands,
            per=per,
            local_dates=local_dates,
        ),
        out_shape=[jax.ShapeDtypeStruct((bands, share, BCOLS), f32)] * cores,
        in_specs=vmem(5),
        out_specs=vmem(cores),
        scratch_shapes=[
            pltpu.VMEM((sources, per - part, share, BCOLS), f32),
            pltpu.VMEM((cores, bands, share, BCOLS), f32),
        ],
        compiler_params=params(12),
        name="median",
    )(weights, *columns, full, pixels)

    pieces = across_sides([shares[k % cores] for k in range(dates * cores)], dates, cores)
    return pl.pallas_call(
        functools.partial(place_kernel, dates=dates, cores=cores),
        out_shape=jax.ShapeDtypeStruct((bands, tile_rows, BCOLS), f32),
        in_specs=vmem(dates * cores),
        out_specs=pl.BlockSpec(memory_space=pltpu.VMEM),
        compiler_params=params(4),
        name="place",
    )(*pieces)


def solution(mesh):
    in_specs = (
        P("date", "band", ("groups", "space"), None),
        P(None, "band", None),
        P(None, "band"),
        P(("groups", "space"), None),
        P(("groups", "space")),
        P("date", ("groups", "space")),
        P(("groups", "space"), None, None),
        P(("groups", "space"), None, None),
    )
    out_specs = P("band", ("groups", "space"), None)

    return jax.shard_map(local, mesh=mesh, in_specs=in_specs, out_specs=out_specs, check_vma=False)
```

```python
import functools

import jax
import jax.numpy as jnp
from jax import lax
from jax.experimental import pallas as pl
from jax.experimental.pallas import tpu as pltpu
from jax.sharding import PartitionSpec as P


BROWS = 4
BCOLS = 128
ITERS = 4
LANES = 128
SUBLANES = 8


smooth_sq = 0.01
f32 = jnp.float32
bf16 = jnp.bfloat16


def split(x):
    high = x.astype(bf16)
    return high, (x - high.astype(f32)).astype(bf16)


def mm(a, b):
    return jnp.dot(a, b, preferred_element_type=f32)


def total(terms):
    terms = list(terms)
    while len(terms) > 1:
        terms = [a + b for a, b in zip(terms[::2], terms[1::2])] + terms[len(terms) & ~1 :]
    return terms[0]


def round_up(value, unit):
    return -(-value // unit) * unit


def vmem(count):
    return [pl.BlockSpec(memory_space=pltpu.VMEM)] * count


def hbm(count):
    return [pl.BlockSpec(memory_space=pltpu.HBM)] * count


def fetch(pairs, sem):
    copies = [pltpu.make_async_copy(src, dst, sem.at[k]) for k, (src, dst) in enumerate(pairs)]
    for copy in copies:
        copy.start()
    return copies


def params(mib):
    return pltpu.CompilerParams(vmem_limit_bytes=mib << 20)


def upright(line):
    size = line.shape[1]
    eye = lax.broadcasted_iota(jnp.int32, (size, size), 0) == lax.broadcasted_iota(
        jnp.int32, (size, size), 1
    )
    spread = jnp.broadcast_to(line, (size, size))
    return jnp.sum(jnp.where(eye, spread, 0.0), axis=1, keepdims=True)


def pack_kernel(
    target_hbm,
    start_hbm,
    rows_hbm,
    count_hbm,
    images_ref,
    *refs,
    part,
    halves,
    table_lines,
):
    spaces, _, strip, width = images_ref.shape
    outs, (target_ref, start_ref, rows_ref, count_ref, sem) = refs[:spaces], refs[spaces:]
    tables = fetch(
        zip(
            (target_hbm, start_hbm, rows_hbm, count_hbm),
            (target_ref, start_ref, rows_ref, count_ref),
        ),
        sem,
    )
    own = lax.axis_index("space")
    size = part * strip
    for d in range(spaces):
        outs[d][:size, :] = images_ref[own ^ d, 0:part].reshape(size, width)
    for table in tables:
        table.wait()
    blocks = target_ref.shape[1]
    rows = spaces * strip
    matrix = rows_ref[0]
    lane = lax.broadcasted_iota(jnp.int32, (BROWS, width), 1) & (BROWS - 1)
    spread = jnp.zeros((BROWS, width), f32)
    for k in range(BROWS):
        spread = jnp.where(lane == k, jnp.broadcast_to(matrix[:, k : k + 1], spread.shape), spread)
    target = upright(target_ref[...].astype(f32))
    start = target * f32(blocks * BROWS) + upright(start_ref[...].astype(f32))
    length = halves * rows
    place = lax.broadcasted_iota(jnp.int32, (blocks, length), 1)
    block = lax.broadcasted_iota(jnp.int32, (blocks, length), 0)
    first = own * strip
    shift = halves.bit_length() - 1
    low = (block & (halves - 1)) * rows + (block >> shift) * BROWS + first
    inside = (place >= low) & (place < low + BROWS)
    lines = [
        jnp.sum(jnp.where(inside, table, 0.0), axis=0, keepdims=True) for table in (start, target)
    ]
    for out in outs:
        out[size:, :] = jnp.zeros((out.shape[0] - size, width), f32)
        out[size : size + BROWS, :] = spread
        for t, line in enumerate(lines):
            for k in range(table_lines):
                at = size + BROWS + t * table_lines + k
                used = min(width, length - k * width)
                out[at : at + 1, 0:used] = line[:, k * width : k * width + used]
        at = size + BROWS + 2 * table_lines
        out[at : at + 1, 0 : count_ref.shape[1]] = count_ref[...].astype(f32)


def cut_kernel(images_ref, out_ref):
    part = images_ref.shape[1] - out_ref.shape[1]
    for s in range(out_ref.shape[0]):
        out_ref[s] = images_ref[s, part:]


def taps_kernel(kernels_hbm, strength_hbm, line_ref, gain_ref, kernels_ref, strength_ref, sem):
    for copy in fetch(((kernels_hbm, kernels_ref), (strength_hbm, strength_ref)), sem):
        copy.wait()
    passes, bands, taps_count = kernels_ref.shape
    wide = line_ref.shape[2]
    pad = jnp.zeros((bands, LANES - taps_count), f32)
    mirror = lax.broadcasted_iota(jnp.int32, (LANES, LANES), 0) + lax.broadcasted_iota(
        jnp.int32, (LANES, LANES), 1
    )
    mirror = jnp.where(mirror == taps_count - 1, 1.0, 0.0).astype(f32)
    rest = jnp.zeros((bands, wide - LANES), f32)
    for p in range(passes):
        taps = kernels_ref[p]
        taps = taps / jnp.sum(taps, axis=1, keepdims=True)
        taps = jnp.concatenate([taps, pad], axis=1)
        strength = upright(strength_ref[p : p + 1, :])
        turned = jnp.dot(taps, mirror, precision=lax.Precision.HIGHEST)
        at = slice(p * bands, (p + 1) * bands)
        line_ref[0, at, :] = jnp.concatenate([taps * strength, rest], axis=1)
        line_ref[1, at, :] = jnp.concatenate([turned, rest], axis=1)
        gain_ref[at, :] = jnp.broadcast_to(1.0 + strength, (bands, gain_ref.shape[1]))


def banded(line, size, radius):
    wide = line.shape[1]
    spread = jnp.broadcast_to(line, (size, wide))
    return split(pltpu.roll(spread, wide - radius, 1, stride=1, stride_axis=0)[:, :size])


def corrections(state, line_ref, gain_ref, first, passes, bands, radius):
    part, rows, width = state.shape
    groups = [[i for i in range(part) if (first + i) % bands == slot] for slot in range(bands)]
    for step in range(passes):
        middle = {}
        for slot, group in enumerate(groups):
            if group:
                k = step * bands + slot
                rh, rl = banded(line_ref[0, k : k + 1, :], rows, radius)
                left = jnp.concatenate([rh, rh], axis=1)
            for i in group:
                xh, xl = split(state[i])
                both = mm(left, jnp.concatenate([xh, xl], axis=0))
                middle[i] = split(both + mm(rl, xh))
        for slot, group in enumerate(groups):
            if not group:
                continue
            k = step * bands + slot
            ch, cl = banded(line_ref[1, k : k + 1, :], width, radius)
            high = jnp.concatenate([middle[i][0] for i in group], axis=0)
            low = jnp.concatenate([middle[i][1] for i in group], axis=0)
            both = mm(jnp.concatenate([high, low], axis=0), ch)
            size = high.shape[0]
            blurred = both[:size] + both[size:] + mm(high, cl)
            gain = gain_ref[k : k + 1, :]
            for q, i in enumerate(group):
                state[i] = gain * state[i] - blurred[q * rows : (q + 1) * rows]


def laid_pairs(state, ah, al):
    part, _, width = state.shape
    map_rows = ah.shape[0]
    stacked = jnp.concatenate([ah, al], axis=0)
    for i in range(0, part, 2):
        pair = range(i, min(i + 2, part))
        z = jnp.concatenate(
            [
                jnp.concatenate(
                    [state[j, :, h : h + BCOLS] for h in range(0, width, BCOLS)], axis=0
                )
                for j in pair
            ],
            axis=1,
        )
        zh, zl = split(z)
        both = mm(stacked, zh)
        yield pair, both[:map_rows] + both[map_rows:] + mm(ah, zl)


def small_kernel(
    line_ref, gain_ref, *refs, spaces, cores, passes, bands, radius, share, table_lines
):
    x_refs, (*out_refs, ah_ref, al_ref, state, laid_ref) = refs[:spaces], refs[spaces:]
    part, rows, width = state.shape
    strip = rows // spaces
    tables = part * strip
    length = width // BCOLS * rows
    own = lax.axis_index("space")
    for d in range(spaces):
        at = pl.ds(pl.multiple_of((own ^ d) * strip, strip), strip)
        for i in range(part):
            state[i, at, :] = x_refs[d][i * strip : (i + 1) * strip, :]

    def table(t):
        lines = []
        for k in range(table_lines):
            at = tables + BROWS + t * table_lines + k
            used = min(width, length - k * width)
            lines.append(total(ref[at : at + 1, 0:used] for ref in x_refs))
        return jnp.concatenate(lines, axis=1)

    start, target = table(0), table(1)
    entries = jnp.zeros((BROWS, length), f32)
    for d in range(spaces):
        matrix = x_refs[d][tables : tables + BROWS, :]
        matrix = jnp.concatenate([matrix] * (length // width), axis=1)
        entries = jnp.where(target == (own ^ d).astype(f32), matrix, entries)
    line = lax.broadcasted_iota(jnp.int32, ah_ref.shape, 0)
    offset = line - start.astype(jnp.int32)
    placer = jnp.zeros(ah_ref.shape, f32)
    for i in range(BROWS):
        placer = jnp.where(offset == i, entries[i : i + 1, :], placer)
    ah, al = split(placer)
    ah_ref[...] = ah
    al_ref[...] = al
    corrections(state, line_ref, gain_ref, 0, passes, bands, radius)
    x, c = lax.axis_index("date"), lax.axis_index("band")
    groups = laid_ref.shape[0]
    unit = out_refs[0].shape[1]
    for pair, laid in laid_pairs(state, ah, al):
        for m in range(groups):
            laid_ref[m, :, : laid.shape[1]] = laid[m * share : (m + 1) * share]
        for k, out in enumerate(out_refs):
            mine = (x ^ (k // cores)) * cores + (c ^ (k % cores))
            for g in range(spaces):
                lines = laid_ref[g * (groups // spaces) + mine]
                for p, j in enumerate(pair):
                    for r in range(0, share, unit):
                        out[(g * part * share + j * share + r) // unit] = lines[
                            r : r + unit, p * BCOLS : (p + 1) * BCOLS
                        ]
    at = tables + BROWS + 2 * table_lines
    counted = [ref[at : at + 1, 0:BCOLS] for ref in x_refs]
    for out in out_refs:
        out[out.shape[0] - 1] = jnp.concatenate(
            [counted[0], total(counted)] + [jnp.zeros_like(counted[0])] * (unit - 2), axis=0
        )


def large_kernel(
    x_ref, line_ref, gain_ref, ah_ref, al_ref, out_ref, state, piece, sem, *, first, passes, bands, radius
):
    spaces, part = x_ref.shape[:2]
    for i in range(part):
        state[i] = jnp.concatenate([x_ref[s, i] for s in range(spaces)], axis=0)
    corrections(state, line_ref, gain_ref, first, passes, bands, radius)
    share = out_ref.shape[1] // part
    copies = []
    for pair, laid in laid_pairs(state, ah_ref[...], al_ref[...]):
        for p, j in enumerate(pair):
            for d in range(out_ref.shape[0]):
                piece[d, j * share : (j + 1) * share, :] = laid[
                    d * share : (d + 1) * share, p * BCOLS : (p + 1) * BCOLS
                ]
        at = slice(pair[0] * share, (pair[-1] + 1) * share)
        copies.append(
            pltpu.make_async_copy(piece.at[:, at], out_ref.at[:, at], sem.at[len(copies)])
        )
        copies[-1].start()
    for copy in copies:
        copy.wait()


def columns_of(block, kh, kl):
    bh, bl = split(block)
    both = mm(jnp.concatenate([bh, bl], axis=0), kh)
    size = block.shape[0]
    return both[:size] + both[size:] + mm(bh, kl)


def halve_kernel(cols_ref, kh_ref, kl_ref):
    kh_ref[...], kl_ref[...] = split(cols_ref[0])


def regroup_kernel(*refs, spaces):
    groups, size = refs[-2].shape[:2]
    unit = refs[0].shape[1]
    own = lax.axis_index("space")
    for k in range(groups):
        for d in range(spaces):
            for r in range(0, size, unit):
                refs[groups + d][k, r : r + unit, :] = refs[k][
                    (own ^ d) * (size // unit) + r // unit
                ]
        refs[-1][k] = refs[k][refs[k].shape[0] - 1]


def columns_kernel(
    kh_ref, kl_ref, count_ref, *refs, spaces, dates, cores, local_dates
):
    y_refs, (full_ref, weight_ref) = refs[:spaces], refs[spaces:]
    sides, part, share, width = full_ref.shape[1:]
    size = part * share
    kh, kl = kh_ref[...], kl_ref[...]
    for d in range(spaces):
        block = y_refs[d][...].reshape(sides * size, width)
        full_ref[d] = columns_of(block, kh, kl).reshape(sides, part, share, width)
    counted = total(count_ref[dx * cores, 1:2, :] for dx in range(dates))
    summed = jnp.sum(counted, axis=1, keepdims=True)
    mean_count = summed / f32(spaces * dates * local_dates)
    for dx in range(dates):
        own = count_ref[dx * cores, 0:1, :]
        weight = own / (own + mean_count)
        for t in range(local_dates):
            weight_ref[dx * local_dates + t] = jnp.broadcast_to(
                weight[:, t : t + 1], weight_ref.shape[1:]
            )


def median_kernel(
    weight_ref,
    kh_ref,
    kl_ref,
    small_ref,
    y_ref,
    *refs,
    spaces,
    dates,
    cores,
    bands,
    per,
    local_dates,
):
    out_refs, (large_ref, result) = refs[:cores], refs[cores:]
    share, width = small_ref.shape[3:]
    part = small_ref.shape[2]
    kh, kl = kh_ref[...], kl_ref[...]
    for s in range(y_ref.shape[0]):
        large_ref[s] = columns_of(y_ref[s], kh, kl).reshape(per - part, share, width)
    z, x, c = (lax.axis_index(a) for a in ("space", "date", "band"))
    across = max(1, bands // per)
    inside = max(1, per // bands)
    span = bands // across
    tile = weight_ref.shape[1]
    slots = [(dc, b) for dc in range(cores) for b in range(bands)]
    order = [
        (d, dx, t) for d in range(0, spaces, across) for dx in range(dates) for t in range(inside)
    ]
    for start in range(0, share, tile):
        rows = pl.ds(start, tile)

        def load(d, dx, t):
            values = []
            for dc, b in slots:
                far = d ^ (b // span)
                image = t * bands + b % span
                if image < part:
                    values.append(small_ref[far, dx * cores + dc, image, rows, :])
                else:
                    source = ((z ^ far) * dates + (x ^ dx)) * cores + (c ^ dc)
                    values.append(large_ref[source, image - part, rows, :])
            return values

        def weight(d, dx, t):
            return weight_ref[dx * local_dates + (z ^ d) // across * inside + t]

        number = [jnp.zeros((tile, width), f32)] * len(slots)
        below = jnp.zeros((tile, width), f32)
        for key in order:
            w = weight(*key)
            below = below + w
            number = [n + w * v for n, v in zip(number, load(*key))]
        estimate = [n / below for n in number]
        for _ in range(ITERS):
            number = [jnp.zeros((tile, width), f32)] * len(slots)
            below = jnp.zeros((tile, width), f32)
            for key in order:
                values = load(*key)
                squares = []
                for v, e in zip(values, estimate):
                    gap = v - e
                    squares.append(gap * gap)
                scaled = weight(*key) / jnp.sqrt(total(squares) + smooth_sq)
                below = below + scaled
                number = [n + scaled * v for n, v in zip(number, values)]
            estimate = [n / below for n in number]
        for (dc, b), value in zip(slots, estimate):
            if across == 1:
                out_refs[dc][b, rows, :] = value
            else:
                result[dc, ((z % across) ^ (b // span)) * span + b % span, rows, :] = value
    if across > 1:
        for dc in range(cores):
            out_refs[dc][...] = result[dc]


def place_kernel(*refs, dates, cores):
    out_ref = refs[-1]
    share = refs[0].shape[1]
    x, c = lax.axis_index("date"), lax.axis_index("band")
    for dx in range(dates):
        for dc in range(cores):
            j = (x ^ dx) * cores + (c ^ dc)
            at = pl.ds(pl.multiple_of(j * share, share), share)
            out_ref[:, at, :] = refs[dx * cores + dc][...]


def across_sides(pieces, dates, cores):
    received = [pieces[0]]
    for k in range(1, dates * cores):
        pairs = [
            (x * cores + c, (x ^ (k // cores)) * cores + (c ^ (k % cores)))
            for x in range(dates)
            for c in range(cores)
        ]
        received.append(lax.ppermute(pieces[k], ("date", "band"), pairs))
    return received


def local(
    reflect, kernels, strength, destinations, offsets, counts, resample_rows, resample_columns
):
    spaces, dates, cores = (lax.axis_size(a) for a in ("space", "date", "band"))
    local_dates, bands, strip, width = reflect.shape
    passes = kernels.shape[0]
    blocks = offsets.shape[0]
    rows = spaces * strip
    halves = width // BCOLS
    length = halves * rows
    table_lines = -(-length // width)
    tile_rows = blocks * BROWS
    sources = spaces * dates * cores
    share = tile_rows // (dates * cores)
    tile = min(share, SUBLANES)
    per = local_dates * bands // spaces
    part = max(1, per * 3 // 8)
    images = reflect.reshape(spaces, per, strip, width)
    pack = pl.pallas_call(
        functools.partial(pack_kernel, part=part, halves=halves, table_lines=table_lines),
        out_shape=[
            jax.ShapeDtypeStruct(
                (part * strip + round_up(BROWS + 2 * table_lines + 1, SUBLANES), width), f32
            )
        ]
        * spaces,
        in_specs=hbm(4) + vmem(1),
        out_specs=vmem(spaces),
        scratch_shapes=[
            pltpu.VMEM((1, blocks), jnp.int32),
            pltpu.VMEM((1, blocks), jnp.int32),
            pltpu.VMEM((1, BROWS, BROWS), f32),
            pltpu.VMEM((1, local_dates), jnp.int32),
            pltpu.SemaphoreType.DMA((4,)),
        ],
        compiler_params=params(4),
        name="pack",
    )
    small = list(
        pack(
            destinations.reshape(1, blocks),
            offsets.reshape(1, blocks),
            resample_rows,
            counts.reshape(1, local_dates),
            images,
        )
    )
    for d in range(spaces - 1, 0, -1):
        small[d] = lax.ppermute(small[d], "space", [(i, i ^ d) for i in range(spaces)])
    cut = pl.pallas_call(
        cut_kernel,
        out_shape=jax.ShapeDtypeStruct((spaces, per - part, strip, width), f32),
        in_specs=vmem(1),
        out_specs=pl.BlockSpec(memory_space=pltpu.VMEM),
        compiler_params=params(4),
        name="cut",
    )
    rest = cut(images)
    large = lax.all_to_all(rest, "space", split_axis=0, concat_axis=0, tiled=True)

    here = bands if per % bands == 0 else per
    if here != bands:
        first_band = (lax.axis_index("space") * per) % bands
        kernels = lax.dynamic_slice_in_dim(kernels, first_band, here, axis=1)
        strength = lax.dynamic_slice_in_dim(strength, first_band, here, axis=1)
    wide = max(rows, width) + LANES
    count = passes * here
    make_lines = pl.pallas_call(
        taps_kernel,
        out_shape=[
            jax.ShapeDtypeStruct((2, count, wide), f32),
            jax.ShapeDtypeStruct((count, width), f32),
        ],
        in_specs=hbm(2),
        out_specs=vmem(2),
        scratch_shapes=[
            pltpu.VMEM(kernels.shape, f32),
            pltpu.VMEM(strength.shape, f32),
            pltpu.SemaphoreType.DMA((2,)),
        ],
        compiler_params=params(4),
        name="taps",
    )
    lines, gains = make_lines(kernels, strength)

    settings = dict(passes=passes, bands=here, radius=kernels.shape[2] // 2)
    unit = min(share, SUBLANES)
    small_blocks = spaces * part * share // unit + 1
    correct_small = pl.pallas_call(
        functools.partial(
            small_kernel,
            spaces=spaces,
            cores=cores,
            share=share,
            table_lines=table_lines,
            **settings,
        ),
        out_shape=[jax.ShapeDtypeStruct((small_blocks, unit, BCOLS), f32)] * (dates * cores)
        + [jax.ShapeDtypeStruct((spaces * tile_rows, length), bf16)] * 2,
        in_specs=vmem(2 + spaces),
        out_specs=vmem(dates * cores + 2),
        scratch_shapes=[
            pltpu.VMEM((part, rows, width), f32),
            pltpu.VMEM((spaces * tile_rows // share, share, 2 * BCOLS), f32),
        ],
        compiler_params=params(20),
        name="correct0",
    )
    *sides, ah, al = correct_small(lines, gains, *small)
    sides = across_sides(sides, dates, cores)
    regroup = pl.pallas_call(
        functools.partial(regroup_kernel, spaces=spaces),
        out_shape=[jax.ShapeDtypeStruct((dates * cores, part * share, BCOLS), f32)] * spaces
        + [jax.ShapeDtypeStruct((dates * cores, unit, BCOLS), f32)],
        in_specs=vmem(dates * cores),
        out_specs=vmem(spaces + 1),
        compiler_params=params(4),
        name="regroup",
    )
    *small, counted = regroup(*sides)
    for d in range(spaces - 1, 0, -1):
        small[d] = lax.ppermute(small[d], "space", [(i, i ^ d) for i in range(spaces)])

    correct_large = pl.pallas_call(
        functools.partial(large_kernel, first=part, **settings),
        out_shape=jax.ShapeDtypeStruct((sources, (per - part) * share, BCOLS), f32),
        in_specs=vmem(5),
        out_specs=pl.BlockSpec(memory_space=pltpu.HBM),
        scratch_shapes=[
            pltpu.VMEM((per - part, rows, width), f32),
            pltpu.VMEM((sources, (per - part) * share, BCOLS), f32),
            pltpu.SemaphoreType.DMA((per - part,)),
        ],
        compiler_params=params(20),
        name="correct1",
    )
    laid = correct_large(large, lines, gains, ah, al)
    pixels = lax.all_to_all(
        laid, ("space", "date", "band"), split_axis=0, concat_axis=0, tiled=True
    )

    halve = pl.pallas_call(
        halve_kernel,
        out_shape=[jax.ShapeDtypeStruct((BCOLS, BCOLS), bf16)] * 2,
        in_specs=vmem(1),
        out_specs=vmem(2),
        compiler_params=params(2),
        name="halve",
    )
    columns = halve(resample_columns)
    columns_call = pl.pallas_call(
        functools.partial(
            columns_kernel, spaces=spaces, dates=dates, cores=cores, local_dates=local_dates
        ),
        out_shape=[
            jax.ShapeDtypeStruct((spaces, dates * cores, part, share, BCOLS), f32),
            jax.ShapeDtypeStruct((dates * local_dates, tile, BCOLS), f32),
        ],
        in_specs=vmem(3 + spaces),
        out_specs=vmem(2),
        compiler_params=params(8),
        name="columns",
    )
    full, weights = columns_call(*columns, counted, *small)
    shares = pl.pallas_call(
        functools.partial(
            median_kernel,
            spaces=spaces,
            dates=dates,
            cores=cores,
            bands=bands,
            per=per,
            local_dates=local_dates,
        ),
        out_shape=[jax.ShapeDtypeStruct((bands, share, BCOLS), f32)] * cores,
        in_specs=vmem(5),
        out_specs=vmem(cores),
        scratch_shapes=[
            pltpu.VMEM((sources, per - part, share, BCOLS), f32),
            pltpu.VMEM((cores, bands, share, BCOLS), f32),
        ],
        compiler_params=params(12),
        name="median",
    )(weights, *columns, full, pixels)

    pieces = across_sides([shares[k % cores] for k in range(dates * cores)], dates, cores)
    return pl.pallas_call(
        functools.partial(place_kernel, dates=dates, cores=cores),
        out_shape=jax.ShapeDtypeStruct((bands, tile_rows, BCOLS), f32),
        in_specs=vmem(dates * cores),
        out_specs=pl.BlockSpec(memory_space=pltpu.VMEM),
        compiler_params=params(4),
        name="place",
    )(*pieces)


def solution(mesh):
    in_specs = (
        P("date", "band", ("groups", "space"), None),
        P(None, "band", None),
        P(None, "band"),
        P(("groups", "space"), None),
        P(("groups", "space")),
        P("date", ("groups", "space")),
        P(("groups", "space"), None, None),
        P(("groups", "space"), None, None),
    )
    out_specs = P("band", ("groups", "space"), None)

    return jax.shard_map(local, mesh=mesh, in_specs=in_specs, out_specs=out_specs, check_vma=False)
```
